32 devices in a mesh: gx: 4 (over z), gy: 4 (over y, core), gz: 2 (over x).
Axes of the slice: x: 2, y: 2, z: 4, core: 2. Of those that a mesh axis runs over, the one named last changes fastest.
Arguments:
- load: bfloat16 [4, 4, 2, 64, 1152], P('gx', 'gy', 'gz'), may hold values from -6 to 6
- schur: bfloat16 [4, 4, 2, 1152, 1152], P('gx', 'gy', 'gz')
- neumann: bfloat16 [4, 4, 2, 6, 192, 192], P('gx', 'gy', 'gz')
- coarse_basis: bfloat16 [4, 4, 2, 8, 1152], P('gx', 'gy', 'gz'), may hold values from -5 to 5
- coarse_rows: bfloat16 [4, 4, 2, 8, 256], P('gx', 'gy', 'gz'), may hold values from -0.0078125 to 0.0078125
Outputs:
- iterate: bfloat16 [4, 4, 2, 64, 1152], P('gx', 'gy', 'gz')
The draws below stay inside these ranges and needn't reach their ends.
All inputs are finite; a program needn't handle non-finite values.
Results may differ from the reference program's by a relative error of at most 0.0048.
Values sent between devices are 32-bit elements; how exact they have to be, the bound alone decides.
No kernel may reach another device: no remote copies, remote signals or barrier semaphores. Data moves between devices by JAX's collectives and lax.ppermute only.
A program may use at most 64 MiB of HBM per device.

```python
import jax
import jax.numpy as jnp
from jax import lax

NI = 1152
NCF = 8
RHS = 64
ITERS = 2
NC = 256
N_GX = 4
N_GY = 4
N_GZ = 2


def draw_schur(key, part):
    first, second = jax.random.split(jax.random.fold_in(key, 11))
    shape = (N_GX, N_GY, N_GZ, NI, NI)
    diag = jax.random.uniform(first, shape[:-1] + (1,), jnp.float32, 2.0, 4.0)
    rough = jax.random.normal(second, shape, jnp.float32) * (0.6 / NI ** 0.5)
    eye = jnp.eye(NI, dtype=jnp.float32)
    return (rough + diag * eye).astype(jnp.bfloat16)


def draw_neumann(key, part):
    face = NI // 6
    first, second = jax.random.split(jax.random.fold_in(key, 23))
    shape = (N_GX, N_GY, N_GZ, 6, face, face)
    diag = jax.random.uniform(first, shape[:-1] + (1,), jnp.float32, 0.25, 0.5)
    rough = jax.random.normal(second, shape, jnp.float32) * (0.15 / face ** 0.5)
    eye = jnp.eye(face, dtype=jnp.float32)
    return (rough + diag * eye).astype(jnp.bfloat16)


def levels(rng, extent, cuts, smallest, largest):
    loudness = 1.0
    for position, parts in cuts:
        steps = jax.random.uniform(jax.random.fold_in(jax.random.fold_in(rng, 6), position), (parts,), jnp.float32, smallest / len(cuts), largest / len(cuts))
        loudness = loudness * jnp.repeat(jnp.exp(steps), extent[position] // parts).reshape((-1,) + (1,) * (len(extent) - 1 - position))
    return loudness


def scatter_about(key, dims, spread, most, cuts=(), kind=jnp.bfloat16):
    result = jax.random.normal(key, dims, jnp.float32) * spread
    if len(cuts) > 0:
        result = levels(key, dims, cuts, -0.22, 0.18) * result
    return jnp.clip(result, min=-most, max=most).astype(kind)


def setup_inputs(seed: int = 0) -> dict:
    key_of = jax.random.split(jax.random.key(seed), 6)
    load = scatter_about(key_of[0], (N_GX, N_GY, N_GZ, RHS, NI), 1.0, 6.0, ((0, 4), (1, 4), (2, 2)))
    schur = draw_schur(jax.random.fold_in(key_of[5], 71), 0)
    neumann = draw_neumann(jax.random.fold_in(key_of[5], 71), 0)
    coarse_basis = scatter_about(key_of[3], (N_GX, N_GY, N_GZ, NCF, NI), 1.0, 5.0, ((0, 4), (1, 4), (2, 2)))
    coarse_rows = scatter_about(key_of[4], (N_GX, N_GY, N_GZ, NCF, NC), (0.3 * (NI * NC) ** -0.5), 0.0078125, ((0, 4), (1, 4), (2, 2)))
    return dict(load=load, schur=schur, neumann=neumann, coarse_basis=coarse_basis, coarse_rows=coarse_rows)


def pads_for(ndim, axis, low, high):
    pads = [(0, 0)] * ndim
    pads[axis] = (low, high)
    return pads


def from_lower(face, axis):
    count = face.shape[axis]
    padded = jnp.pad(face, pads_for(face.ndim, axis, 1, 0))
    return lax.slice_in_dim(padded, 0, count, axis=axis)


def from_upper(face, axis):
    count = face.shape[axis]
    padded = jnp.pad(face, pads_for(face.ndim, axis, 0, 1))
    return lax.slice_in_dim(padded, 1, count + 1, axis=axis)


def assemble(vec):
    pieces = []
    for axis in range(3):
        pieces.append(from_lower(vec[:, :, :, :, 2 * axis + 1, :], axis))
        pieces.append(from_upper(vec[:, :, :, :, 2 * axis, :], axis))
    return vec + jnp.stack(pieces, axis=4)


def face_weights():
    sizes = (N_GX, N_GY, N_GZ)
    columns = []
    for axis in range(3):
        shape = [1, 1, 1]
        shape[axis] = sizes[axis]
        place = jnp.arange(sizes[axis], dtype=jnp.int32).reshape(shape)
        lower = jnp.where(place > 0, 0.5, 1.0).astype(jnp.float32)
        upper = jnp.where(place < sizes[axis] - 1, 0.5, 1.0).astype(jnp.float32)
        columns.append(jnp.broadcast_to(lower, (N_GX, N_GY, N_GZ)))
        columns.append(jnp.broadcast_to(upper, (N_GX, N_GY, N_GZ)))
    return jnp.stack(columns, axis=3).reshape(N_GX, N_GY, N_GZ, 1, 6, 1)


def apply_schur(pair):
    matrix, vector = pair
    return jnp.dot(vector.astype(jnp.float32), matrix.astype(jnp.float32), precision=lax.Precision.HIGHEST)


def reference(load, schur, neumann, coarse_basis, coarse_rows):
    count = N_GX * N_GY * N_GZ
    face = NI // 6
    shape6 = (N_GX, N_GY, N_GZ, RHS, 6, face)
    weight = face_weights()
    load_f = load.astype(jnp.float32)
    blocks = neumann.astype(jnp.float32)
    basis = coarse_basis.astype(jnp.float32)
    rows = coarse_rows.astype(jnp.float32).reshape(count, NCF, NC)
    schur_flat = schur.reshape(count, NI, NI)
    iterate = jnp.zeros((N_GX, N_GY, N_GZ, RHS, NI), jnp.float32)
    for step in range(ITERS):
        if step == 0:
            local = load_f
        else:
            rounded = iterate.astype(jnp.bfloat16).reshape(count, RHS, NI)
            product = lax.map(apply_schur, (schur_flat, rounded))
            local = load_f - product.reshape(N_GX, N_GY, N_GZ, RHS, NI)
        resid = assemble(local.reshape(shape6))
        scaled = (resid * weight).astype(jnp.bfloat16)
        scaled_f = scaled.astype(jnp.float32)
        flat = scaled_f.reshape(N_GX, N_GY, N_GZ, RHS, NI)
        coarse_in = jnp.einsum("xyzrn,xyzkn->xyzrk", flat, basis, precision=lax.Precision.HIGHEST)
        whole = coarse_in.reshape(count, RHS, NCF).transpose(1, 0, 2).reshape(RHS, NC)
        coarse_out = jnp.einsum("rj,dkj->drk", whole, rows, precision=lax.Precision.HIGHEST)
        coarse_out = coarse_out.reshape(N_GX, N_GY, N_GZ, RHS, NCF)
        local_part = jnp.einsum("xyzrfa,xyzfab->xyzrfb", scaled_f, blocks, precision=lax.Precision.HIGHEST)
        coarse_part = jnp.einsum("xyzrk,xyzkn->xyzrn", coarse_out, basis, precision=lax.Precision.HIGHEST)
        correction = local_part + coarse_part.reshape(shape6)
        update = assemble(correction * weight)
        iterate = iterate + 0.5 * update.reshape(N_GX, N_GY, N_GZ, RHS, NI)
    return iterate.astype(jnp.bfloat16)
```

```python
import functools

import jax
import jax.numpy as jnp
from jax import lax
from jax.experimental import pallas as pl
from jax.experimental.pallas import tpu as pltpu
from jax.sharding import PartitionSpec as P

AXES = ("gx", "gy", "gz")


def links():
    swaps = []
    for axis in AXES:
        devices = lax.axis_size(axis)
        for first in (0, 1):
            pairs = [(i, i + 1) for i in range(first, devices - 1, 2)]
            if pairs:
                swaps.append((axis, first, pairs + [(j, i) for i, j in pairs]))
    return swaps


def swap(buffers):
    return [lax.ppermute(buf, axis, pairs) for buf, (axis, _, pairs) in zip(buffers, links())]


def odd_place(axis):
    return lax.rem(lax.axis_index(axis), 2) == 1


def weights():
    values = []
    for axis in AXES:
        place = lax.axis_index(axis)
        values.append(jnp.where(place > 0, 0.5, 1.0).astype(jnp.float32))
        values.append(jnp.where(place < lax.axis_size(axis) - 1, 0.5, 1.0).astype(jnp.float32))
    return values


def outgoing(faces):
    picked = []
    for axis, first, _ in links():
        number = AXES.index(axis)
        lower, upper = faces[2 * number], faces[2 * number + 1]
        odd = odd_place(axis)
        picked.append(jnp.where(odd, lower, upper) if first == 0 else jnp.where(odd, upper, lower))
    return picked


def incoming(received):
    faces = []
    for axis in AXES:
        got = {first: buf for buf, (name, first, _) in zip(received, links()) if name == axis}
        even = got[0]
        other = got.get(1, None)
        if other is None:
            other = jnp.zeros_like(even)
        odd = odd_place(axis)
        faces.append(jnp.where(odd, even, other))
        faces.append(jnp.where(odd, other, even))
    return faces


def split(value):
    high = value.astype(jnp.bfloat16)
    low = (value - high.astype(jnp.float32)).astype(jnp.bfloat16)
    return high, low


def dot(a, b, dims):
    return lax.dot_general(a, b, (dims, ((), ())), preferred_element_type=jnp.float32)


def cut(ref, face):
    return [ref[:, f * face:(f + 1) * face].astype(jnp.float32) for f in range(6)]


def call(kernel, shapes, *args, flops=10 ** 7):
    vmem = pl.BlockSpec(memory_space=pltpu.VMEM)
    size = sum(a.size * a.dtype.itemsize for a in args) + sum(s.size * s.dtype.itemsize for s in shapes)
    return pl.pallas_call(
        kernel,
        out_shape=shapes,
        in_specs=[vmem] * len(args),
        out_specs=[vmem] * len(shapes),
        cost_estimate=pl.CostEstimate(flops=flops, bytes_accessed=size, transcendentals=0),
        compiler_params=pltpu.CompilerParams(vmem_limit_bytes=32 * 2 ** 20),
    )(*args)


def f32(*shape):
    return jax.ShapeDtypeStruct(shape, jnp.float32)


def bf16(*shape):
    return jax.ShapeDtypeStruct(shape, jnp.bfloat16)


def send_kernel(face, vec_ref, *outs):
    for out, value in zip(outs, outgoing(cut(vec_ref, face))):
        out[...] = value


def residual_kernel(face, pack, n_in, vec_ref, basis_ref, *refs):
    received = [r[...] for r in refs[:n_in]]
    scaled_ref, slots_ref = refs[n_in:]
    own = cut(vec_ref, face)
    other = incoming(received)
    weight = weights()
    coarse = None
    for f in range(6):
        scaled = ((own[f] + other[f]) * weight[f]).astype(jnp.bfloat16)
        scaled_ref[f] = scaled
        part = dot(basis_ref[:, f * face:(f + 1) * face], scaled, ((1,), (1,)))
        coarse = part if coarse is None else coarse + part
    rows = coarse.shape[0] // pack
    slot = jnp.concatenate([coarse[i * rows:(i + 1) * rows] for i in range(pack)], axis=1)
    for d in range(slots_ref.shape[0]):
        slots_ref[d] = slot


def local_kernel(face, scaled_ref, blocks_ref, basis_ref, rows_ref, local_ref, *outs):
    count = scaled_ref.shape[1]
    ncf = basis_ref.shape[0]
    parts = []
    for f in range(6):
        part = dot(scaled_ref[f], blocks_ref[f], ((1,), (0,)))
        local_ref[f] = part
        parts.append(part)
    sent = outgoing(parts)
    bases = outgoing(cut(basis_ref, face))
    rows = rows_ref[...].astype(jnp.float32)
    for out, part, base in zip(outs, sent, bases):
        out[0:count, 0:face] = part
        out[count:count + ncf, 0:face] = base
        out[count + ncf:, :] = rows


def local_again_kernel(face, scaled_ref, blocks_ref, local_ref, *outs):
    parts = []
    for f in range(6):
        part = dot(scaled_ref[f], blocks_ref[f], ((1,), (0,)))
        local_ref[f] = part
        parts.append(part)
    for out, part in zip(outs, outgoing(parts)):
        out[...] = part


def gather_kernel(face, n_in, local_ref, basis_ref, rows_ref, *refs):
    count = local_ref.shape[1]
    ncf = basis_ref.shape[0]
    received = [r[...] for r in refs[:n_in]]
    start_ref, bases_ref, all_rows_ref = refs[n_in:]
    other = incoming(received)
    weight = weights()
    bases_ref[...] = jnp.zeros_like(bases_ref)
    own = cut(basis_ref, face)
    all_rows = [rows_ref[...].astype(jnp.float32)]
    base_rows = []
    for f in range(6):
        half = 0.5 * weight[f]
        at = slice(f * face, (f + 1) * face)
        start_ref[:, at] = (local_ref[f] + other[f][0:count, 0:face]) * half
        bases_ref[0:ncf, at] = own[f] * half
        bases_ref[ncf * (f + 1):ncf * (f + 2), at] = other[f][count:count + ncf, 0:face] * half
        all_rows.append(other[f][count + ncf:, :])
    all_rows_ref[...] = jnp.concatenate(all_rows, axis=0)


def advance_kernel(face, n_in, start_ref, local_ref, *refs):
    received = [r[...] for r in refs[:n_in]]
    out_ref = refs[n_in]
    other = incoming(received)
    weight = weights()
    for f in range(6):
        at = slice(f * face, (f + 1) * face)
        out_ref[:, at] = start_ref[:, at] + (local_ref[f] + other[f]) * (0.5 * weight[f])


def coarse_update(slots_ref, rows_ref, bases_ref, count):
    devices, rows, lanes = slots_ref.shape
    whole = slots_ref[...].reshape(devices * rows, lanes)
    pack = lanes // count
    each = devices * rows
    values = None
    for i in range(pack):
        high, low = split(whole[:, i * count:(i + 1) * count])
        matrix = rows_ref[:, i * each:(i + 1) * each]
        part = dot(matrix, high, ((1,), (0,))) + dot(matrix, low, ((1,), (0,)))
        values = part if values is None else values + part
    high, low = split(values)
    bases = bases_ref[...]
    return dot(high, bases, ((0,), (0,))) + dot(low, bases, ((0,), (0,)))


def middle_kernel(face, slots_ref, rows_ref, bases_ref, start_ref, load_ref, schur_ref, iterate_ref, local_ref, *outs):
    iterate = start_ref[...] + coarse_update(slots_ref, rows_ref, bases_ref, start_ref.shape[0])
    iterate_ref[...] = iterate
    product = dot(iterate.astype(jnp.bfloat16), schur_ref[...], ((1,), (0,)))
    local = load_ref[...].astype(jnp.float32) - product
    local_ref[...] = local
    faces = [local[:, f * face:(f + 1) * face] for f in range(6)]
    for out, value in zip(outs, outgoing(faces)):
        out[...] = value


def last_kernel(slots_ref, rows_ref, bases_ref, start_ref, out_ref):
    update = coarse_update(slots_ref, rows_ref, bases_ref, start_ref.shape[0])
    out_ref[...] = (start_ref[...] + update).astype(jnp.bfloat16)


def body(load, schur, neumann, coarse_basis, coarse_rows):
    count, width = load.shape[3], load.shape[4]
    face = width // 6
    ncf, total = coarse_rows.shape[3], coarse_rows.shape[4]
    devices = total // ncf
    pack = max(128 // count, 1)
    while ncf % pack:
        pack -= 1
    load2 = load.reshape(count, width)
    schur2 = schur.reshape(width, width)
    blocks = neumann.reshape(6, face, face)
    basis = coarse_basis.reshape(ncf, width)
    rows = coarse_rows.reshape(ncf, total)
    rows = rows.reshape(ncf, devices, pack, ncf // pack).transpose(0, 2, 1, 3).reshape(ncf, total)
    swaps = len(links())
    wide = max(face, 256)
    wide = -(-wide // 128) * 128
    flat_rows = ncf * total // wide
    part = [f32(count, face)] * swaps
    slots = f32(devices, ncf // pack, pack * count)

    def gather(value):
        return lax.all_to_all(value, AXES, 0, 0)

    sent = call(functools.partial(send_kernel, face), part, load2)
    vec = load2
    received = swap(sent)
    scaled, slot = call(
        functools.partial(residual_kernel, face, pack, swaps), [bf16(6, count, face), slots], vec, basis, *received
    )
    whole = gather(slot)
    out = [f32(count + ncf + flat_rows, wide)] * swaps
    local, *sent = call(
        functools.partial(local_kernel, face), [f32(6, count, face)] + out,
        scaled, blocks, basis, rows.reshape(flat_rows, wide),
    )
    received = swap(sent)
    start, bases, all_rows = call(
        functools.partial(gather_kernel, face, swaps),
        [f32(count, width), f32(7 * ncf, width), f32(7 * flat_rows, wide)],
        local, basis, rows.reshape(flat_rows, wide), *received,
    )
    bases = bases.astype(jnp.bfloat16)
    all_rows = all_rows.reshape(7 * ncf, total).astype(jnp.bfloat16)
    iterate, vec, *sent = call(
        functools.partial(middle_kernel, face), [f32(count, width), f32(count, width)] + part,
        whole, all_rows, bases, start, load2, schur2,
    )
    received = swap(sent)
    scaled, slot = call(
        functools.partial(residual_kernel, face, pack, swaps), [bf16(6, count, face), slots], vec, basis, *received
    )
    whole = gather(slot)
    local, *sent = call(
        functools.partial(local_again_kernel, face), [f32(6, count, face)] + part, scaled, blocks
    )
    received = swap(sent)
    (start,) = call(
        functools.partial(advance_kernel, face, swaps), [f32(count, width)], iterate, local, *received
    )
    (result,) = call(last_kernel, [bf16(count, width)], whole, all_rows, bases, start)
    return result.reshape(load.shape)


def solution(mesh):
    placed = (
        P("gx", "gy", "gz", None, None),
        P("gx", "gy", "gz", None, None),
        P("gx", "gy", "gz", None, None, None),
        P("gx", "gy", "gz", None, None),
        P("gx", "gy", "gz", None, None),
    )
    return jax.shard_map(
        body, mesh=mesh, in_specs=placed, out_specs=P("gx", "gy", "gz", None, None), check_vma=False
    )
```

```python
import functools

import jax
import jax.numpy as jnp
from jax import lax
from jax.experimental import pallas as pl
from jax.experimental.pallas import tpu as pltpu
from jax.sharding import PartitionSpec as P

AXES = ("gx", "gy", "gz")


def links():
    swaps = []
    for axis, first in (("gz", 0), ("gz", 1), ("gx", 0), ("gx", 1), ("gy", 1), ("gy", 0)):
        pairs = [(i, i + 1) for i in range(first, lax.axis_size(axis) - 1, 2)]
        if pairs:
            swaps.append((axis, first, pairs + [(j, i) for i, j in pairs]))
    return swaps


def swap(buffers):
    return [lax.ppermute(buf, axis, pairs) for buf, (axis, _, pairs) in zip(buffers, links())]


def odd_place(axis):
    return lax.rem(lax.axis_index(axis), 2) == 1


def weights():
    values = []
    for axis in AXES:
        place = lax.axis_index(axis)
        values.append(jnp.where(place > 0, 0.5, 1.0).astype(jnp.float32))
        values.append(jnp.where(place < lax.axis_size(axis) - 1, 0.5, 1.0).astype(jnp.float32))
    return values


def outgoing(faces):
    picked = []
    for axis, first, _ in links():
        number = AXES.index(axis)
        lower, upper = faces[2 * number], faces[2 * number + 1]
        odd = odd_place(axis)
        picked.append(jnp.where(odd, lower, upper) if first == 0 else jnp.where(odd, upper, lower))
    return picked


def incoming(received):
    faces = []
    for axis in AXES:
        got = {first: buf for buf, (name, first, _) in zip(received, links()) if name == axis}
        even = got[0]
        other = got.get(1, None)
        if other is None:
            other = jnp.zeros_like(even)
        odd = odd_place(axis)
        faces.append(jnp.where(odd, even, other))
        faces.append(jnp.where(odd, other, even))
    return faces


def split(value):
    high = value.astype(jnp.bfloat16)
    low = (value - high.astype(jnp.float32)).astype(jnp.bfloat16)
    return high, low


def dot(a, b, dims):
    return lax.dot_general(a, b, (dims, ((), ())), preferred_element_type=jnp.float32)


def cut(ref, face):
    return [ref[:, f * face:(f + 1) * face].astype(jnp.float32) for f in range(6)]


def call(kernel, shapes, *args, far=(), scratch=(), limit=4):
    vmem = pl.BlockSpec(memory_space=pltpu.VMEM)
    hbm = pl.BlockSpec(memory_space=pltpu.HBM)
    size = sum(a.size * a.dtype.itemsize for a in args) + sum(s.size * s.dtype.itemsize for s in shapes)
    return pl.pallas_call(
        kernel,
        out_shape=shapes,
        in_specs=[hbm if i in far else vmem for i in range(len(args))],
        out_specs=[vmem] * len(shapes),
        scratch_shapes=scratch,
        cost_estimate=pl.CostEstimate(flops=10 ** 7, bytes_accessed=size, transcendentals=0),
        compiler_params=pltpu.CompilerParams(vmem_limit_bytes=limit * 2 ** 20),
    )(*[pltpu.with_memory_space_constraint(a, pltpu.HBM) if i in far else a for i, a in enumerate(args)])


def chunks(size):
    return [(at, min(256, size - at)) for at in range(0, size, 256)]


def stage_kernel(*refs):
    half = (len(refs) - 1) // 2
    copies = [pltpu.make_async_copy(refs[i], refs[half + i], refs[-1].at[i]) for i in range(half)]
    for copy in copies:
        copy.start()
    for copy in copies:
        copy.wait()


def stage(*args):
    return call(
        stage_kernel, [jax.ShapeDtypeStruct(a.shape, a.dtype) for a in args], *args, far=range(len(args)),
        scratch=[pltpu.SemaphoreType.DMA((len(args),))],
    )


def f32(*shape):
    return jax.ShapeDtypeStruct(shape, jnp.float32)


def bf16(*shape):
    return jax.ShapeDtypeStruct(shape, jnp.bfloat16)


def send_kernel(face, load_ref, vec_ref, *outs):
    vec_ref[...] = load_ref[...].astype(jnp.float32)
    for out, value in zip(outs, outgoing(cut(load_ref, face))):
        out[...] = value


def residual_kernel(face, pack, n_in, vec_ref, basis_ref, *refs):
    received = [r[...] for r in refs[:n_in]]
    scaled_ref, slots_ref = refs[n_in:]
    own = cut(vec_ref, face)
    other = incoming(received)
    weight = weights()
    coarse = None
    for f in range(6):
        scaled = ((own[f] + other[f]) * weight[f]).astype(jnp.bfloat16)
        scaled_ref[f] = scaled
        part = dot(basis_ref[:, f * face:(f + 1) * face], scaled, ((1,), (1,)))
        coarse = part if coarse is None else coarse + part
    rows = coarse.shape[0] // pack
    slot = jnp.concatenate([coarse[i * rows:(i + 1) * rows] for i in range(pack)], axis=1)
    for d in range(slots_ref.shape[0]):
        slots_ref[d] = slot


def local_kernel(face, scaled_ref, blocks_ref, basis_ref, rows_ref, local_ref, *outs):
    count = scaled_ref.shape[1]
    ncf = basis_ref.shape[0]
    parts = []
    for f in range(6):
        part = dot(scaled_ref[f], blocks_ref[f], ((1,), (0,)))
        local_ref[f] = part
        parts.append(part)
    sent = outgoing(parts)
    bases = outgoing(cut(basis_ref, face))
    rows = rows_ref[...].astype(jnp.float32)
    for out, part, base in zip(outs, sent, bases):
        out[0:count, 0:face] = part
        out[count:count + ncf, 0:face] = base
        out[count + ncf:, :] = rows


def local_again_kernel(face, scaled_ref, blocks_ref, local_ref, *outs):
    parts = []
    for f in range(6):
        part = dot(scaled_ref[f], blocks_ref[f], ((1,), (0,)))
        local_ref[f] = part
        parts.append(part)
    for out, part in zip(outs, outgoing(parts)):
        out[...] = part


def gather_kernel(face, n_in, local_ref, basis_ref, rows_ref, *refs):
    count = local_ref.shape[1]
    ncf = basis_ref.shape[0]
    received = [r[...] for r in refs[:n_in]]
    start_ref, bases_ref, all_rows_ref = refs[n_in:]
    other = incoming(received)
    weight = weights()
    bases_ref[...] = jnp.zeros_like(bases_ref)
    own = cut(basis_ref, face)
    all_rows = [rows_ref[...].astype(jnp.float32)]
    base_rows = []
    for f in range(6):
        half = 0.5 * weight[f]
        at = slice(f * face, (f + 1) * face)
        start_ref[:, at] = (local_ref[f] + other[f][0:count, 0:face]) * half
        bases_ref[0:ncf, at] = own[f] * half
        bases_ref[ncf * (f + 1):ncf * (f + 2), at] = other[f][count:count + ncf, 0:face] * half
        all_rows.append(other[f][count + ncf:, :])
    all_rows_ref[...] = jnp.concatenate(all_rows, axis=0)


def advance_kernel(face, n_in, start_ref, local_ref, *refs):
    received = [r[...] for r in refs[:n_in]]
    out_ref = refs[n_in]
    other = incoming(received)
    weight = weights()
    for f in range(6):
        at = slice(f * face, (f + 1) * face)
        out_ref[:, at] = start_ref[:, at] + (local_ref[f] + other[f]) * (0.5 * weight[f])


def coarse_update(slots_ref, rows_ref, bases_ref, count):
    devices, rows, lanes = slots_ref.shape
    slots = slots_ref[...]
    whole = jnp.concatenate([slots[:, :, i:i + count] for i in range(0, lanes, count)], axis=1)
    high, low = split(whole.reshape(devices * rows * (lanes // count), count))
    matrix = rows_ref[...]
    values = dot(matrix, high, ((1,), (0,))) + dot(matrix, low, ((1,), (0,)))
    high, low = split(values)
    bases = bases_ref[...]
    return dot(high, bases, ((0,), (0,))) + dot(low, bases, ((0,), (0,)))


def middle_kernel(face, slots_ref, rows_ref, bases_ref, start_ref, load_ref, schur_ref, iterate_ref, local_ref, *refs):
    outs, near_ref, sems = refs[:-2], refs[-2], refs[-1]
    width = near_ref.shape[0]
    copies = []
    for i, (at, size) in enumerate(chunks(width)):
        rows = pl.ds(at, size)
        copies.append(pltpu.make_async_copy(schur_ref.at[rows], near_ref.at[rows], sems.at[i]))
        copies[i].start()
    iterate = start_ref[...] + coarse_update(slots_ref, rows_ref, bases_ref, start_ref.shape[0])
    iterate_ref[...] = iterate
    rounded = iterate.astype(jnp.bfloat16)
    local = load_ref[...]
    for i, (at, size) in enumerate(chunks(width)):
        copies[i].wait()
        local = local - dot(rounded[:, at:at + size], near_ref[at:at + size], ((1,), (0,)))
    local_ref[...] = local
    faces = [local[:, f * face:(f + 1) * face] for f in range(6)]
    for out, value in zip(outs, outgoing(faces)):
        out[...] = value


def last_kernel(slots_ref, rows_ref, bases_ref, start_ref, out_ref):
    update = coarse_update(slots_ref, rows_ref, bases_ref, start_ref.shape[0])
    out_ref[...] = (start_ref[...] + update).astype(jnp.bfloat16)


def body(load, schur, neumann, coarse_basis, coarse_rows):
    count, width = load.shape[3], load.shape[4]
    face = width // 6
    ncf, total = coarse_rows.shape[3], coarse_rows.shape[4]
    devices = total // ncf
    pack = max(128 // count, 1)
    while ncf % pack:
        pack -= 1
    schur2 = schur.reshape(width, width)
    blocks = neumann.reshape(6, face, face)
    basis = coarse_basis.reshape(ncf, width)
    rows = coarse_rows.reshape(ncf, total)
    swaps = len(links())
    wide = max(face, 256)
    wide = -(-wide // 128) * 128
    flat_rows = ncf * total // wide
    part = [f32(count, face)] * swaps
    slots = f32(devices, ncf // pack, pack * count)

    def gather(value):
        return lax.all_to_all(value, AXES, 0, 0)

    load_f, *sent = call(functools.partial(send_kernel, face), [f32(count, width)] + part, load.reshape(count, width))
    received = swap(sent)
    blocks, basis, rows = stage(blocks, basis, rows)
    scaled, slot = call(
        functools.partial(residual_kernel, face, pack, swaps), [bf16(6, count, face), slots], load_f, basis, *received
    )
    whole = gather(slot)
    out = [f32(count + ncf + flat_rows, wide)] * swaps
    local, *sent = call(
        functools.partial(local_kernel, face), [f32(6, count, face)] + out,
        scaled, blocks, basis, rows.reshape(flat_rows, wide),
    )
    received = swap(sent)
    start, bases, all_rows = call(
        functools.partial(gather_kernel, face, swaps),
        [f32(count, width), f32(7 * ncf, width), f32(7 * flat_rows, wide)],
        local, basis, rows.reshape(flat_rows, wide), *received,
    )
    bases = bases.astype(jnp.bfloat16)
    all_rows = all_rows.reshape(7 * ncf, total).astype(jnp.bfloat16)
    iterate, vec, *sent = call(
        functools.partial(middle_kernel, face), [f32(count, width), f32(count, width)] + part,
        whole, all_rows, bases, start, load_f, schur2, far=(5,), limit=8,
        scratch=[pltpu.VMEM((width, width), jnp.bfloat16), pltpu.SemaphoreType.DMA((len(chunks(width)),))],
    )
    received = swap(sent)
    scaled, slot = call(
        functools.partial(residual_kernel, face, pack, swaps), [bf16(6, count, face), slots], vec, basis, *received
    )
    whole = gather(slot)
    local, *sent = call(
        functools.partial(local_again_kernel, face), [f32(6, count, face)] + part, scaled, blocks
    )
    received = swap(sent)
    (start,) = call(
        functools.partial(advance_kernel, face, swaps), [f32(count, width)], iterate, local, *received
    )
    (result,) = call(last_kernel, [bf16(count, width)], whole, all_rows, bases, start)
    return result.reshape(load.shape)


def solution(mesh):
    placed = (
        P("gx", "gy", "gz", None, None),
        P("gx", "gy", "gz", None, None),
        P("gx", "gy", "gz", None, None, None),
        P("gx", "gy", "gz", None, None),
        P("gx", "gy", "gz", None, None),
    )
    return jax.shard_map(
        body, mesh=mesh, in_specs=placed, out_specs=P("gx", "gy", "gz", None, None), check_vma=False
    )
```

```python
import functools

import jax
import jax.numpy as jnp
from jax import lax
from jax.experimental import pallas as pl
from jax.experimental.pallas import tpu as pltpu
from jax.sharding import PartitionSpec as P

AXES = ("gx", "gy", "gz")


def links():
    swaps = []
    for axis, first in (("gz", 0), ("gz", 1), ("gx", 0), ("gx", 1), ("gy", 1), ("gy", 0)):
        pairs = [(i, i + 1) for i in range(first, lax.axis_size(axis) - 1, 2)]
        if pairs:
            swaps.append((axis, first, pairs + [(j, i) for i, j in pairs]))
    return swaps


def swap(buffers):
    return [lax.ppermute(buf, axis, pairs) for buf, (axis, _, pairs) in zip(buffers, links())]


def odd_place(axis):
    return lax.rem(lax.axis_index(axis), 2) == 1


def weights():
    values = []
    for axis in AXES:
        place = lax.axis_index(axis)
        values.append(jnp.where(place > 0, 0.5, 1.0).astype(jnp.float32))
        values.append(jnp.where(place < lax.axis_size(axis) - 1, 0.5, 1.0).astype(jnp.float32))
    return values


def outgoing(faces):
    picked = []
    for axis, first, _ in links():
        number = AXES.index(axis)
        lower, upper = faces[2 * number], faces[2 * number + 1]
        odd = odd_place(axis)
        picked.append(jnp.where(odd, lower, upper) if first == 0 else jnp.where(odd, upper, lower))
    return picked


def incoming(received):
    faces = []
    for axis in AXES:
        got = {first: buf for buf, (name, first, _) in zip(received, links()) if name == axis}
        even = got[0]
        other = got.get(1, None)
        if other is None:
            other = jnp.zeros_like(even)
        odd = odd_place(axis)
        faces.append(jnp.where(odd, even, other))
        faces.append(jnp.where(odd, other, even))
    return faces


def split(value):
    high = value.astype(jnp.bfloat16)
    low = (value - high.astype(jnp.float32)).astype(jnp.bfloat16)
    return high, low


def dot(a, b, dims):
    return lax.dot_general(a, b, (dims, ((), ())), preferred_element_type=jnp.float32)


def cut(ref, face):
    return [ref[:, f * face:(f + 1) * face].astype(jnp.float32) for f in range(6)]


def call(kernel, shapes, *args, far=(), scratch=()):
    vmem = pl.BlockSpec(memory_space=pltpu.VMEM)
    hbm = pl.BlockSpec(memory_space=pltpu.HBM)
    near = [a for i, a in enumerate(args) if i not in far] + list(shapes)
    near += [a for a in scratch if isinstance(a, jax.ShapeDtypeStruct)]
    size = sum(a.size * a.dtype.itemsize for a in near)
    scratch = [pltpu.VMEM(a.shape, a.dtype) if isinstance(a, jax.ShapeDtypeStruct) else a for a in scratch]
    return pl.pallas_call(
        kernel,
        out_shape=shapes,
        in_specs=[hbm if i in far else vmem for i in range(len(args))],
        out_specs=[vmem] * len(shapes),
        scratch_shapes=scratch,
        cost_estimate=pl.CostEstimate(flops=10 ** 7, bytes_accessed=size, transcendentals=0),
        compiler_params=pltpu.CompilerParams(vmem_limit_bytes=2 ** 21 + 3 * size // 2),
    )(*[pltpu.with_memory_space_constraint(a, pltpu.HBM) if i in far else a for i, a in enumerate(args)])


def chunks(size):
    return [(at, min(256, size - at)) for at in range(0, size, 256)]


def f32(*shape):
    return jax.ShapeDtypeStruct(shape, jnp.float32)


def bf16(*shape):
    return jax.ShapeDtypeStruct(shape, jnp.bfloat16)


def fold(value):
    rows, width = value.shape
    tail = width % 128
    pieces = [value[:, i:i + 128] for i in range(0, width - tail, 128)]
    if tail:
        step = rows * tail // 128
        last = value[:, width - tail:]
        pieces.append(jnp.concatenate([last[i:i + step] for i in range(0, rows, step)], axis=1))
    return jnp.concatenate(pieces, axis=0)


def unfold(value, rows, width):
    tail = width % 128
    full = width // 128
    pieces = [value[i * rows:(i + 1) * rows] for i in range(full)]
    if tail:
        last = value[full * rows:]
        pieces.append(jnp.concatenate([last[:, i:i + tail] for i in range(0, 128, tail)], axis=0))
    return jnp.concatenate(pieces, axis=1)


def even_rows(ncf):
    return 2 * ncf


def spans(count, face, ncf, total):
    sizes = [count * face // 128, face * face // 128, even_rows(ncf) * face // 128, ncf * total // 128]
    ends = [sum(sizes[:i + 1]) for i in range(4)]
    return [slice(e - n, e) for e, n in zip(ends, sizes)]


def start_kernel(face, load_ref, blocks_ref, basis_ref, rows_ref, vec_ref, bases_ref, flat_ref, *refs):
    outs, load_near, near_ref, sems = refs[:-3], refs[-3], refs[-2], refs[-1]
    pairs = ((load_ref, load_near), (basis_ref, bases_ref), (rows_ref, flat_ref), (blocks_ref, near_ref))
    copies = [pltpu.make_async_copy(far, near, sems.at[i]) for i, (far, near) in enumerate(pairs)]
    for copy in copies:
        copy.start()
    count, ncf = load_near.shape[0], bases_ref.shape[0]
    at = spans(count, face, ncf, flat_ref.shape[0] * flat_ref.shape[1] // ncf)
    copies[0].wait()
    vec_ref[...] = load_near[...].astype(jnp.float32)
    for out, value in zip(outs, outgoing(cut(vec_ref, face))):
        out[at[0]] = fold(value)
    copies[1].wait()
    copies[2].wait()
    zeros = jnp.zeros((even_rows(ncf) - ncf, face), jnp.float32)
    flat = fold(flat_ref[...].astype(jnp.float32))
    for out, value in zip(outs, outgoing(cut(bases_ref, face))):
        out[at[2]] = fold(jnp.concatenate([value, zeros], axis=0))
        out[at[3]] = flat
    copies[3].wait()
    for out, (axis, first, _) in zip(outs, links()):
        upper = lax.rem(lax.axis_index(axis) + 1 + first, 2)
        out[at[1]] = fold(near_ref[2 * AXES.index(axis) + upper].astype(jnp.float32))


def scaled_faces(face, vec_ref, received):
    count = vec_ref.shape[0]
    own = cut(vec_ref, face)
    other = incoming([r[0:count * face // 128] for r in received])
    weight = weights()
    return [((own[f] + unfold(other[f], count, face)) * weight[f]).astype(jnp.bfloat16) for f in range(6)]


def residual_kernel(face, pack, vec_ref, basis_ref, *refs):
    received, slots_ref = refs[:-1], refs[-1]
    coarse = None
    for f, scaled in enumerate(scaled_faces(face, vec_ref, received)):
        part = dot(basis_ref[:, f * face:(f + 1) * face], scaled, ((1,), (1,)))
        coarse = part if coarse is None else coarse + part
    rows = coarse.shape[0] // pack
    slot = jnp.concatenate([coarse[i * rows:(i + 1) * rows] for i in range(pack)], axis=1)
    for d in range(slots_ref.shape[0]):
        slots_ref[d] = slot


def local_kernel(face, n_in, vec_ref, blocks_ref, basis_ref, rows_ref, schur_ref, *refs):
    count = vec_ref.shape[0]
    ncf = basis_ref.shape[0]
    received = refs[:n_in]
    start_ref, others_ref, bases_ref, all_rows_ref, near_ref, own_ref, sems = refs[n_in:]
    copy = pltpu.make_async_copy(blocks_ref, own_ref, sems.at[0])
    early = pltpu.make_async_copy(schur_ref.at[pl.ds(0, near_ref.shape[0])], near_ref, sems.at[1])
    copy.start()
    early.start()
    at = spans(count, face, ncf, rows_ref.shape[0] * rows_ref.shape[1] // ncf)
    blocks, bases, rows = [incoming([r[at[i]] for r in received]) for i in (1, 2, 3)]
    weight = weights()
    bases_ref[...] = jnp.zeros_like(bases_ref)
    own = cut(basis_ref, face)
    all_rows = [rows_ref[...].astype(jnp.float32)]
    scaled = scaled_faces(face, vec_ref, received)
    copy.wait()
    for f in range(6):
        half = 0.5 * weight[f]
        to = slice(f * face, (f + 1) * face)
        block = unfold(blocks[f], face, face).astype(jnp.bfloat16)
        others_ref[f] = block
        local = dot(scaled[f], own_ref[f], ((1,), (0,))) + dot(scaled[f], block, ((1,), (0,)))
        start_ref[:, to] = local * half
        bases_ref[0:ncf, to] = own[f] * half
        bases_ref[ncf * (f + 1):ncf * (f + 2), to] = unfold(bases[f], even_rows(ncf), face)[0:ncf] * half
        all_rows.append(unfold(rows[f], *rows_ref.shape))
    all_rows_ref[...] = jnp.concatenate(all_rows, axis=0)
    early.wait()


def advance_kernel(face, vec_ref, blocks_ref, others_ref, iterate_ref, *refs):
    received, out_ref, own_ref, sem = refs[:-3], refs[-3], refs[-2], refs[-1]
    copy = pltpu.make_async_copy(blocks_ref, own_ref, sem)
    copy.start()
    weight = weights()
    scaled = scaled_faces(face, vec_ref, received)
    copy.wait()
    for f in range(6):
        to = slice(f * face, (f + 1) * face)
        local = dot(scaled[f], own_ref[f], ((1,), (0,))) + dot(scaled[f], others_ref[f], ((1,), (0,)))
        out_ref[:, to] = iterate_ref[:, to] + local * (0.5 * weight[f])


def coarse_update(slots_ref, rows_ref, bases_ref, count):
    devices, rows, lanes = slots_ref.shape
    slots = slots_ref[...]
    whole = jnp.concatenate([slots[:, :, i:i + count] for i in range(0, lanes, count)], axis=1)
    high, low = split(whole.reshape(devices * rows * (lanes // count), count))
    matrix = rows_ref[...]
    values = dot(matrix, high, ((1,), (0,))) + dot(matrix, low, ((1,), (0,)))
    high, low = split(values)
    bases = bases_ref[...]
    return dot(high, bases, ((0,), (0,))) + dot(low, bases, ((0,), (0,)))


def middle_kernel(face, slots_ref, rows_ref, bases_ref, start_ref, load_ref, first_ref, schur_ref, iterate_ref, local_ref, *refs):
    outs, near_ref, sems = refs[:-2], refs[-2], refs[-1]
    done = first_ref.shape[0]
    copies = []
    for i, (at, size) in enumerate(chunks(near_ref.shape[0])):
        copies.append(pltpu.make_async_copy(
            schur_ref.at[pl.ds(done + at, size)], near_ref.at[pl.ds(at, size)], sems.at[i]
        ))
        copies[i].start()
    iterate = start_ref[...] + coarse_update(slots_ref, rows_ref, bases_ref, start_ref.shape[0])
    iterate_ref[...] = iterate
    rounded = iterate.astype(jnp.bfloat16)
    local = load_ref[...] - dot(rounded[:, 0:done], first_ref[...], ((1,), (0,)))
    for i, (at, size) in enumerate(chunks(near_ref.shape[0])):
        copies[i].wait()
        local = local - dot(rounded[:, done + at:done + at + size], near_ref[at:at + size], ((1,), (0,)))
    local_ref[...] = local
    faces = [local[:, f * face:(f + 1) * face] for f in range(6)]
    for out, value in zip(outs, outgoing(faces)):
        out[...] = fold(value)


def last_kernel(slots_ref, rows_ref, bases_ref, start_ref, out_ref):
    update = coarse_update(slots_ref, rows_ref, bases_ref, start_ref.shape[0])
    out_ref[...] = (start_ref[...] + update).astype(jnp.bfloat16)


def body(load, schur, neumann, coarse_basis, coarse_rows):
    count, width = load.shape[3], load.shape[4]
    face = width // 6
    ncf, total = coarse_rows.shape[3], coarse_rows.shape[4]
    devices = total // ncf
    pack = max(128 // count, 1)
    while ncf % pack:
        pack -= 1
    schur2 = schur.reshape(width, width)
    swaps = len(links())
    flat_shape = (ncf * total // 256, 256)
    part = [f32(count * face // 128, 128)] * swaps
    big = [f32(spans(count, face, ncf, total)[-1].stop, 128)] * swaps
    slots = f32(devices, ncf // pack, pack * count)
    blocks_shape = bf16(6, face, face)
    early = min(width, 384)

    def gather(value):
        return lax.all_to_all(value, AXES, 0, 0)

    blocks = neumann.reshape(6, face, face)
    load_f, basis, rows, *sent = call(
        functools.partial(start_kernel, face),
        [f32(count, width), bf16(ncf, width), bf16(*flat_shape)] + big,
        load.reshape(count, width), blocks, coarse_basis.reshape(ncf, width),
        coarse_rows.reshape(flat_shape), far=(0, 1, 2, 3),
        scratch=[bf16(count, width), blocks_shape, pltpu.SemaphoreType.DMA((4,))],
    )
    received = swap(sent)
    (slot,) = call(functools.partial(residual_kernel, face, pack), [slots], load_f, basis, *received)
    whole = gather(slot)
    start, others, bases, all_rows, near = call(
        functools.partial(local_kernel, face, swaps),
        [f32(count, width), blocks_shape, f32(7 * ncf, width), f32(7 * flat_shape[0], 256), bf16(early, width)],
        load_f, blocks, basis, rows, schur2, *received, far=(1, 4),
        scratch=[blocks_shape, pltpu.SemaphoreType.DMA((2,))],
    )
    bases = bases.astype(jnp.bfloat16)
    all_rows = all_rows.reshape(7 * ncf, total).astype(jnp.bfloat16)
    iterate, vec, *sent = call(
        functools.partial(middle_kernel, face), [f32(count, width), f32(count, width)] + part,
        whole, all_rows, bases, start, load_f, near, schur2, far=(6,),
        scratch=[bf16(width - early, width), pltpu.SemaphoreType.DMA((len(chunks(width - early)),))],
    )
    received = swap(sent)
    (slot,) = call(functools.partial(residual_kernel, face, pack), [slots], vec, basis, *received)
    whole = gather(slot)
    (start,) = call(
        functools.partial(advance_kernel, face), [f32(count, width)], vec, blocks, others, iterate, *received,
        far=(1,),
        scratch=[blocks_shape, pltpu.SemaphoreType.DMA],
    )
    (result,) = call(last_kernel, [bf16(count, width)], whole, all_rows, bases, start)
    return result.reshape(load.shape)


def solution(mesh):
    placed = (
        P("gx", "gy", "gz", None, None),
        P("gx", "gy", "gz", None, None),
        P("gx", "gy", "gz", None, None, None),
        P("gx", "gy", "gz", None, None),
        P("gx", "gy", "gz", None, None),
    )
    return jax.shard_map(
        body, mesh=mesh, in_specs=placed, out_specs=P("gx", "gy", "gz", None, None), check_vma=False
    )
```

```python
import functools
import itertools

import jax
import jax.numpy as jnp
from jax import lax
from jax.experimental import pallas as pl
from jax.experimental.pallas import tpu as pltpu
from jax.sharding import PartitionSpec as P

AXES = ("gx", "gy", "gz")


FIRST = (("gz", 0), ("gz", 1), ("gx", 1), ("gx", 0), ("gy", 1), ("gy", 0))
SECOND = (("gy", 0), ("gz", 0), ("gz", 1), ("gx", 1), ("gy", 1), ("gx", 0))
IDLE = {"gx": ("gy", 2), "gy": ("gz", 1), "gz": ("gy", 2)}


def links(order):
    return [(axis, first) for axis, first in order if first + 1 < lax.axis_size(axis)]


def partners(axis, first):
    sizes = [lax.axis_size(name) for name in AXES]
    main = AXES.index(axis)
    spare, step = AXES.index(IDLE[axis][0]), IDLE[axis][1]
    pairs = []
    for at in itertools.product(*map(range, sizes)):
        to = list(at)
        if first <= at[main] < sizes[main] - (sizes[main] - first) % 2:
            to[main] += 1 - 2 * ((at[main] - first) % 2)
        else:
            to[spare] += step - 2 * step * (at[spare] // step % 2)
        if to[spare] < sizes[spare]:
            pairs.append(tuple((v[0] * sizes[1] + v[1]) * sizes[2] + v[2] for v in (at, to)))
    return pairs


def swap(buffers, order):
    return [lax.ppermute(buf, AXES, partners(*link)) for buf, link in zip(buffers, links(order))]


def odd_place(axis):
    return lax.rem(lax.axis_index(axis), 2) == 1


def weights():
    values = []
    for axis in AXES:
        place = lax.axis_index(axis)
        values.append(jnp.where(place > 0, 0.5, 1.0).astype(jnp.float32))
        values.append(jnp.where(place < lax.axis_size(axis) - 1, 0.5, 1.0).astype(jnp.float32))
    return values


def outgoing(faces, order):
    picked = []
    for axis, first in links(order):
        number = AXES.index(axis)
        lower, upper = faces[2 * number], faces[2 * number + 1]
        odd = odd_place(axis)
        picked.append(jnp.where(odd, lower, upper) if first == 0 else jnp.where(odd, upper, lower))
    return picked


def incoming(received, order):
    faces = []
    for axis in AXES:
        got = {first: buf for buf, (name, first) in zip(received, links(order)) if name == axis}
        zeros = jnp.zeros_like(received[0])
        even, other = got.get(0, zeros), got.get(1, zeros)
        odd = odd_place(axis)
        place = lax.axis_index(axis)
        faces.append(jnp.where(place > 0, jnp.where(odd, even, other), zeros))
        faces.append(jnp.where(place < lax.axis_size(axis) - 1, jnp.where(odd, other, even), zeros))
    return faces


def split(value):
    high = value.astype(jnp.bfloat16)
    low = (value - high.astype(jnp.float32)).astype(jnp.bfloat16)
    return high, low


def dot(a, b, dims):
    return lax.dot_general(a, b, (dims, ((), ())), preferred_element_type=jnp.float32)


def cut(ref, face):
    return [ref[:, f * face:(f + 1) * face].astype(jnp.float32) for f in range(6)]


def call(kernel, shapes, *args, far=(), far_out=(), scratch=()):
    vmem = pl.BlockSpec(memory_space=pltpu.VMEM)
    hbm = pl.BlockSpec(memory_space=pltpu.HBM)
    near = [a for i, a in enumerate(args) if i not in far] + list(shapes)
    near += [a for a in scratch if isinstance(a, jax.ShapeDtypeStruct)]
    size = sum(a.size * a.dtype.itemsize for a in near)
    scratch = [pltpu.VMEM(a.shape, a.dtype) if isinstance(a, jax.ShapeDtypeStruct) else a for a in scratch]
    return pl.pallas_call(
        kernel,
        out_shape=[pltpu.HBM(s.shape, s.dtype) if i in far_out else s for i, s in enumerate(shapes)],
        in_specs=[hbm if i in far else vmem for i in range(len(args))],
        out_specs=[hbm if i in far_out else vmem for i in range(len(shapes))],
        scratch_shapes=scratch,
        cost_estimate=pl.CostEstimate(flops=10 ** 7, bytes_accessed=size, transcendentals=0),
        compiler_params=pltpu.CompilerParams(vmem_limit_bytes=2 ** 21 + 3 * size // 2),
    )(*[pltpu.with_memory_space_constraint(a, pltpu.HBM) if i in far else a for i, a in enumerate(args)])


def chunks(size):
    return [(at, min(256, size - at)) for at in range(0, size, 256)]


def f32(*shape):
    return jax.ShapeDtypeStruct(shape, jnp.float32)


def bf16(*shape):
    return jax.ShapeDtypeStruct(shape, jnp.bfloat16)


def fold(value):
    rows, width = value.shape
    tail = width % 128
    pieces = [value[:, i:i + 128] for i in range(0, width - tail, 128)]
    if tail:
        step = rows * tail // 128
        last = value[:, width - tail:]
        pieces.append(jnp.concatenate([last[i:i + step] for i in range(0, rows, step)], axis=1))
    return jnp.concatenate(pieces, axis=0)


def unfold(value, rows, width):
    tail = width % 128
    full = width // 128
    pieces = [value[i * rows:(i + 1) * rows] for i in range(full)]
    if tail:
        last = value[full * rows:]
        pieces.append(jnp.concatenate([last[:, i:i + tail] for i in range(0, 128, tail)], axis=0))
    return jnp.concatenate(pieces, axis=1)


def even_rows(ncf):
    return 2 * ncf


def spans(count, face, ncf, total):
    sizes = [count * face // 128, face * face // 128, even_rows(ncf) * face // 128, ncf * total // 128]
    ends = [sum(sizes[:i + 1]) for i in range(4)]
    return [slice(e - n, e) for e, n in zip(ends, sizes)]


def start_kernel(face, load_ref, blocks_ref, basis_ref, rows_ref, vec_ref, bases_ref, flat_ref, *refs):
    outs, load_near, near_ref, sems = refs[:-3], refs[-3], refs[-2], refs[-1]
    pairs = ((load_ref, load_near), (basis_ref, bases_ref), (rows_ref, flat_ref), (blocks_ref, near_ref))
    copies = [pltpu.make_async_copy(far, near, sems.at[i]) for i, (far, near) in enumerate(pairs)]
    for copy in copies:
        copy.start()
    count, ncf = load_near.shape[0], bases_ref.shape[0]
    at = spans(count, face, ncf, flat_ref.shape[0] * flat_ref.shape[1] // ncf)
    copies[0].wait()
    vec_ref[...] = load_near[...].astype(jnp.float32)
    for out, value in zip(outs, outgoing(cut(vec_ref, face), FIRST)):
        out[at[0]] = fold(value)
    copies[1].wait()
    copies[2].wait()
    zeros = jnp.zeros((even_rows(ncf) - ncf, face), jnp.float32)
    flat = fold(flat_ref[...].astype(jnp.float32))
    for out, value in zip(outs, outgoing(cut(bases_ref, face), FIRST)):
        out[at[2]] = fold(jnp.concatenate([value, zeros], axis=0))
        out[at[3]] = flat
    copies[3].wait()
    for out, (axis, first) in zip(outs, links(FIRST)):
        upper = lax.rem(lax.axis_index(axis) + 1 + first, 2)
        out[at[1]] = fold(near_ref[2 * AXES.index(axis) + upper].astype(jnp.float32))


def scaled_faces(face, order, vec_ref, received):
    count = vec_ref.shape[0]
    own = cut(vec_ref, face)
    other = incoming([r[0:count * face // 128] for r in received], order)
    weight = weights()
    return [((own[f] + unfold(other[f], count, face)) * weight[f]).astype(jnp.bfloat16) for f in range(6)]


def residual_kernel(face, order, pack, vec_ref, basis_ref, *refs):
    received, slots_ref = refs[:-1], refs[-1]
    coarse = None
    for f, scaled in enumerate(scaled_faces(face, order, vec_ref, received)):
        part = dot(basis_ref[:, f * face:(f + 1) * face], scaled, ((1,), (1,)))
        coarse = part if coarse is None else coarse + part
    rows = coarse.shape[0] // pack
    slot = jnp.concatenate([coarse[i * rows:(i + 1) * rows] for i in range(pack)], axis=1)
    for d in range(slots_ref.shape[0]):
        slots_ref[d] = slot


def local_kernel(face, n_in, vec_ref, blocks_ref, basis_ref, rows_ref, schur_ref, *refs):
    count = vec_ref.shape[0]
    ncf = basis_ref.shape[0]
    received = refs[:n_in]
    start_ref, others_ref, bases_ref, all_rows_ref, near_ref, own_ref, other_ref, sems = refs[n_in:]
    copy = pltpu.make_async_copy(blocks_ref, own_ref, sems.at[0])
    early = pltpu.make_async_copy(schur_ref.at[pl.ds(0, near_ref.shape[0])], near_ref, sems.at[1])
    copy.start()
    early.start()
    at = spans(count, face, ncf, rows_ref.shape[0] * rows_ref.shape[1] // ncf)
    blocks, bases, rows = [incoming([r[at[i]] for r in received], FIRST) for i in (1, 2, 3)]
    weight = weights()
    bases_ref[...] = jnp.zeros_like(bases_ref)
    own = cut(basis_ref, face)
    all_rows = [rows_ref[...].astype(jnp.float32)]
    scaled = scaled_faces(face, FIRST, vec_ref, received)
    copy.wait()
    for f in range(6):
        half = 0.5 * weight[f]
        to = slice(f * face, (f + 1) * face)
        block = unfold(blocks[f], face, face).astype(jnp.bfloat16)
        other_ref[f] = block
        local = dot(scaled[f], own_ref[f], ((1,), (0,))) + dot(scaled[f], block, ((1,), (0,)))
        start_ref[:, to] = local * half
        bases_ref[0:ncf, to] = own[f] * half
        bases_ref[ncf * (f + 1):ncf * (f + 2), to] = unfold(bases[f], even_rows(ncf), face)[0:ncf] * half
        all_rows.append(unfold(rows[f], *rows_ref.shape))
    last = pltpu.make_async_copy(other_ref, others_ref, sems.at[0])
    last.start()
    all_rows_ref[...] = jnp.concatenate(all_rows, axis=0)
    early.wait()
    last.wait()


def advance_kernel(face, vec_ref, blocks_ref, others_ref, iterate_ref, *refs):
    received, out_ref, own_ref, other_ref, sems = refs[:-4], refs[-4], refs[-3], refs[-2], refs[-1]
    pairs = ((blocks_ref, own_ref), (others_ref, other_ref))
    copies = [pltpu.make_async_copy(far, near, sems.at[i]) for i, (far, near) in enumerate(pairs)]
    for copy in copies:
        copy.start()
    weight = weights()
    scaled = scaled_faces(face, SECOND, vec_ref, received)
    for copy in copies:
        copy.wait()
    for f in range(6):
        to = slice(f * face, (f + 1) * face)
        local = dot(scaled[f], own_ref[f], ((1,), (0,))) + dot(scaled[f], other_ref[f], ((1,), (0,)))
        out_ref[:, to] = iterate_ref[:, to] + local * (0.5 * weight[f])


def coarse_update(slots_ref, rows_ref, bases_ref, count):
    devices, rows, lanes = slots_ref.shape
    slots = slots_ref[...]
    whole = jnp.concatenate([slots[:, :, i:i + count] for i in range(0, lanes, count)], axis=1)
    high, low = split(whole.reshape(devices * rows * (lanes // count), count))
    matrix = rows_ref[...]
    values = dot(matrix, high, ((1,), (0,))) + dot(matrix, low, ((1,), (0,)))
    high, low = split(values)
    bases = bases_ref[...]
    return dot(high, bases, ((0,), (0,))) + dot(low, bases, ((0,), (0,)))


def middle_kernel(face, slots_ref, rows_ref, bases_ref, start_ref, load_ref, first_ref, schur_ref, iterate_ref, local_ref, *refs):
    outs, near_ref, sems = refs[:-2], refs[-2], refs[-1]
    done = first_ref.shape[0]
    copies = []
    for i, (at, size) in enumerate(chunks(near_ref.shape[0])):
        copies.append(pltpu.make_async_copy(
            schur_ref.at[pl.ds(done + at, size)], near_ref.at[pl.ds(at, size)], sems.at[i]
        ))
        copies[i].start()
    iterate = start_ref[...] + coarse_update(slots_ref, rows_ref, bases_ref, start_ref.shape[0])
    iterate_ref[...] = iterate
    rounded = iterate.astype(jnp.bfloat16)
    local = load_ref[...] - dot(rounded[:, 0:done], first_ref[...], ((1,), (0,)))
    for i, (at, size) in enumerate(chunks(near_ref.shape[0])):
        copies[i].wait()
        local = local - dot(rounded[:, done + at:done + at + size], near_ref[at:at + size], ((1,), (0,)))
    local_ref[...] = local
    faces = [local[:, f * face:(f + 1) * face] for f in range(6)]
    for out, value in zip(outs, outgoing(faces, SECOND)):
        out[...] = fold(value)


def last_kernel(slots_ref, rows_ref, bases_ref, start_ref, out_ref):
    update = coarse_update(slots_ref, rows_ref, bases_ref, start_ref.shape[0])
    out_ref[...] = (start_ref[...] + update).astype(jnp.bfloat16)


def body(load, schur, neumann, coarse_basis, coarse_rows):
    count, width = load.shape[3], load.shape[4]
    face = width // 6
    ncf, total = coarse_rows.shape[3], coarse_rows.shape[4]
    devices = total // ncf
    pack = max(128 // count, 1)
    while ncf % pack:
        pack -= 1
    schur2 = schur.reshape(width, width)
    swaps = len(links(FIRST))
    flat_shape = (ncf * total // 256, 256)
    part = [f32(count * face // 128, 128)] * swaps
    big = [f32(spans(count, face, ncf, total)[-1].stop, 128)] * swaps
    slots = f32(devices, ncf // pack, pack * count)
    blocks_shape = bf16(6, face, face)
    early = min(width, 768)

    def gather(value):
        return lax.all_to_all(value, AXES, 0, 0)

    blocks = neumann.reshape(6, face, face)
    load_f, basis, rows, *sent = call(
        functools.partial(start_kernel, face),
        [f32(count, width), bf16(ncf, width), bf16(*flat_shape)] + big,
        load.reshape(count, width), blocks, coarse_basis.reshape(ncf, width),
        coarse_rows.reshape(flat_shape), far=(0, 1, 2, 3),
        scratch=[bf16(count, width), blocks_shape, pltpu.SemaphoreType.DMA((4,))],
    )
    received = swap(sent, FIRST)
    (slot,) = call(functools.partial(residual_kernel, face, FIRST, pack), [slots], load_f, basis, *received)
    whole = gather(slot)
    start, others, bases, all_rows, near = call(
        functools.partial(local_kernel, face, swaps),
        [f32(count, width), blocks_shape, f32(7 * ncf, width), f32(7 * flat_shape[0], 256), bf16(early, width)],
        load_f, blocks, basis, rows, schur2, *received, far=(1, 4), far_out=(1,),
        scratch=[blocks_shape, blocks_shape, pltpu.SemaphoreType.DMA((2,))],
    )
    bases = bases.astype(jnp.bfloat16)
    all_rows = all_rows.reshape(7 * ncf, total).astype(jnp.bfloat16)
    iterate, vec, *sent = call(
        functools.partial(middle_kernel, face), [f32(count, width), f32(count, width)] + part,
        whole, all_rows, bases, start, load_f, near, schur2, far=(6,),
        scratch=[bf16(width - early, width), pltpu.SemaphoreType.DMA((len(chunks(width - early)),))],
    )
    received = swap(sent, SECOND)
    (slot,) = call(functools.partial(residual_kernel, face, SECOND, pack), [slots], vec, basis, *received)
    whole = gather(slot)
    (start,) = call(
        functools.partial(advance_kernel, face), [f32(count, width)], vec, blocks, others, iterate, *received,
        far=(1, 2), scratch=[blocks_shape, blocks_shape, pltpu.SemaphoreType.DMA((2,))],
    )
    (result,) = call(last_kernel, [bf16(count, width)], whole, all_rows, bases, start)
    return result.reshape(load.shape)


def solution(mesh):
    placed = (
        P("gx", "gy", "gz", None, None),
        P("gx", "gy", "gz", None, None),
        P("gx", "gy", "gz", None, None, None),
        P("gx", "gy", "gz", None, None),
        P("gx", "gy", "gz", None, None),
    )
    return jax.shard_map(
        body, mesh=mesh, in_specs=placed, out_specs=P("gx", "gy", "gz", None, None), check_vma=False
    )
```

```python
import functools
import itertools

import jax
import jax.numpy as jnp
from jax import lax
from jax.experimental import pallas as pl
from jax.experimental.pallas import tpu as pltpu
from jax.sharding import PartitionSpec as P

AXES = ("gx", "gy", "gz")


FIRST = (("gy", 1), ("gz", 0), ("gz", 1), ("gx", 0), ("gx", 1), ("gy", 0))
SECOND = (("gx", 0), ("gx", 1), ("gy", 1), ("gz", 0), ("gz", 1), ("gy", 0))
IDLE_FIRST = {"gx": ("gy", 1), "gy": ("gy", 0), "gz": ("gy", 2)}
IDLE_SECOND = {"gx": ("gy", 1), "gy": ("gy", 0), "gz": ("gy", 2)}


def links(order):
    return [(axis, first) for axis, first in order if first + 1 < lax.axis_size(axis)]


def partners(axis, first, idle):
    sizes = [lax.axis_size(name) for name in AXES]
    main = AXES.index(axis)
    spare, step = idle.get(axis, (axis, 0))
    spare = AXES.index(spare)
    pairs = []
    for at in itertools.product(*map(range, sizes)):
        to = list(at)
        if first <= at[main] < sizes[main] - (sizes[main] - first) % 2:
            to[main] += 1 - 2 * ((at[main] - first) % 2)
        elif step:
            to[spare] += step - 2 * step * (at[spare] // step % 2)
        else:
            to[spare] = sizes[spare] - 1 - at[spare]
        if to[spare] < sizes[spare]:
            pairs.append(tuple((v[0] * sizes[1] + v[1]) * sizes[2] + v[2] for v in (at, to)))
    return pairs


def swap(buffers, order, idle):
    return [lax.ppermute(buf, AXES, partners(*link, idle)) for buf, link in zip(buffers, links(order))]


def odd_place(axis):
    return lax.rem(lax.axis_index(axis), 2) == 1


def weights():
    values = []
    for axis in AXES:
        place = lax.axis_index(axis)
        values.append(jnp.where(place > 0, 0.5, 1.0).astype(jnp.float32))
        values.append(jnp.where(place < lax.axis_size(axis) - 1, 0.5, 1.0).astype(jnp.float32))
    return values


def outgoing(faces, order):
    picked = []
    for axis, first in links(order):
        number = AXES.index(axis)
        lower, upper = faces[2 * number], faces[2 * number + 1]
        odd = odd_place(axis)
        picked.append(jnp.where(odd, lower, upper) if first == 0 else jnp.where(odd, upper, lower))
    return picked


def incoming(received, order):
    faces = []
    for axis in AXES:
        got = {first: buf for buf, (name, first) in zip(received, links(order)) if name == axis}
        zeros = jnp.zeros_like(received[0])
        even, other = got.get(0, zeros), got.get(1, zeros)
        odd = odd_place(axis)
        place = lax.axis_index(axis)
        faces.append(jnp.where(place > 0, jnp.where(odd, even, other), zeros))
        faces.append(jnp.where(place < lax.axis_size(axis) - 1, jnp.where(odd, other, even), zeros))
    return faces


def split(value):
    high = value.astype(jnp.bfloat16)
    low = (value - high.astype(jnp.float32)).astype(jnp.bfloat16)
    return high, low


def dot(a, b, dims):
    return lax.dot_general(a, b, (dims, ((), ())), preferred_element_type=jnp.float32)


def cut(ref, face):
    return [ref[:, f * face:(f + 1) * face].astype(jnp.float32) for f in range(6)]


def call(kernel, shapes, *args, far=(), far_out=(), scratch=()):
    vmem = pl.BlockSpec(memory_space=pltpu.VMEM)
    hbm = pl.BlockSpec(memory_space=pltpu.HBM)
    near = [a for i, a in enumerate(args) if i not in far] + list(shapes)
    near += [a for a in scratch if isinstance(a, jax.ShapeDtypeStruct)]
    size = sum(a.size * a.dtype.itemsize for a in near)
    scratch = [pltpu.VMEM(a.shape, a.dtype) if isinstance(a, jax.ShapeDtypeStruct) else a for a in scratch]
    return pl.pallas_call(
        kernel,
        out_shape=[pltpu.HBM(s.shape, s.dtype) if i in far_out else s for i, s in enumerate(shapes)],
        in_specs=[hbm if i in far else vmem for i in range(len(args))],
        out_specs=[hbm if i in far_out else vmem for i in range(len(shapes))],
        scratch_shapes=scratch,
        cost_estimate=pl.CostEstimate(flops=10 ** 7, bytes_accessed=size, transcendentals=0),
        compiler_params=pltpu.CompilerParams(vmem_limit_bytes=2 ** 21 + 3 * size // 2),
    )(*[pltpu.with_memory_space_constraint(a, pltpu.HBM) if i in far else a for i, a in enumerate(args)])


def f32(*shape):
    return jax.ShapeDtypeStruct(shape, jnp.float32)


def bf16(*shape):
    return jax.ShapeDtypeStruct(shape, jnp.bfloat16)


def fold(value):
    rows, width = value.shape
    tail = width % 128
    pieces = [value[:, i:i + 128] for i in range(0, width - tail, 128)]
    if tail:
        step = rows * tail // 128
        last = value[:, width - tail:]
        pieces.append(jnp.concatenate([last[i:i + step] for i in range(0, rows, step)], axis=1))
    return jnp.concatenate(pieces, axis=0)


def unfold(value, rows, width):
    tail = width % 128
    full = width // 128
    pieces = [value[i * rows:(i + 1) * rows] for i in range(full)]
    if tail:
        last = value[full * rows:]
        pieces.append(jnp.concatenate([last[:, i:i + tail] for i in range(0, 128, tail)], axis=0))
    return jnp.concatenate(pieces, axis=1)


def even_rows(ncf):
    return 2 * ncf


def spans(count, face, ncf, total):
    sizes = [count * face // 128, face * face // 128, even_rows(ncf) * face // 128, ncf * total // 128]
    ends = [sum(sizes[:i + 1]) for i in range(4)]
    return [slice(e - n, e) for e, n in zip(ends, sizes)]


def start_kernel(face, load_ref, blocks_ref, basis_ref, rows_ref, vec_ref, bases_ref, flat_ref, *refs):
    outs, load_near, near_ref, sems = refs[:-3], refs[-3], refs[-2], refs[-1]
    pairs = ((load_ref, load_near), (basis_ref, bases_ref), (rows_ref, flat_ref), (blocks_ref, near_ref))
    copies = [pltpu.make_async_copy(far, near, sems.at[i]) for i, (far, near) in enumerate(pairs)]
    for copy in copies:
        copy.start()
    count, ncf = load_near.shape[0], bases_ref.shape[0]
    at = spans(count, face, ncf, flat_ref.shape[0] * flat_ref.shape[1] // ncf)
    copies[0].wait()
    vec_ref[...] = load_near[...].astype(jnp.float32)
    for out, value in zip(outs, outgoing(cut(vec_ref, face), FIRST)):
        out[at[0]] = fold(value)
    copies[1].wait()
    copies[2].wait()
    zeros = jnp.zeros((even_rows(ncf) - ncf, face), jnp.float32)
    flat = fold(flat_ref[...].astype(jnp.float32))
    for out, value in zip(outs, outgoing(cut(bases_ref, face), FIRST)):
        out[at[2]] = fold(jnp.concatenate([value, zeros], axis=0))
        out[at[3]] = flat
    copies[3].wait()
    for out, (axis, first) in zip(outs, links(FIRST)):
        upper = lax.rem(lax.axis_index(axis) + 1 + first, 2)
        out[at[1]] = fold(near_ref[2 * AXES.index(axis) + upper].astype(jnp.float32))


def scaled_faces(face, order, vec_ref, received):
    count = vec_ref.shape[0]
    own = cut(vec_ref, face)
    other = incoming([r[0:count * face // 128] for r in received], order)
    weight = weights()
    return [((own[f] + unfold(other[f], count, face)) * weight[f]).astype(jnp.bfloat16) for f in range(6)]


def residual_kernel(face, order, pack, vec_ref, basis_ref, *refs):
    received, slots_ref = refs[:-1], refs[-1]
    coarse = None
    for f, scaled in enumerate(scaled_faces(face, order, vec_ref, received)):
        part = dot(basis_ref[:, f * face:(f + 1) * face], scaled, ((1,), (1,)))
        coarse = part if coarse is None else coarse + part
    rows = coarse.shape[0] // pack
    slot = jnp.concatenate([coarse[i * rows:(i + 1) * rows] for i in range(pack)], axis=1)
    for d in range(slots_ref.shape[0]):
        slots_ref[d] = slot


def local_kernel(face, n_in, vec_ref, blocks_ref, basis_ref, rows_ref, schur_ref, *refs):
    count = vec_ref.shape[0]
    ncf = basis_ref.shape[0]
    received = refs[:n_in]
    start_ref, others_ref, bases_ref, all_rows_ref, near_ref, own_ref, other_ref, sems = refs[n_in:]
    copy = pltpu.make_async_copy(blocks_ref, own_ref, sems.at[0])
    early = pltpu.make_async_copy(schur_ref.at[pl.ds(0, near_ref.shape[0])], near_ref, sems.at[1])
    copy.start()
    early.start()
    at = spans(count, face, ncf, rows_ref.shape[0] * rows_ref.shape[1] // ncf)
    blocks, bases, rows = [incoming([r[at[i]] for r in received], FIRST) for i in (1, 2, 3)]
    weight = weights()
    bases_ref[...] = jnp.zeros_like(bases_ref)
    own = cut(basis_ref, face)
    all_rows = [rows_ref[...].astype(jnp.float32)]
    scaled = scaled_faces(face, FIRST, vec_ref, received)
    copy.wait()
    for f in range(6):
        half = 0.5 * weight[f]
        to = slice(f * face, (f + 1) * face)
        block = unfold(blocks[f], face, face).astype(jnp.bfloat16)
        other_ref[f] = block
        local = dot(scaled[f], own_ref[f], ((1,), (0,))) + dot(scaled[f], block, ((1,), (0,)))
        start_ref[:, to] = local * half
        bases_ref[0:ncf, to] = own[f] * half
        bases_ref[ncf * (f + 1):ncf * (f + 2), to] = unfold(bases[f], even_rows(ncf), face)[0:ncf] * half
        all_rows.append(unfold(rows[f], *rows_ref.shape))
    last = pltpu.make_async_copy(other_ref, others_ref, sems.at[0])
    last.start()
    all_rows_ref[...] = jnp.concatenate(all_rows, axis=0)
    early.wait()
    last.wait()


def advance_kernel(face, vec_ref, blocks_ref, others_ref, iterate_ref, *refs):
    received, out_ref, own_ref, other_ref, sems = refs[:-4], refs[-4], refs[-3], refs[-2], refs[-1]
    pairs = ((blocks_ref, own_ref), (others_ref, other_ref))
    copies = [pltpu.make_async_copy(far, near, sems.at[i]) for i, (far, near) in enumerate(pairs)]
    for copy in copies:
        copy.start()
    weight = weights()
    scaled = scaled_faces(face, SECOND, vec_ref, received)
    for copy in copies:
        copy.wait()
    for f in range(6):
        to = slice(f * face, (f + 1) * face)
        local = dot(scaled[f], own_ref[f], ((1,), (0,))) + dot(scaled[f], other_ref[f], ((1,), (0,)))
        out_ref[:, to] = iterate_ref[:, to] + local * (0.5 * weight[f])


def coarse_update(slots_ref, rows_ref, bases_ref, count):
    devices, rows, lanes = slots_ref.shape
    slots = slots_ref[...]
    whole = jnp.concatenate([slots[:, :, i:i + count] for i in range(0, lanes, count)], axis=1)
    high, low = split(whole.reshape(devices * rows * (lanes // count), count))
    matrix = rows_ref[...]
    values = dot(matrix, high, ((1,), (0,))) + dot(matrix, low, ((1,), (0,)))
    high, low = split(values)
    bases = bases_ref[...]
    return dot(high, bases, ((0,), (0,))) + dot(low, bases, ((0,), (0,)))


def middle_kernel(face, slots_ref, rows_ref, bases_ref, start_ref, load_ref, first_ref, schur_ref, iterate_ref, local_ref, *refs):
    outs, near_ref, sems = refs[:-2], refs[-2], refs[-1]
    done = first_ref.shape[0]
    size = near_ref.shape[0] // sems.shape[0]

    def piece(i):
        near = pl.ds(pl.multiple_of(i * size, size), size)
        far = pl.ds(pl.multiple_of(done + i * size, size), size)
        return pltpu.make_async_copy(schur_ref.at[far], near_ref.at[near], sems.at[i])

    lax.fori_loop(0, sems.shape[0], lambda i, _: piece(i).start(), None)
    iterate = start_ref[...] + coarse_update(slots_ref, rows_ref, bases_ref, start_ref.shape[0])
    iterate_ref[...] = iterate
    rounded = iterate.astype(jnp.bfloat16)
    for i in range(sems.shape[0]):
        piece(i).wait()
    for number, axis in enumerate(AXES):
        at = slice(2 * number * face, 2 * (number + 1) * face)
        local = load_ref[:, at] - dot(rounded[:, 0:done], first_ref[:, at], ((1,), (0,)))
        local = local - dot(rounded[:, done:], near_ref[:, at], ((1,), (0,)))
        local_ref[:, at] = local
        lower, upper = local[:, 0:face], local[:, face:]
        odd = odd_place(axis)
        for out, (name, first) in zip(outs, links(SECOND)):
            if name == axis:
                out[...] = fold(jnp.where(odd, lower, upper) if first == 0 else jnp.where(odd, upper, lower))


def last_kernel(slots_ref, rows_ref, bases_ref, start_ref, out_ref):
    update = coarse_update(slots_ref, rows_ref, bases_ref, start_ref.shape[0])
    out_ref[...] = (start_ref[...] + update).astype(jnp.bfloat16)


def body(load, schur, neumann, coarse_basis, coarse_rows):
    count, width = load.shape[3], load.shape[4]
    face = width // 6
    ncf, total = coarse_rows.shape[3], coarse_rows.shape[4]
    devices = total // ncf
    pack = max(128 // count, 1)
    while ncf % pack:
        pack -= 1
    schur2 = schur.reshape(width, width)
    swaps = len(links(FIRST))
    flat_shape = (ncf * total // 256, 256)
    part = [f32(count * face // 128, 128)] * swaps
    big = [f32(spans(count, face, ncf, total)[-1].stop, 128)] * swaps
    slots = f32(devices, ncf // pack, pack * count)
    blocks_shape = bf16(6, face, face)
    early = min(width, 768)

    def gather(value):
        return lax.all_to_all(value, AXES, 0, 0)

    blocks = neumann.reshape(6, face, face)
    load_f, basis, rows, *sent = call(
        functools.partial(start_kernel, face),
        [f32(count, width), bf16(ncf, width), bf16(*flat_shape)] + big,
        load.reshape(count, width), blocks, coarse_basis.reshape(ncf, width),
        coarse_rows.reshape(flat_shape), far=(0, 1, 2, 3),
        scratch=[bf16(count, width), blocks_shape, pltpu.SemaphoreType.DMA((4,))],
    )
    received = swap(sent, FIRST, IDLE_FIRST)
    (slot,) = call(functools.partial(residual_kernel, face, FIRST, pack), [slots], load_f, basis, *received)
    whole = gather(slot)
    start, others, bases, all_rows, near = call(
        functools.partial(local_kernel, face, swaps),
        [f32(count, width), blocks_shape, f32(7 * ncf, width), f32(7 * flat_shape[0], 256), bf16(early, width)],
        load_f, blocks, basis, rows, schur2, *received, far=(1, 4), far_out=(1,),
        scratch=[blocks_shape, blocks_shape, pltpu.SemaphoreType.DMA((2,))],
    )
    bases = bases.astype(jnp.bfloat16)
    all_rows = all_rows.reshape(7 * ncf, total).astype(jnp.bfloat16)
    iterate, vec, *sent = call(
        functools.partial(middle_kernel, face), [f32(count, width), f32(count, width)] + part,
        whole, all_rows, bases, start, load_f, near, schur2, far=(6,),
        scratch=[bf16(width - early, width), pltpu.SemaphoreType.DMA((3,))],
    )
    received = swap(sent, SECOND, IDLE_SECOND)
    (slot,) = call(functools.partial(residual_kernel, face, SECOND, pack), [slots], vec, basis, *received)
    whole = gather(slot)
    (start,) = call(
        functools.partial(advance_kernel, face), [f32(count, width)], vec, blocks, others, iterate, *received,
        far=(1, 2), scratch=[blocks_shape, blocks_shape, pltpu.SemaphoreType.DMA((2,))],
    )
    (result,) = call(last_kernel, [bf16(count, width)], whole, all_rows, bases, start)
    return result.reshape(load.shape)


def solution(mesh):
    placed = (
        P("gx", "gy", "gz", None, None),
        P("gx", "gy", "gz", None, None),
        P("gx", "gy", "gz", None, None, None),
        P("gx", "gy", "gz", None, None),
        P("gx", "gy", "gz", None, None),
    )
    return jax.shard_map(
        body, mesh=mesh, in_specs=placed, out_specs=P("gx", "gy", "gz", None, None), check_vma=False
    )
```

```python
import functools
import itertools
import math

import jax
import jax.numpy as jnp
from jax import lax
from jax.experimental import pallas as pl
from jax.experimental.pallas import tpu as pltpu
from jax.sharding import PartitionSpec as P

AXES = ("gx", "gy", "gz")


FIRST = (("gy", 1), ("gz", 0), ("gz", 1), ("gx", 0), ("gx", 1), ("gy", 0))
SECOND = (("gx", 0), ("gx", 1), ("gy", 1), ("gz", 0), ("gz", 1), ("gy", 0))
BLOCKS = (("gy", 1), ("gz", 0), ("gz", 1), ("gx", 0), ("gx", 1), ("gy", 0))
IDLE_BLOCKS = {"gx": ("gy", 1), "gy": ("gy", 0), "gz": ("gy", 2)}
IDLE_FIRST = {"gx": ("gy", 1), "gy": ("gy", 0), "gz": ("gy", 2)}
IDLE_SECOND = {"gx": ("gy", 1), "gy": ("gy", 0), "gz": ("gy", 2)}


def links(order):
    return [(axis, first) for axis, first in order if first + 1 < lax.axis_size(axis)]


def partners(axis, first, idle):
    sizes = [lax.axis_size(name) for name in AXES]
    main = AXES.index(axis)
    spare, step = idle.get(axis, (axis, 0))
    spare = AXES.index(spare)
    pairs = []
    for at in itertools.product(*map(range, sizes)):
        to = list(at)
        if first <= at[main] < sizes[main] - (sizes[main] - first) % 2:
            to[main] += 1 - 2 * ((at[main] - first) % 2)
        elif step:
            to[spare] += step - 2 * step * (at[spare] // step % 2)
        else:
            to[spare] = sizes[spare] - 1 - at[spare]
        if to[spare] < sizes[spare]:
            pairs.append(tuple((v[0] * sizes[1] + v[1]) * sizes[2] + v[2] for v in (at, to)))
    return pairs


def swap(buffers, order, idle):
    return [lax.ppermute(buf, AXES, partners(*link, idle)) for buf, link in zip(buffers, links(order))]


def odd_place(axis):
    return lax.rem(lax.axis_index(axis), 2) == 1


def weights():
    values = []
    for axis in AXES:
        place = lax.axis_index(axis)
        values.append(jnp.where(place > 0, 0.5, 1.0).astype(jnp.float32))
        values.append(jnp.where(place < lax.axis_size(axis) - 1, 0.5, 1.0).astype(jnp.float32))
    return values


def outgoing(faces, order):
    picked = []
    for axis, first in links(order):
        number = AXES.index(axis)
        lower, upper = faces[2 * number], faces[2 * number + 1]
        odd = odd_place(axis)
        picked.append(jnp.where(odd, lower, upper) if first == 0 else jnp.where(odd, upper, lower))
    return picked


def incoming(received, order):
    faces = []
    for axis in AXES:
        got = {first: buf for buf, (name, first) in zip(received, links(order)) if name == axis}
        zeros = jnp.zeros_like(received[0])
        even, other = got.get(0, zeros), got.get(1, zeros)
        odd = odd_place(axis)
        place = lax.axis_index(axis)
        faces.append(jnp.where(place > 0, jnp.where(odd, even, other), zeros))
        faces.append(jnp.where(place < lax.axis_size(axis) - 1, jnp.where(odd, other, even), zeros))
    return faces


def split(value):
    high = value.astype(jnp.bfloat16)
    low = (value - high.astype(jnp.float32)).astype(jnp.bfloat16)
    return high, low


def dot(a, b, dims):
    return lax.dot_general(a, b, (dims, ((), ())), preferred_element_type=jnp.float32)


def cut(ref, face):
    return [ref[:, f * face:(f + 1) * face].astype(jnp.float32) for f in range(6)]


def call(kernel, shapes, *args, far=(), far_out=(), scratch=()):
    vmem = pl.BlockSpec(memory_space=pltpu.VMEM)
    hbm = pl.BlockSpec(memory_space=pltpu.HBM)
    near = [a for i, a in enumerate(args) if i not in far] + list(shapes)
    near += [a for a in scratch if isinstance(a, jax.ShapeDtypeStruct)]
    size = sum(a.size * a.dtype.itemsize for a in near)
    scratch = [pltpu.VMEM(a.shape, a.dtype) if isinstance(a, jax.ShapeDtypeStruct) else a for a in scratch]
    return pl.pallas_call(
        kernel,
        out_shape=[pltpu.HBM(s.shape, s.dtype) if i in far_out else s for i, s in enumerate(shapes)],
        in_specs=[hbm if i in far else vmem for i in range(len(args))],
        out_specs=[hbm if i in far_out else vmem for i in range(len(shapes))],
        scratch_shapes=scratch,
        cost_estimate=pl.CostEstimate(flops=10 ** 7, bytes_accessed=size, transcendentals=0),
        compiler_params=pltpu.CompilerParams(vmem_limit_bytes=2 ** 21 + 3 * size // 2),
    )(*[pltpu.with_memory_space_constraint(a, pltpu.HBM) if i in far else a for i, a in enumerate(args)])


def f32(*shape):
    return jax.ShapeDtypeStruct(shape, jnp.float32)


def bf16(*shape):
    return jax.ShapeDtypeStruct(shape, jnp.bfloat16)


def fold(value):
    rows, width = value.shape
    tail = width % 128
    pieces = [value[:, i:i + 128] for i in range(0, width - tail, 128)]
    if tail:
        step = rows * tail // 128
        last = value[:, width - tail:]
        pieces.append(jnp.concatenate([last[i:i + step] for i in range(0, rows, step)], axis=1))
    return jnp.concatenate(pieces, axis=0)


def unfold(value, rows, width):
    tail = width % 128
    full = width // 128
    pieces = [value[i * rows:(i + 1) * rows] for i in range(full)]
    if tail:
        last = value[full * rows:]
        pieces.append(jnp.concatenate([last[:, i:i + tail] for i in range(0, 128, tail)], axis=0))
    return jnp.concatenate(pieces, axis=1)


def even_rows(ncf):
    return 2 * ncf


def spans(face, ncf, total):
    sizes = [face * face // 128, even_rows(ncf) * face // 128, ncf * total // 128]
    ends = [sum(sizes[:i + 1]) for i in range(3)]
    return [slice(e - n, e) for e, n in zip(ends, sizes)]


def start_kernel(face, load_ref, blocks_ref, basis_ref, rows_ref, vec_ref, bases_ref, flat_ref, *refs):
    load_near, near_ref, sems = refs[-3:]
    swaps = (len(refs) - 3) // 2
    outs, block_outs = refs[:swaps], refs[swaps:2 * swaps]
    pairs = ((load_ref, load_near), (basis_ref, bases_ref), (rows_ref, flat_ref), (blocks_ref, near_ref))
    copies = [pltpu.make_async_copy(far, near, sems.at[i]) for i, (far, near) in enumerate(pairs)]
    for copy in copies:
        copy.start()
    ncf = bases_ref.shape[0]
    at = spans(face, ncf, flat_ref.shape[0] * flat_ref.shape[1] // ncf)
    copies[0].wait()
    vec_ref[...] = load_near[...].astype(jnp.float32)
    for out, value in zip(outs, outgoing(cut(vec_ref, face), FIRST)):
        out[...] = fold(value)
    copies[1].wait()
    copies[2].wait()
    zeros = jnp.zeros((even_rows(ncf) - ncf, face), jnp.float32)
    flat = fold(flat_ref[...].astype(jnp.float32))
    for out, value in zip(block_outs, outgoing(cut(bases_ref, face), BLOCKS)):
        out[at[1]] = fold(jnp.concatenate([value, zeros], axis=0))
        out[at[2]] = flat
    copies[3].wait()
    for out, (axis, first) in zip(block_outs, links(BLOCKS)):
        upper = lax.rem(lax.axis_index(axis) + 1 + first, 2)
        out[at[0]] = fold(near_ref[2 * AXES.index(axis) + upper].astype(jnp.float32))


def scaled_faces(face, order, vec_ref, received):
    count = vec_ref.shape[0]
    own = cut(vec_ref, face)
    other = incoming([r[...] for r in received], order)
    weight = weights()
    return [((own[f] + unfold(other[f], count, face)) * weight[f]).astype(jnp.bfloat16) for f in range(6)]


def residual_kernel(face, order, pack, vec_ref, basis_ref, *refs):
    received, slots_ref = refs[:-1], refs[-1]
    coarse = None
    for f, scaled in enumerate(scaled_faces(face, order, vec_ref, received)):
        part = dot(basis_ref[:, f * face:(f + 1) * face], scaled, ((1,), (1,)))
        coarse = part if coarse is None else coarse + part
    rows = coarse.shape[0] // pack
    slot = jnp.concatenate([coarse[i * rows:(i + 1) * rows] for i in range(pack)], axis=1)
    for d in range(slots_ref.shape[0]):
        slots_ref[d] = slot


def local_kernel(face, n_in, vec_ref, blocks_ref, basis_ref, rows_ref, schur_ref, *refs):
    ncf = basis_ref.shape[0]
    received, blocks_received = refs[:n_in], refs[n_in:2 * n_in]
    start_ref, others_ref, bases_ref, all_rows_ref, near_ref, own_ref, other_ref, sems = refs[2 * n_in:]
    copy = pltpu.make_async_copy(blocks_ref, own_ref, sems.at[0])
    early = pltpu.make_async_copy(schur_ref.at[pl.ds(0, near_ref.shape[0])], near_ref, sems.at[1])
    copy.start()
    early.start()
    at = spans(face, ncf, rows_ref.shape[0] * rows_ref.shape[1] // ncf)
    blocks, bases, rows = [incoming([r[part] for r in blocks_received], BLOCKS) for part in at]
    weight = weights()
    bases_ref[...] = jnp.zeros_like(bases_ref)
    own = cut(basis_ref, face)
    all_rows = [rows_ref[...].astype(jnp.float32)]
    scaled = scaled_faces(face, FIRST, vec_ref, received)
    copy.wait()
    for f in range(6):
        half = 0.5 * weight[f]
        to = slice(f * face, (f + 1) * face)
        block = unfold(blocks[f], face, face).astype(jnp.bfloat16)
        other_ref[f] = block
        local = dot(scaled[f], own_ref[f], ((1,), (0,))) + dot(scaled[f], block, ((1,), (0,)))
        start_ref[:, to] = local * half
        bases_ref[0:ncf, to] = own[f] * half
        bases_ref[ncf * (f + 1):ncf * (f + 2), to] = unfold(bases[f], even_rows(ncf), face)[0:ncf] * half
        all_rows.append(unfold(rows[f], *rows_ref.shape))
    last = pltpu.make_async_copy(other_ref, others_ref, sems.at[0])
    last.start()
    all_rows_ref[...] = jnp.concatenate(all_rows, axis=0)
    early.wait()
    last.wait()


def advance_kernel(face, vec_ref, blocks_ref, others_ref, iterate_ref, *refs):
    received, out_ref, own_ref, other_ref, sems = refs[:-4], refs[-4], refs[-3], refs[-2], refs[-1]
    pairs = ((blocks_ref, own_ref), (others_ref, other_ref))
    copies = [pltpu.make_async_copy(far, near, sems.at[i]) for i, (far, near) in enumerate(pairs)]
    for copy in copies:
        copy.start()
    weight = weights()
    scaled = scaled_faces(face, SECOND, vec_ref, received)
    for copy in copies:
        copy.wait()
    for f in range(6):
        to = slice(f * face, (f + 1) * face)
        local = dot(scaled[f], own_ref[f], ((1,), (0,))) + dot(scaled[f], other_ref[f], ((1,), (0,)))
        out_ref[:, to] = iterate_ref[:, to] + local * (0.5 * weight[f])


def coarse_update(slots_ref, rows_ref, bases_ref, count):
    devices, rows, lanes = slots_ref.shape
    slots = slots_ref[...]
    whole = jnp.concatenate([slots[:, :, i:i + count] for i in range(0, lanes, count)], axis=1)
    high, low = split(whole.reshape(devices * rows * (lanes // count), count))
    matrix = rows_ref[...]
    values = dot(matrix, high, ((1,), (0,))) + dot(matrix, low, ((1,), (0,)))
    high, low = split(values)
    bases = bases_ref[...]
    return dot(high, bases, ((0,), (0,))) + dot(low, bases, ((0,), (0,)))


def middle_kernel(face, slots_ref, rows_ref, bases_ref, start_ref, load_ref, first_ref, schur_ref, iterate_ref, local_ref, *refs):
    outs, near_ref, sems = refs[:-2], refs[-2], refs[-1]
    done = first_ref.shape[0]
    size = near_ref.shape[0] // sems.shape[0]

    def piece(i):
        near = pl.ds(pl.multiple_of(i * size, size), size)
        far = pl.ds(pl.multiple_of(done + i * size, size), size)
        return pltpu.make_async_copy(schur_ref.at[far], near_ref.at[near], sems.at[i])

    lax.fori_loop(0, sems.shape[0], lambda i, _: piece(i).start(), None)
    iterate = start_ref[...] + coarse_update(slots_ref, rows_ref, bases_ref, start_ref.shape[0])
    iterate_ref[...] = iterate
    rounded = iterate.astype(jnp.bfloat16)
    for i in range(sems.shape[0]):
        piece(i).wait()
    for number, axis in enumerate(AXES):
        at = slice(2 * number * face, 2 * (number + 1) * face)
        local = load_ref[:, at] - dot(rounded[:, 0:done], first_ref[:, at], ((1,), (0,)))
        local = local - dot(rounded[:, done:], near_ref[:, at], ((1,), (0,)))
        local_ref[:, at] = local
        lower, upper = local[:, 0:face], local[:, face:]
        odd = odd_place(axis)
        for out, (name, first) in zip(outs, links(SECOND)):
            if name == axis:
                out[...] = fold(jnp.where(odd, lower, upper) if first == 0 else jnp.where(odd, upper, lower))


def last_kernel(slots_ref, rows_ref, bases_ref, start_ref, out_ref):
    update = coarse_update(slots_ref, rows_ref, bases_ref, start_ref.shape[0])
    out_ref[...] = (start_ref[...] + update).astype(jnp.bfloat16)


def body(load, schur, neumann, coarse_basis, coarse_rows):
    count, width = load.shape[3], load.shape[4]
    face = width // 6
    ncf, total = coarse_rows.shape[3], coarse_rows.shape[4]
    devices = total // ncf
    pack = max(128 // count, 1)
    while ncf % pack:
        pack -= 1
    schur2 = schur.reshape(width, width)
    swaps = len(links(FIRST))
    flat_shape = (ncf * total // 256, 256)
    part = [f32(count * face // 128, 128)] * swaps
    big = [f32(spans(face, ncf, total)[-1].stop, 128)] * swaps
    slots = f32(devices, ncf // pack, pack * count)
    blocks_shape = bf16(6, face, face)
    early = min(width, 640)

    def gather(value):
        return lax.all_to_all(value, AXES, 0, 0)

    blocks = neumann.reshape(6, face, face)
    load_f, basis, rows, *sent = call(
        functools.partial(start_kernel, face),
        [f32(count, width), bf16(ncf, width), bf16(*flat_shape)] + part + big,
        load.reshape(count, width), blocks, coarse_basis.reshape(ncf, width),
        coarse_rows.reshape(flat_shape), far=(0, 1, 2, 3),
        scratch=[bf16(count, width), blocks_shape, pltpu.SemaphoreType.DMA((4,))],
    )
    received = swap(sent[:swaps], FIRST, IDLE_FIRST)
    blocks_received = swap(sent[swaps:], BLOCKS, IDLE_BLOCKS)
    (slot,) = call(functools.partial(residual_kernel, face, FIRST, pack), [slots], load_f, basis, *received)
    whole = gather(slot)
    start, others, bases, all_rows, near = call(
        functools.partial(local_kernel, face, swaps),
        [f32(count, width), blocks_shape, f32(7 * ncf, width), f32(7 * flat_shape[0], 256), bf16(early, width)],
        load_f, blocks, basis, rows, schur2, *received, *blocks_received, far=(1, 4), far_out=(1,),
        scratch=[blocks_shape, blocks_shape, pltpu.SemaphoreType.DMA((2,))],
    )
    bases = bases.astype(jnp.bfloat16)
    all_rows = all_rows.reshape(7 * ncf, total).astype(jnp.bfloat16)
    iterate, vec, *sent = call(
        functools.partial(middle_kernel, face), [f32(count, width), f32(count, width)] + part,
        whole, all_rows, bases, start, load_f, near, schur2, far=(6,),
        scratch=[bf16(width - early, width), pltpu.SemaphoreType.DMA(((width - early) // math.gcd(early, width),))],
    )
    received = swap(sent, SECOND, IDLE_SECOND)
    (slot,) = call(functools.partial(residual_kernel, face, SECOND, pack), [slots], vec, basis, *received)
    whole = gather(slot)
    (start,) = call(
        functools.partial(advance_kernel, face), [f32(count, width)], vec, blocks, others, iterate, *received,
        far=(1, 2), scratch=[blocks_shape, blocks_shape, pltpu.SemaphoreType.DMA((2,))],
    )
    (result,) = call(last_kernel, [bf16(count, width)], whole, all_rows, bases, start)
    return result.reshape(load.shape)


def solution(mesh):
    placed = (
        P("gx", "gy", "gz", None, None),
        P("gx", "gy", "gz", None, None),
        P("gx", "gy", "gz", None, None, None),
        P("gx", "gy", "gz", None, None),
        P("gx", "gy", "gz", None, None),
    )
    return jax.shard_map(
        body, mesh=mesh, in_specs=placed, out_specs=P("gx", "gy", "gz", None, None), check_vma=False
    )
```

```python
import functools
import itertools
import math

import jax
import jax.numpy as jnp
from jax import lax
from jax.experimental import pallas as pl
from jax.experimental.pallas import tpu as pltpu
from jax.sharding import PartitionSpec as P

AXES = ("gx", "gy", "gz")


FIRST = (("gy", 1), ("gz", 0), ("gz", 1), ("gx", 0), ("gx", 1), ("gy", 0))
SECOND = (("gx", 0), ("gx", 1), ("gy", 1), ("gz", 0), ("gz", 1), ("gy", 0))
BLOCKS = (("gy", 1), ("gz", 0), ("gz", 1), ("gx", 0), ("gx", 1), ("gy", 0))
IDLE_BLOCKS = {"gx": ("gy", 1), "gy": ("gy", 0), "gz": ("gy", 2)}
IDLE_FIRST = {"gx": ("gy", 1), "gy": ("gy", 0), "gz": ("gy", 2)}
IDLE_SECOND = {"gx": ("gy", 1), "gy": ("gy", 0), "gz": ("gy", 2)}


def links(order):
    return [(axis, first) for axis, first in order if first + 1 < lax.axis_size(axis)]


def partners(axis, first, idle):
    sizes = [lax.axis_size(name) for name in AXES]
    main = AXES.index(axis)
    spare, step = idle.get(axis, (axis, 0))
    spare = AXES.index(spare)
    pairs = []
    for at in itertools.product(*map(range, sizes)):
        to = list(at)
        if first <= at[main] < sizes[main] - (sizes[main] - first) % 2:
            to[main] += 1 - 2 * ((at[main] - first) % 2)
        elif step:
            to[spare] += step - 2 * step * (at[spare] // step % 2)
        else:
            to[spare] = sizes[spare] - 1 - at[spare]
        if to[spare] < sizes[spare]:
            pairs.append(tuple((v[0] * sizes[1] + v[1]) * sizes[2] + v[2] for v in (at, to)))
    return pairs


def swap(buffers, order, idle):
    return [lax.ppermute(buf, AXES, partners(*link, idle)) for buf, link in zip(buffers, links(order))]


def odd_place(axis):
    return lax.rem(lax.axis_index(axis), 2) == 1


def weights():
    values = []
    for axis in AXES:
        place = lax.axis_index(axis)
        values.append(jnp.where(place > 0, 0.5, 1.0).astype(jnp.float32))
        values.append(jnp.where(place < lax.axis_size(axis) - 1, 0.5, 1.0).astype(jnp.float32))
    return values


def outgoing(faces, order):
    picked = []
    for axis, first in links(order):
        number = AXES.index(axis)
        lower, upper = faces[2 * number], faces[2 * number + 1]
        odd = odd_place(axis)
        picked.append(jnp.where(odd, lower, upper) if first == 0 else jnp.where(odd, upper, lower))
    return picked


def incoming(received, order):
    faces = []
    for axis in AXES:
        got = {first: buf for buf, (name, first) in zip(received, links(order)) if name == axis}
        zeros = jnp.zeros_like(received[0])
        even, other = got.get(0, zeros), got.get(1, zeros)
        odd = odd_place(axis)
        place = lax.axis_index(axis)
        faces.append(jnp.where(place > 0, jnp.where(odd, even, other), zeros))
        faces.append(jnp.where(place < lax.axis_size(axis) - 1, jnp.where(odd, other, even), zeros))
    return faces


def split(value):
    high = value.astype(jnp.bfloat16)
    low = (value - high.astype(jnp.float32)).astype(jnp.bfloat16)
    return high, low


def dot(a, b, dims):
    return lax.dot_general(a, b, (dims, ((), ())), preferred_element_type=jnp.float32)


def cut(ref, face):
    return [ref[:, f * face:(f + 1) * face].astype(jnp.float32) for f in range(6)]


def call(kernel, shapes, *args, far=(), far_out=(), scratch=()):
    vmem = pl.BlockSpec(memory_space=pltpu.VMEM)
    hbm = pl.BlockSpec(memory_space=pltpu.HBM)
    near = [a for i, a in enumerate(args) if i not in far] + list(shapes)
    near += [a for a in scratch if isinstance(a, jax.ShapeDtypeStruct)]
    size = sum(a.size * a.dtype.itemsize for a in near)
    scratch = [pltpu.VMEM(a.shape, a.dtype) if isinstance(a, jax.ShapeDtypeStruct) else a for a in scratch]
    return pl.pallas_call(
        kernel,
        out_shape=[pltpu.HBM(s.shape, s.dtype) if i in far_out else s for i, s in enumerate(shapes)],
        in_specs=[hbm if i in far else vmem for i in range(len(args))],
        out_specs=[hbm if i in far_out else vmem for i in range(len(shapes))],
        scratch_shapes=scratch,
        cost_estimate=pl.CostEstimate(flops=10 ** 7, bytes_accessed=size, transcendentals=0),
        compiler_params=pltpu.CompilerParams(vmem_limit_bytes=2 ** 21 + 3 * size // 2),
    )(*[pltpu.with_memory_space_constraint(a, pltpu.HBM) if i in far else a for i, a in enumerate(args)])


def f32(*shape):
    return jax.ShapeDtypeStruct(shape, jnp.float32)


def bf16(*shape):
    return jax.ShapeDtypeStruct(shape, jnp.bfloat16)


def fold(value):
    rows, width = value.shape
    tail = width % 128
    pieces = [value[:, i:i + 128] for i in range(0, width - tail, 128)]
    if tail:
        step = rows * tail // 128
        last = value[:, width - tail:]
        pieces.append(jnp.concatenate([last[i:i + step] for i in range(0, rows, step)], axis=1))
    return jnp.concatenate(pieces, axis=0)


def unfold(value, rows, width):
    tail = width % 128
    full = width // 128
    pieces = [value[i * rows:(i + 1) * rows] for i in range(full)]
    if tail:
        last = value[full * rows:]
        pieces.append(jnp.concatenate([last[:, i:i + tail] for i in range(0, 128, tail)], axis=0))
    return jnp.concatenate(pieces, axis=1)


def pack_face(value, upper):
    rows, width = value.shape
    tail = width % 128
    full = value[:, tail:] if upper else value[:, 0:width - tail]
    rest = value[:, 0:tail] if upper else value[:, width - tail:]
    pieces = [full[:, i:i + 128] for i in range(0, width - tail, 128)]
    if tail:
        step = rows * tail // 128
        pieces.append(jnp.concatenate([rest[i:i + step] for i in range(0, rows, step)], axis=1))
    return jnp.concatenate(pieces, axis=0)


def unpack_pair(from_upper, from_lower, rows, width):
    tail = width % 128
    full = width // 128

    def parts(value):
        pieces = [value[i * rows:(i + 1) * rows] for i in range(full)]
        rest = value[full * rows:]
        return pieces, [jnp.concatenate([rest[:, i:i + tail] for i in range(0, 128, tail)], axis=0)] if tail else []

    below, below_rest = parts(from_upper)
    above, above_rest = parts(from_lower)
    return jnp.concatenate(below_rest + below + above + above_rest, axis=1)


def pick_face(pair, axis, first):
    face = pair.shape[1] // 2
    lower, upper = pack_face(pair[:, 0:face], False), pack_face(pair[:, face:], True)
    odd = odd_place(axis)
    return jnp.where(odd, lower, upper) if first == 0 else jnp.where(odd, upper, lower)


def even_rows(ncf):
    return 2 * ncf


def spans(face, ncf, total):
    sizes = [face * face // 128, even_rows(ncf) * face // 128, ncf * total // 128]
    ends = [sum(sizes[:i + 1]) for i in range(3)]
    return [slice(e - n, e) for e, n in zip(ends, sizes)]


def start_kernel(face, load_ref, blocks_ref, basis_ref, rows_ref, vec_ref, bases_ref, flat_ref, *refs):
    load_near, near_ref, sems = refs[-3:]
    swaps = (len(refs) - 3) // 2
    outs, block_outs = refs[:swaps], refs[swaps:2 * swaps]
    pairs = ((load_ref, load_near), (basis_ref, bases_ref), (rows_ref, flat_ref), (blocks_ref, near_ref))
    copies = [pltpu.make_async_copy(far, near, sems.at[i]) for i, (far, near) in enumerate(pairs)]
    for copy in copies:
        copy.start()
    ncf = bases_ref.shape[0]
    at = spans(face, ncf, flat_ref.shape[0] * flat_ref.shape[1] // ncf)
    copies[0].wait()
    vec_ref[...] = load_near[...].astype(jnp.float32)
    for out, (axis, first) in zip(outs, links(FIRST)):
        low = 2 * face * AXES.index(axis)
        out[...] = pick_face(vec_ref[:, low:low + 2 * face], axis, first)
    copies[1].wait()
    copies[2].wait()
    zeros = jnp.zeros((even_rows(ncf) - ncf, face), jnp.float32)
    flat = fold(flat_ref[...].astype(jnp.float32))
    for out, value in zip(block_outs, outgoing(cut(bases_ref, face), BLOCKS)):
        out[at[1]] = fold(jnp.concatenate([value, zeros], axis=0))
        out[at[2]] = flat
    copies[3].wait()
    for out, (axis, first) in zip(block_outs, links(BLOCKS)):
        upper = lax.rem(lax.axis_index(axis) + 1 + first, 2)
        out[at[0]] = fold(near_ref[2 * AXES.index(axis) + upper].astype(jnp.float32))


def scaled_pairs(face, order, vec_ref, received):
    count = vec_ref.shape[0]
    other = incoming([r[...] for r in received], order)
    weight = weights()
    is_lower = lax.broadcasted_iota(jnp.int32, (1, 2 * face), 1) < face
    pairs = []
    for number in range(len(AXES)):
        low, up = 2 * number, 2 * number + 1
        resid = vec_ref[:, low * face:(low + 2) * face] + unpack_pair(other[low], other[up], count, face)
        pairs.append((resid * jnp.where(is_lower, weight[low], weight[up])).astype(jnp.bfloat16))
    return pairs


def scaled_faces(face, order, vec_ref, received):
    pairs = scaled_pairs(face, order, vec_ref, received)
    return [pair[:, i * face:(i + 1) * face] for pair in pairs for i in range(2)]


def residual_kernel(face, order, pack, vec_ref, basis_ref, *refs):
    received, slots_ref = refs[:-1], refs[-1]
    coarse = None
    for number, scaled in enumerate(scaled_pairs(face, order, vec_ref, received)):
        part = dot(basis_ref[:, 2 * number * face:2 * (number + 1) * face], scaled, ((1,), (1,)))
        coarse = part if coarse is None else coarse + part
    rows = coarse.shape[0] // pack
    slot = jnp.concatenate([coarse[i * rows:(i + 1) * rows] for i in range(pack)], axis=1)
    for d in range(slots_ref.shape[0]):
        slots_ref[d] = slot


def local_kernel(face, n_in, vec_ref, blocks_ref, basis_ref, rows_ref, schur_ref, *refs):
    ncf = basis_ref.shape[0]
    received, blocks_received = refs[:n_in], refs[n_in:2 * n_in]
    start_ref, others_ref, bases_ref, all_rows_ref, near_ref, own_ref, other_ref, sems = refs[2 * n_in:]
    copy = pltpu.make_async_copy(blocks_ref, own_ref, sems.at[0])
    early = pltpu.make_async_copy(schur_ref.at[pl.ds(0, near_ref.shape[0])], near_ref, sems.at[1])
    copy.start()
    early.start()
    at = spans(face, ncf, rows_ref.shape[0] * rows_ref.shape[1] // ncf)
    blocks, bases, rows = [incoming([r[part] for r in blocks_received], BLOCKS) for part in at]
    weight = weights()
    bases_ref[...] = jnp.zeros_like(bases_ref)
    own = cut(basis_ref, face)
    all_rows = [rows_ref[...].astype(jnp.float32)]
    scaled = scaled_faces(face, FIRST, vec_ref, received)
    copy.wait()
    for f in range(6):
        half = 0.5 * weight[f]
        to = slice(f * face, (f + 1) * face)
        block = unfold(blocks[f], face, face).astype(jnp.bfloat16)
        other_ref[f] = block
        local = dot(scaled[f], own_ref[f], ((1,), (0,))) + dot(scaled[f], block, ((1,), (0,)))
        start_ref[:, to] = local * half
        bases_ref[0:ncf, to] = own[f] * half
        bases_ref[ncf * (f + 1):ncf * (f + 2), to] = unfold(bases[f], even_rows(ncf), face)[0:ncf] * half
        all_rows.append(unfold(rows[f], *rows_ref.shape))
    last = pltpu.make_async_copy(other_ref, others_ref, sems.at[0])
    last.start()
    all_rows_ref[...] = jnp.concatenate(all_rows, axis=0)
    early.wait()
    last.wait()


def advance_kernel(face, vec_ref, blocks_ref, others_ref, iterate_ref, *refs):
    received, out_ref, own_ref, other_ref, sems = refs[:-4], refs[-4], refs[-3], refs[-2], refs[-1]
    pairs = ((blocks_ref, own_ref), (others_ref, other_ref))
    copies = [pltpu.make_async_copy(far, near, sems.at[i]) for i, (far, near) in enumerate(pairs)]
    for copy in copies:
        copy.start()
    weight = weights()
    scaled = scaled_faces(face, SECOND, vec_ref, received)
    for copy in copies:
        copy.wait()
    for f in range(6):
        to = slice(f * face, (f + 1) * face)
        local = dot(scaled[f], own_ref[f], ((1,), (0,))) + dot(scaled[f], other_ref[f], ((1,), (0,)))
        out_ref[:, to] = iterate_ref[:, to] + local * (0.5 * weight[f])


def coarse_update(slots_ref, rows_ref, bases_ref, count):
    devices, rows, lanes = slots_ref.shape
    slots = slots_ref[...]
    whole = jnp.concatenate([slots[:, :, i:i + count] for i in range(0, lanes, count)], axis=1)
    high, low = split(whole.reshape(devices * rows * (lanes // count), count))
    matrix = rows_ref[...]
    values = dot(matrix, high, ((1,), (0,))) + dot(matrix, low, ((1,), (0,)))
    high, low = split(values)
    bases = bases_ref[...]
    return dot(high, bases, ((0,), (0,))) + dot(low, bases, ((0,), (0,)))


def middle_kernel(face, slots_ref, rows_ref, bases_ref, start_ref, load_ref, first_ref, schur_ref, iterate_ref, local_ref, *refs):
    outs, near_ref, sems = refs[:-2], refs[-2], refs[-1]
    done = first_ref.shape[0]
    size = near_ref.shape[0] // sems.shape[0]

    def piece(i):
        near = pl.ds(pl.multiple_of(i * size, size), size)
        far = pl.ds(pl.multiple_of(done + i * size, size), size)
        return pltpu.make_async_copy(schur_ref.at[far], near_ref.at[near], sems.at[i])

    lax.fori_loop(0, sems.shape[0], lambda i, _: piece(i).start(), None)
    iterate = start_ref[...] + coarse_update(slots_ref, rows_ref, bases_ref, start_ref.shape[0])
    iterate_ref[...] = iterate
    rounded = iterate.astype(jnp.bfloat16)
    for i in range(sems.shape[0]):
        piece(i).wait()
    for number, axis in enumerate(AXES):
        at = slice(2 * number * face, 2 * (number + 1) * face)
        local = load_ref[:, at] - dot(rounded[:, 0:done], first_ref[:, at], ((1,), (0,)))
        local = local - dot(rounded[:, done:], near_ref[:, at], ((1,), (0,)))
        local_ref[:, at] = local
        for out, (name, first) in zip(outs, links(SECOND)):
            if name == axis:
                out[...] = pick_face(local, axis, first)


def last_kernel(slots_ref, rows_ref, bases_ref, start_ref, out_ref):
    update = coarse_update(slots_ref, rows_ref, bases_ref, start_ref.shape[0])
    out_ref[...] = (start_ref[...] + update).astype(jnp.bfloat16)


def body(load, schur, neumann, coarse_basis, coarse_rows):
    count, width = load.shape[3], load.shape[4]
    face = width // 6
    ncf, total = coarse_rows.shape[3], coarse_rows.shape[4]
    devices = total // ncf
    pack = max(128 // count, 1)
    while ncf % pack:
        pack -= 1
    schur2 = schur.reshape(width, width)
    swaps = len(links(FIRST))
    flat_shape = (ncf * total // 256, 256)
    part = [f32(count * face // 128, 128)] * swaps
    big = [f32(spans(face, ncf, total)[-1].stop, 128)] * swaps
    slots = f32(devices, ncf // pack, pack * count)
    blocks_shape = bf16(6, face, face)
    early = min(width, 640)

    def gather(value):
        return lax.all_to_all(value, AXES, 0, 0)

    blocks = neumann.reshape(6, face, face)
    load_f, basis, rows, *sent = call(
        functools.partial(start_kernel, face),
        [f32(count, width), bf16(ncf, width), bf16(*flat_shape)] + part + big,
        load.reshape(count, width), blocks, coarse_basis.reshape(ncf, width),
        coarse_rows.reshape(flat_shape), far=(0, 1, 2, 3),
        scratch=[bf16(count, width), blocks_shape, pltpu.SemaphoreType.DMA((4,))],
    )
    received = swap(sent[:swaps], FIRST, IDLE_FIRST)
    blocks_received = swap(sent[swaps:], BLOCKS, IDLE_BLOCKS)
    (slot,) = call(functools.partial(residual_kernel, face, FIRST, pack), [slots], load_f, basis, *received)
    whole = gather(slot)
    start, others, bases, all_rows, near = call(
        functools.partial(local_kernel, face, swaps),
        [f32(count, width), blocks_shape, f32(7 * ncf, width), f32(7 * flat_shape[0], 256), bf16(early, width)],
        load_f, blocks, basis, rows, schur2, *received, *blocks_received, far=(1, 4), far_out=(1,),
        scratch=[blocks_shape, blocks_shape, pltpu.SemaphoreType.DMA((2,))],
    )
    bases = bases.astype(jnp.bfloat16)
    all_rows = all_rows.reshape(7 * ncf, total).astype(jnp.bfloat16)
    iterate, vec, *sent = call(
        functools.partial(middle_kernel, face), [f32(count, width), f32(count, width)] + part,
        whole, all_rows, bases, start, load_f, near, schur2, far=(6,),
        scratch=[bf16(width - early, width), pltpu.SemaphoreType.DMA(((width - early) // math.gcd(early, width),))],
    )
    received = swap(sent, SECOND, IDLE_SECOND)
    (slot,) = call(functools.partial(residual_kernel, face, SECOND, pack), [slots], vec, basis, *received)
    whole = gather(slot)
    (start,) = call(
        functools.partial(advance_kernel, face), [f32(count, width)], vec, blocks, others, iterate, *received,
        far=(1, 2), scratch=[blocks_shape, blocks_shape, pltpu.SemaphoreType.DMA((2,))],
    )
    (result,) = call(last_kernel, [bf16(count, width)], whole, all_rows, bases, start)
    return result.reshape(load.shape)


def solution(mesh):
    placed = (
        P("gx", "gy", "gz", None, None),
        P("gx", "gy", "gz", None, None),
        P("gx", "gy", "gz", None, None, None),
        P("gx", "gy", "gz", None, None),
        P("gx", "gy", "gz", None, None),
    )
    return jax.shard_map(
        body, mesh=mesh, in_specs=placed, out_specs=P("gx", "gy", "gz", None, None), check_vma=False
    )
```

```python
import functools
import itertools

import jax
import jax.numpy as jnp
from jax import lax
from jax.experimental import pallas as pl
from jax.experimental.pallas import tpu as pltpu
from jax.sharding import PartitionSpec as P

AXES = ("gx", "gy", "gz")


FIRST = (("gy", 1), ("gz", 0), ("gz", 1), ("gx", 0), ("gx", 1), ("gy", 0))
SECOND = (("gx", 0), ("gx", 1), ("gy", 1), ("gz", 0), ("gz", 1), ("gy", 0))
BLOCKS = (("gy", 1), ("gz", 0), ("gz", 1), ("gx", 0), ("gx", 1), ("gy", 0))
IDLE_BLOCKS = {"gx": ("gy", 1), "gy": ("gy", 0), "gz": ("gy", 2)}
IDLE_FIRST = {"gx": ("gy", 1), "gy": ("gy", 0), "gz": ("gy", 2)}
IDLE_SECOND = {"gx": ("gy", 1), "gy": ("gy", 0), "gz": ("gy", 2)}


def links(order):
    return [(axis, first) for axis, first in order if first + 1 < lax.axis_size(axis)]


def partners(axis, first, idle):
    sizes = [lax.axis_size(name) for name in AXES]
    main = AXES.index(axis)
    spare, step = idle.get(axis, (axis, 0))
    spare = AXES.index(spare)
    pairs = []
    for at in itertools.product(*map(range, sizes)):
        to = list(at)
        if first <= at[main] < sizes[main] - (sizes[main] - first) % 2:
            to[main] += 1 - 2 * ((at[main] - first) % 2)
        elif step:
            to[spare] += step - 2 * step * (at[spare] // step % 2)
        else:
            to[spare] = sizes[spare] - 1 - at[spare]
        if to[spare] < sizes[spare]:
            pairs.append(tuple((v[0] * sizes[1] + v[1]) * sizes[2] + v[2] for v in (at, to)))
    return pairs


def swap(buffers, order, idle):
    return [lax.ppermute(buf, AXES, partners(*link, idle)) for buf, link in zip(buffers, links(order))]


def odd_place(axis):
    return lax.rem(lax.axis_index(axis), 2) == 1


def weights():
    values = []
    for axis in AXES:
        place = lax.axis_index(axis)
        values.append(jnp.where(place > 0, 0.5, 1.0).astype(jnp.float32))
        values.append(jnp.where(place < lax.axis_size(axis) - 1, 0.5, 1.0).astype(jnp.float32))
    return values


def outgoing(faces, order):
    picked = []
    for axis, first in links(order):
        number = AXES.index(axis)
        lower, upper = faces[2 * number], faces[2 * number + 1]
        odd = odd_place(axis)
        picked.append(jnp.where(odd, lower, upper) if first == 0 else jnp.where(odd, upper, lower))
    return picked


def incoming(received, order):
    faces = []
    for axis in AXES:
        got = {first: buf for buf, (name, first) in zip(received, links(order)) if name == axis}
        zeros = jnp.zeros_like(received[0])
        even, other = got.get(0, zeros), got.get(1, zeros)
        odd = odd_place(axis)
        place = lax.axis_index(axis)
        faces.append(jnp.where(place > 0, jnp.where(odd, even, other), zeros))
        faces.append(jnp.where(place < lax.axis_size(axis) - 1, jnp.where(odd, other, even), zeros))
    return faces


def split(value):
    high = value.astype(jnp.bfloat16)
    low = (value - high.astype(jnp.float32)).astype(jnp.bfloat16)
    return high, low


def dot(a, b, dims):
    return lax.dot_general(a, b, (dims, ((), ())), preferred_element_type=jnp.float32)


def cut(ref, face):
    return [ref[:, f * face:(f + 1) * face].astype(jnp.float32) for f in range(6)]


def call(kernel, shapes, *args, far=(), far_out=(), scratch=()):
    vmem = pl.BlockSpec(memory_space=pltpu.VMEM)
    hbm = pl.BlockSpec(memory_space=pltpu.HBM)
    near = [a for i, a in enumerate(args) if i not in far] + list(shapes)
    near += [a for a in scratch if isinstance(a, jax.ShapeDtypeStruct)]
    size = sum(a.size * a.dtype.itemsize for a in near)
    scratch = [pltpu.VMEM(a.shape, a.dtype) if isinstance(a, jax.ShapeDtypeStruct) else a for a in scratch]
    return pl.pallas_call(
        kernel,
        out_shape=[pltpu.HBM(s.shape, s.dtype) if i in far_out else s for i, s in enumerate(shapes)],
        in_specs=[hbm if i in far else vmem for i in range(len(args))],
        out_specs=[hbm if i in far_out else vmem for i in range(len(shapes))],
        scratch_shapes=scratch,
        cost_estimate=pl.CostEstimate(flops=10 ** 7, bytes_accessed=size, transcendentals=0),
        compiler_params=pltpu.CompilerParams(vmem_limit_bytes=2 ** 21 + 3 * size // 2),
    )(*[pltpu.with_memory_space_constraint(a, pltpu.HBM) if i in far else a for i, a in enumerate(args)])


def f32(*shape):
    return jax.ShapeDtypeStruct(shape, jnp.float32)


def bf16(*shape):
    return jax.ShapeDtypeStruct(shape, jnp.bfloat16)


def fold(value):
    rows, width = value.shape
    tail = width % 128
    pieces = [value[:, i:i + 128] for i in range(0, width - tail, 128)]
    if tail:
        step = rows * tail // 128
        last = value[:, width - tail:]
        pieces.append(jnp.concatenate([last[i:i + step] for i in range(0, rows, step)], axis=1))
    return jnp.concatenate(pieces, axis=0)


def unfold(value, rows, width):
    tail = width % 128
    full = width // 128
    pieces = [value[i * rows:(i + 1) * rows] for i in range(full)]
    if tail:
        last = value[full * rows:]
        pieces.append(jnp.concatenate([last[:, i:i + tail] for i in range(0, 128, tail)], axis=0))
    return jnp.concatenate(pieces, axis=1)


def pack_face(value, upper):
    rows, width = value.shape
    tail = width % 128
    full = value[:, tail:] if upper else value[:, 0:width - tail]
    rest = value[:, 0:tail] if upper else value[:, width - tail:]
    pieces = [full[:, i:i + 128] for i in range(0, width - tail, 128)]
    if tail:
        step = rows * tail // 128
        pieces.append(jnp.concatenate([rest[i:i + step] for i in range(0, rows, step)], axis=1))
    return jnp.concatenate(pieces, axis=0)


def unpack_pair(from_upper, from_lower, rows, width):
    tail = width % 128
    full = width // 128

    def parts(value):
        pieces = [value[i * rows:(i + 1) * rows] for i in range(full)]
        rest = value[full * rows:]
        return pieces, [jnp.concatenate([rest[:, i:i + tail] for i in range(0, 128, tail)], axis=0)] if tail else []

    below, below_rest = parts(from_upper)
    above, above_rest = parts(from_lower)
    return jnp.concatenate(below_rest + below + above + above_rest, axis=1)


def pick_face(pair, axis, first):
    face = pair.shape[1] // 2
    lower, upper = pack_face(pair[:, 0:face], False), pack_face(pair[:, face:], True)
    odd = odd_place(axis)
    return jnp.where(odd, lower, upper) if first == 0 else jnp.where(odd, upper, lower)


def even_rows(ncf):
    return 2 * ncf


def spans(face, ncf, total):
    sizes = [face * face // 128, even_rows(ncf) * face // 128, ncf * total // 128]
    ends = [sum(sizes[:i + 1]) for i in range(3)]
    return [slice(e - n, e) for e, n in zip(ends, sizes)]


def start_kernel(face, load_ref, blocks_ref, basis_ref, rows_ref, vec_ref, bases_ref, flat_ref, *refs):
    load_near, near_ref, sems = refs[-3:]
    swaps = (len(refs) - 3) // 2
    outs, block_outs = refs[:swaps], refs[swaps:2 * swaps]
    pairs = ((load_ref, load_near), (basis_ref, bases_ref), (rows_ref, flat_ref), (blocks_ref, near_ref))
    copies = [pltpu.make_async_copy(far, near, sems.at[i]) for i, (far, near) in enumerate(pairs)]
    for copy in copies:
        copy.start()
    ncf = bases_ref.shape[0]
    at = spans(face, ncf, flat_ref.shape[0] * flat_ref.shape[1] // ncf)
    copies[0].wait()
    vec_ref[...] = load_near[...].astype(jnp.float32)
    for out, (axis, first) in zip(outs, links(FIRST)):
        low = 2 * face * AXES.index(axis)
        out[...] = pick_face(vec_ref[:, low:low + 2 * face], axis, first)
    copies[1].wait()
    copies[2].wait()
    zeros = jnp.zeros((even_rows(ncf) - ncf, face), jnp.float32)
    flat = fold(flat_ref[...].astype(jnp.float32))
    for out, value in zip(block_outs, outgoing(cut(bases_ref, face), BLOCKS)):
        out[at[1]] = fold(jnp.concatenate([value, zeros], axis=0))
        out[at[2]] = flat
    copies[3].wait()
    for out, (axis, first) in zip(block_outs, links(BLOCKS)):
        upper = lax.rem(lax.axis_index(axis) + 1 + first, 2)
        out[at[0]] = fold(near_ref[2 * AXES.index(axis) + upper].astype(jnp.float32))


def scaled_pairs(face, order, vec_ref, received):
    count = vec_ref.shape[0]
    other = incoming([r[...] for r in received], order)
    weight = weights()
    is_lower = lax.broadcasted_iota(jnp.int32, (1, 2 * face), 1) < face
    pairs = []
    for number in range(len(AXES)):
        low, up = 2 * number, 2 * number + 1
        resid = vec_ref[:, low * face:(low + 2) * face] + unpack_pair(other[low], other[up], count, face)
        pairs.append((resid * jnp.where(is_lower, weight[low], weight[up])).astype(jnp.bfloat16))
    return pairs


def scaled_faces(face, order, vec_ref, received):
    pairs = scaled_pairs(face, order, vec_ref, received)
    return [pair[:, i * face:(i + 1) * face] for pair in pairs for i in range(2)]


def residual_kernel(face, order, pack, vec_ref, basis_ref, *refs):
    received, slots_ref = refs[:-1], refs[-1]
    coarse = None
    for number, scaled in enumerate(scaled_pairs(face, order, vec_ref, received)):
        part = dot(basis_ref[:, 2 * number * face:2 * (number + 1) * face], scaled, ((1,), (1,)))
        coarse = part if coarse is None else coarse + part
    rows = coarse.shape[0] // pack
    slot = jnp.concatenate([coarse[i * rows:(i + 1) * rows] for i in range(pack)], axis=1)
    for d in range(slots_ref.shape[0]):
        slots_ref[d] = slot


def local_kernel(face, n_in, vec_ref, blocks_ref, basis_ref, rows_ref, schur_ref, *refs):
    ncf = basis_ref.shape[0]
    count, width = vec_ref.shape
    received, blocks_received = refs[:n_in], refs[n_in:2 * n_in]
    (start_ref, others_ref, table_ref, all_rows_ref, local_ref,
     own_ref, other_ref, near_ref, bases_ref, sems) = refs[2 * n_in:]
    copy = pltpu.make_async_copy(blocks_ref, own_ref, sems.at[0])
    whole = pltpu.make_async_copy(schur_ref, near_ref, sems.at[1])
    copy.start()
    whole.start()
    at = spans(face, ncf, rows_ref.shape[0] * rows_ref.shape[1] // ncf)
    blocks, bases, rows = [incoming([r[part] for r in blocks_received], BLOCKS) for part in at]
    weight = weights()
    bases_ref[...] = jnp.zeros_like(bases_ref)
    own = cut(basis_ref, face)
    all_rows = [rows_ref[...].astype(jnp.float32)]
    scaled = scaled_faces(face, FIRST, vec_ref, received)
    copy.wait()
    for f in range(6):
        half = 0.5 * weight[f]
        to = slice(f * face, (f + 1) * face)
        block = unfold(blocks[f], face, face).astype(jnp.bfloat16)
        other_ref[f] = block
        local = dot(scaled[f], own_ref[f], ((1,), (0,))) + dot(scaled[f], block, ((1,), (0,)))
        start_ref[:, to] = local * half
        bases_ref[0:ncf, to] = own[f] * half
        bases_ref[ncf * (f + 1):ncf * (f + 2), to] = unfold(bases[f], even_rows(ncf), face)[0:ncf] * half
        all_rows.append(unfold(rows[f], *rows_ref.shape))
    last = pltpu.make_async_copy(other_ref, others_ref, sems.at[0])
    last.start()
    all_rows.append(jnp.zeros_like(all_rows[0]))
    all_rows_ref[...] = jnp.concatenate(all_rows, axis=0)
    terms = bases_ref.shape[0]
    part = bases_ref[...].astype(jnp.bfloat16)
    table_ref[0:terms, 0:width] = part
    table_ref[terms:2 * terms, 0:width] = part
    table_ref[2 * terms:, 0:width] = jnp.zeros_like(part)
    both = jnp.concatenate([start_ref[...].astype(jnp.bfloat16), part], axis=0)
    whole.wait()
    for number in range(len(AXES)):
        to = slice(2 * number * face, 2 * (number + 1) * face)
        product = dot(both, near_ref[:, to], ((1,), (0,)))
        local_ref[:, to] = vec_ref[:, to] - product[0:count]
        high, low = split(product[count:])
        to = slice(width + 2 * number * face, width + 2 * (number + 1) * face)
        table_ref[0:terms, to] = high
        table_ref[terms:2 * terms, to] = high
        table_ref[2 * terms:, to] = low
    last.wait()


def advance_kernel(face, vec_ref, blocks_ref, others_ref, iterate_ref, *refs):
    received, out_ref, own_ref, other_ref, sems = refs[:-4], refs[-4], refs[-3], refs[-2], refs[-1]
    pairs = ((blocks_ref, own_ref), (others_ref, other_ref))
    copies = [pltpu.make_async_copy(far, near, sems.at[i]) for i, (far, near) in enumerate(pairs)]
    for copy in copies:
        copy.start()
    weight = weights()
    scaled = scaled_faces(face, SECOND, vec_ref, received)
    for copy in copies:
        copy.wait()
    for f in range(6):
        to = slice(f * face, (f + 1) * face)
        local = dot(scaled[f], own_ref[f], ((1,), (0,))) + dot(scaled[f], other_ref[f], ((1,), (0,)))
        out_ref[:, to] = iterate_ref[:, to] + local * (0.5 * weight[f])


def coarse_terms(slots_ref, rows_ref, count):
    devices, rows, lanes = slots_ref.shape
    slots = slots_ref[...]
    whole = jnp.concatenate([slots[:, :, i:i + count] for i in range(0, lanes, count)], axis=1)
    high, low = split(whole.reshape(devices * rows * (lanes // count), count))
    matrix = rows_ref[...]
    values = dot(matrix, high, ((1,), (0,))) + dot(matrix, low, ((1,), (0,)))
    high, low = split(values)
    return jnp.concatenate([high, low, high], axis=0)


def middle_kernel(face, slots_ref, rows_ref, table_ref, start_ref, load_ref, iterate_ref, local_ref, *outs):
    terms = coarse_terms(slots_ref, rows_ref, start_ref.shape[0])
    width = start_ref.shape[1]
    for number, axis in enumerate(AXES):
        at = slice(2 * number * face, 2 * (number + 1) * face)
        to = slice(width + 2 * number * face, width + 2 * (number + 1) * face)
        local = load_ref[:, at] - dot(terms, table_ref[:, to], ((0,), (0,)))
        local_ref[:, at] = local
        for out, (name, first) in zip(outs, links(SECOND)):
            if name == axis:
                out[...] = pick_face(local, axis, first)
    iterate_ref[...] = start_ref[...] + dot(terms, table_ref[:, 0:width], ((0,), (0,)))


def last_kernel(slots_ref, rows_ref, table_ref, start_ref, out_ref):
    count, width = start_ref.shape
    two = 2 * table_ref.shape[0] // 3
    terms = coarse_terms(slots_ref, rows_ref, count)[0:two]
    update = dot(terms, table_ref[0:two, 0:width], ((0,), (0,)))
    out_ref[...] = (start_ref[...] + update).astype(jnp.bfloat16)


def body(load, schur, neumann, coarse_basis, coarse_rows):
    count, width = load.shape[3], load.shape[4]
    face = width // 6
    ncf, total = coarse_rows.shape[3], coarse_rows.shape[4]
    devices = total // ncf
    pack = max(128 // count, 1)
    while ncf % pack:
        pack -= 1
    schur2 = schur.reshape(width, width)
    swaps = len(links(FIRST))
    flat_shape = (ncf * total // 256, 256)
    part = [f32(count * face // 128, 128)] * swaps
    big = [f32(spans(face, ncf, total)[-1].stop, 128)] * swaps
    slots = f32(devices, ncf // pack, pack * count)
    blocks_shape = bf16(6, face, face)

    def gather(value):
        return lax.all_to_all(value, AXES, 0, 0)

    blocks = neumann.reshape(6, face, face)
    load_f, basis, rows, *sent = call(
        functools.partial(start_kernel, face),
        [f32(count, width), bf16(ncf, width), bf16(*flat_shape)] + part + big,
        load.reshape(count, width), blocks, coarse_basis.reshape(ncf, width),
        coarse_rows.reshape(flat_shape), far=(0, 1, 2, 3),
        scratch=[bf16(count, width), blocks_shape, pltpu.SemaphoreType.DMA((4,))],
    )
    received = swap(sent[:swaps], FIRST, IDLE_FIRST)
    blocks_received = swap(sent[swaps:], BLOCKS, IDLE_BLOCKS)
    (slot,) = call(functools.partial(residual_kernel, face, FIRST, pack), [slots], load_f, basis, *received)
    whole = gather(slot)
    start, others, table, all_rows, local = call(
        functools.partial(local_kernel, face, swaps),
        [f32(count, width), blocks_shape, bf16(24 * ncf, 2 * width), f32(8 * flat_shape[0], 256), f32(count, width)],
        load_f, blocks, basis, rows, schur2, *received, *blocks_received, far=(1, 4), far_out=(1,),
        scratch=[blocks_shape, blocks_shape, bf16(width, width), f32(8 * ncf, width), pltpu.SemaphoreType.DMA((2,))],
    )
    all_rows = all_rows.reshape(8 * ncf, total).astype(jnp.bfloat16)
    iterate, vec, *sent = call(
        functools.partial(middle_kernel, face), [f32(count, width), f32(count, width)] + part,
        whole, all_rows, table, start, local,
    )
    received = swap(sent, SECOND, IDLE_SECOND)
    (slot,) = call(functools.partial(residual_kernel, face, SECOND, pack), [slots], vec, basis, *received)
    whole = gather(slot)
    (start,) = call(
        functools.partial(advance_kernel, face), [f32(count, width)], vec, blocks, others, iterate, *received,
        far=(1, 2), scratch=[blocks_shape, blocks_shape, pltpu.SemaphoreType.DMA((2,))],
    )
    (result,) = call(last_kernel, [bf16(count, width)], whole, all_rows, table, start)
    return result.reshape(load.shape)


def solution(mesh):
    placed = (
        P("gx", "gy", "gz", None, None),
        P("gx", "gy", "gz", None, None),
        P("gx", "gy", "gz", None, None, None),
        P("gx", "gy", "gz", None, None),
        P("gx", "gy", "gz", None, None),
    )
    return jax.shard_map(
        body, mesh=mesh, in_specs=placed, out_specs=P("gx", "gy", "gz", None, None), check_vma=False
    )
```

```python
import functools
import itertools

import jax
import jax.numpy as jnp
from jax import lax
from jax.experimental import pallas as pl
from jax.experimental.pallas import tpu as pltpu
from jax.sharding import PartitionSpec as P

AXES = ("gx", "gy", "gz")


FIRST = (("gy", 1), ("gz", 0), ("gz", 1), ("gx", 0), ("gx", 1), ("gy", 0))
SECOND = (("gx", 0), ("gx", 1), ("gy", 1), ("gz", 0), ("gz", 1), ("gy", 0))
BLOCKS = (("gy", 1), ("gz", 0), ("gz", 1), ("gx", 0), ("gx", 1), ("gy", 0))
IDLE_BLOCKS = {"gx": ("gy", 1), "gy": ("gy", 0), "gz": ("gy", 2)}
IDLE_FIRST = {"gx": ("gy", 1), "gy": ("gy", 0), "gz": ("gy", 2)}
IDLE_SECOND = {"gx": ("gy", 1), "gy": ("gy", 0), "gz": ("gy", 2)}


def links(order):
    return [(axis, first) for axis, first in order if first + 1 < lax.axis_size(axis)]


def partners(axis, first, idle):
    sizes = [lax.axis_size(name) for name in AXES]
    main = AXES.index(axis)
    spare, step = idle.get(axis, (axis, 0))
    spare = AXES.index(spare)
    pairs = []
    for at in itertools.product(*map(range, sizes)):
        to = list(at)
        if first <= at[main] < sizes[main] - (sizes[main] - first) % 2:
            to[main] += 1 - 2 * ((at[main] - first) % 2)
        elif step:
            to[spare] += step - 2 * step * (at[spare] // step % 2)
        else:
            to[spare] = sizes[spare] - 1 - at[spare]
        if to[spare] < sizes[spare]:
            pairs.append(tuple((v[0] * sizes[1] + v[1]) * sizes[2] + v[2] for v in (at, to)))
    return pairs


def swap(buffers, order, idle):
    return [lax.ppermute(buf, AXES, partners(*link, idle)) for buf, link in zip(buffers, links(order))]


def odd_place(axis):
    return lax.rem(lax.axis_index(axis), 2) == 1


def weights():
    values = []
    for axis in AXES:
        place = lax.axis_index(axis)
        values.append(jnp.where(place > 0, 0.5, 1.0).astype(jnp.float32))
        values.append(jnp.where(place < lax.axis_size(axis) - 1, 0.5, 1.0).astype(jnp.float32))
    return values


def outgoing(faces, order):
    picked = []
    for axis, first in links(order):
        number = AXES.index(axis)
        lower, upper = faces[2 * number], faces[2 * number + 1]
        odd = odd_place(axis)
        picked.append(jnp.where(odd, lower, upper) if first == 0 else jnp.where(odd, upper, lower))
    return picked


def incoming(received, order):
    faces = []
    for axis in AXES:
        got = {first: buf for buf, (name, first) in zip(received, links(order)) if name == axis}
        zeros = jnp.zeros_like(received[0])
        even, other = got.get(0, zeros), got.get(1, zeros)
        odd = odd_place(axis)
        place = lax.axis_index(axis)
        faces.append(jnp.where(place > 0, jnp.where(odd, even, other), zeros))
        faces.append(jnp.where(place < lax.axis_size(axis) - 1, jnp.where(odd, other, even), zeros))
    return faces


def split(value):
    high = value.astype(jnp.bfloat16)
    low = (value - high.astype(jnp.float32)).astype(jnp.bfloat16)
    return high, low


def dot(a, b, dims):
    return lax.dot_general(a, b, (dims, ((), ())), preferred_element_type=jnp.float32)


def cut(ref, face):
    return [ref[:, f * face:(f + 1) * face].astype(jnp.float32) for f in range(6)]


def call(kernel, shapes, *args, far=(), far_out=(), scratch=()):
    vmem = pl.BlockSpec(memory_space=pltpu.VMEM)
    hbm = pl.BlockSpec(memory_space=pltpu.HBM)
    near = [a for i, a in enumerate(args) if i not in far] + list(shapes)
    near += [a for a in scratch if isinstance(a, jax.ShapeDtypeStruct)]
    size = sum(a.size * a.dtype.itemsize for a in near)
    scratch = [pltpu.VMEM(a.shape, a.dtype) if isinstance(a, jax.ShapeDtypeStruct) else a for a in scratch]
    return pl.pallas_call(
        kernel,
        out_shape=[pltpu.HBM(s.shape, s.dtype) if i in far_out else s for i, s in enumerate(shapes)],
        in_specs=[hbm if i in far else vmem for i in range(len(args))],
        out_specs=[hbm if i in far_out else vmem for i in range(len(shapes))],
        scratch_shapes=scratch,
        cost_estimate=pl.CostEstimate(flops=10 ** 7, bytes_accessed=size, transcendentals=0),
        compiler_params=pltpu.CompilerParams(vmem_limit_bytes=2 ** 21 + 3 * size // 2),
    )(*[pltpu.with_memory_space_constraint(a, pltpu.HBM) if i in far else a for i, a in enumerate(args)])


def f32(*shape):
    return jax.ShapeDtypeStruct(shape, jnp.float32)


def bf16(*shape):
    return jax.ShapeDtypeStruct(shape, jnp.bfloat16)


def fold(value):
    rows, width = value.shape
    tail = width % 128
    pieces = [value[:, i:i + 128] for i in range(0, width - tail, 128)]
    if tail:
        step = rows * tail // 128
        last = value[:, width - tail:]
        pieces.append(jnp.concatenate([last[i:i + step] for i in range(0, rows, step)], axis=1))
    return jnp.concatenate(pieces, axis=0)


def unfold(value, rows, width):
    tail = width % 128
    full = width // 128
    pieces = [value[i * rows:(i + 1) * rows] for i in range(full)]
    if tail:
        last = value[full * rows:]
        pieces.append(jnp.concatenate([last[:, i:i + tail] for i in range(0, 128, tail)], axis=0))
    return jnp.concatenate(pieces, axis=1)


def pack_face(value, upper):
    rows, width = value.shape
    tail = width % 128
    full = value[:, tail:] if upper else value[:, 0:width - tail]
    rest = value[:, 0:tail] if upper else value[:, width - tail:]
    pieces = [full[:, i:i + 128] for i in range(0, width - tail, 128)]
    if tail:
        step = rows * tail // 128
        pieces.append(jnp.concatenate([rest[i:i + step] for i in range(0, rows, step)], axis=1))
    return jnp.concatenate(pieces, axis=0)


def unpack_pair(from_upper, from_lower, rows, width):
    tail = width % 128
    full = width // 128

    def parts(value):
        pieces = [value[i * rows:(i + 1) * rows] for i in range(full)]
        rest = value[full * rows:]
        return pieces, [jnp.concatenate([rest[:, i:i + tail] for i in range(0, 128, tail)], axis=0)] if tail else []

    below, below_rest = parts(from_upper)
    above, above_rest = parts(from_lower)
    return jnp.concatenate(below_rest + below + above + above_rest, axis=1)


def pick_face(pair, axis, first):
    face = pair.shape[1] // 2
    lower, upper = pack_face(pair[:, 0:face], False), pack_face(pair[:, face:], True)
    odd = odd_place(axis)
    return jnp.where(odd, lower, upper) if first == 0 else jnp.where(odd, upper, lower)


def even_rows(ncf):
    return 2 * ncf


def spans(face, ncf, total):
    sizes = [face * face // 128, even_rows(ncf) * face // 128, ncf * total // 128]
    ends = [sum(sizes[:i + 1]) for i in range(3)]
    return [slice(e - n, e) for e, n in zip(ends, sizes)]


def start_kernel(face, load_ref, blocks_ref, basis_ref, rows_ref, vec_ref, bases_ref, flat_ref, *refs):
    load_near, near_ref, sems = refs[-3:]
    swaps = (len(refs) - 3) // 2
    outs, block_outs = refs[:swaps], refs[swaps:2 * swaps]
    pairs = ((load_ref, load_near), (basis_ref, bases_ref), (rows_ref, flat_ref), (blocks_ref, near_ref))
    copies = [pltpu.make_async_copy(far, near, sems.at[i]) for i, (far, near) in enumerate(pairs)]
    for copy in copies:
        copy.start()
    ncf = bases_ref.shape[0]
    at = spans(face, ncf, flat_ref.shape[0] * flat_ref.shape[1] // ncf)
    copies[0].wait()
    vec_ref[...] = load_near[...].astype(jnp.float32)
    for out, (axis, first) in zip(outs, links(FIRST)):
        low = 2 * face * AXES.index(axis)
        out[...] = pick_face(vec_ref[:, low:low + 2 * face], axis, first)
    copies[1].wait()
    copies[2].wait()
    zeros = jnp.zeros((even_rows(ncf) - ncf, face), jnp.float32)
    flat = fold(flat_ref[...].astype(jnp.float32))
    for out, value in zip(block_outs, outgoing(cut(bases_ref, face), BLOCKS)):
        out[at[1]] = fold(jnp.concatenate([value, zeros], axis=0))
        out[at[2]] = flat
    copies[3].wait()
    for out, (axis, first) in zip(block_outs, links(BLOCKS)):
        upper = lax.rem(lax.axis_index(axis) + 1 + first, 2)
        out[at[0]] = fold(near_ref[2 * AXES.index(axis) + upper].astype(jnp.float32))


def scaled_pairs(face, order, vec_ref, received):
    count = vec_ref.shape[0]
    other = incoming([r[...] for r in received], order)
    weight = weights()
    is_lower = lax.broadcasted_iota(jnp.int32, (1, 2 * face), 1) < face
    pairs = []
    for number in range(len(AXES)):
        low, up = 2 * number, 2 * number + 1
        resid = vec_ref[:, low * face:(low + 2) * face] + unpack_pair(other[low], other[up], count, face)
        pairs.append((resid * jnp.where(is_lower, weight[low], weight[up])).astype(jnp.bfloat16))
    return pairs


def scaled_faces(face, order, vec_ref, received):
    pairs = scaled_pairs(face, order, vec_ref, received)
    return [pair[:, i * face:(i + 1) * face] for pair in pairs for i in range(2)]


def residual_kernel(face, order, pack, vec_ref, basis_ref, *refs):
    received, slots_ref = refs[:-1], refs[-1]
    coarse = None
    for number, scaled in enumerate(scaled_pairs(face, order, vec_ref, received)):
        part = dot(basis_ref[:, 2 * number * face:2 * (number + 1) * face], scaled, ((1,), (1,)))
        coarse = part if coarse is None else coarse + part
    rows = coarse.shape[0] // pack
    slot = jnp.concatenate([coarse[i * rows:(i + 1) * rows] for i in range(pack)], axis=1)
    for d in range(slots_ref.shape[0]):
        slots_ref[d] = slot


def local_kernel(face, n_in, vec_ref, blocks_ref, basis_ref, rows_ref, schur_ref, *refs):
    ncf = basis_ref.shape[0]
    count, width = vec_ref.shape
    received, blocks_received = refs[:n_in], refs[n_in:2 * n_in]
    (start_ref, others_ref, table_ref, all_rows_ref, local_ref,
     own_ref, other_ref, near_ref, bases_ref, sems) = refs[2 * n_in:]
    copy = pltpu.make_async_copy(blocks_ref, own_ref, sems.at[0])
    size = width // 3

    def piece(i):
        rows = pl.ds(pl.multiple_of(i * size, size), size)
        return pltpu.make_async_copy(schur_ref.at[rows], near_ref.at[rows], sems.at[i + 1])

    copy.start()
    lax.fori_loop(0, 3, lambda i, _: piece(i).start(), None)
    at = spans(face, ncf, rows_ref.shape[0] * rows_ref.shape[1] // ncf)
    blocks = incoming([r[at[0]].astype(jnp.bfloat16) for r in blocks_received], BLOCKS)
    bases, rows = [incoming([r[part] for r in blocks_received], BLOCKS) for part in at[1:]]
    weight = weights()
    bases_ref[...] = jnp.zeros_like(bases_ref)
    own = cut(basis_ref, face)
    all_rows = [rows_ref[...].astype(jnp.float32)]
    scaled = scaled_faces(face, FIRST, vec_ref, received)
    copy.wait()
    for f in range(6):
        half = 0.5 * weight[f]
        to = slice(f * face, (f + 1) * face)
        block = unfold(blocks[f], face, face)
        other_ref[f] = block
        local = dot(scaled[f], own_ref[f], ((1,), (0,))) + dot(scaled[f], block, ((1,), (0,)))
        start_ref[:, to] = local * half
        bases_ref[0:ncf, to] = own[f] * half
        bases_ref[ncf * (f + 1):ncf * (f + 2), to] = unfold(bases[f], even_rows(ncf), face)[0:ncf] * half
        all_rows.append(unfold(rows[f], *rows_ref.shape))
    last = pltpu.make_async_copy(other_ref, others_ref, sems.at[0])
    last.start()
    all_rows.append(jnp.zeros_like(all_rows[0]))
    all_rows_ref[...] = jnp.concatenate(all_rows, axis=0)
    terms = bases_ref.shape[0]
    part = bases_ref[...].astype(jnp.bfloat16)
    table_ref[0:terms, 0:width] = part
    table_ref[terms:2 * terms, 0:width] = part
    table_ref[2 * terms:, 0:width] = jnp.zeros_like(part)
    high, low = split(start_ref[...])
    factors = jnp.concatenate([high, low, part], axis=0)
    columns = (slice(0, 4 * face), slice(4 * face, width))
    piece(0).wait()
    piece(1).wait()
    products = [dot(factors[:, 0:2 * size], near_ref[0:2 * size, to], ((1,), (0,))) for to in columns]
    piece(2).wait()
    for to, product in zip(columns, products):
        product = product + dot(factors[:, 2 * size:], near_ref[2 * size:, to], ((1,), (0,)))
        local_ref[:, to] = vec_ref[:, to] - (product[0:count] + product[count:2 * count])
        high, low = split(product[2 * count:])
        to = slice(width + to.start, width + to.stop)
        table_ref[0:terms, to] = high
        table_ref[terms:2 * terms, to] = high
        table_ref[2 * terms:, to] = low
    last.wait()


def advance_kernel(face, vec_ref, blocks_ref, others_ref, iterate_ref, *refs):
    received, out_ref, own_ref, other_ref, sems = refs[:-4], refs[-4], refs[-3], refs[-2], refs[-1]
    pairs = ((blocks_ref, own_ref), (others_ref, other_ref))
    copies = [pltpu.make_async_copy(far, near, sems.at[i]) for i, (far, near) in enumerate(pairs)]
    for copy in copies:
        copy.start()
    weight = weights()
    scaled = scaled_faces(face, SECOND, vec_ref, received)
    for copy in copies:
        copy.wait()
    for f in range(6):
        to = slice(f * face, (f + 1) * face)
        local = dot(scaled[f], own_ref[f], ((1,), (0,))) + dot(scaled[f], other_ref[f], ((1,), (0,)))
        out_ref[:, to] = iterate_ref[:, to] + local * (0.5 * weight[f])


def coarse_terms(slots_ref, rows_ref, count):
    devices, rows, lanes = slots_ref.shape
    slots = slots_ref[...]
    whole = jnp.concatenate([slots[:, :, i:i + count] for i in range(0, lanes, count)], axis=1)
    high, low = split(whole.reshape(devices * rows * (lanes // count), count))
    matrix = rows_ref[...]
    values = dot(matrix, high, ((1,), (0,))) + dot(matrix, low, ((1,), (0,)))
    high, low = split(values)
    return jnp.concatenate([high, low, high], axis=0)


def middle_kernel(face, slots_ref, rows_ref, table_ref, start_ref, load_ref, iterate_ref, local_ref, *outs):
    terms = coarse_terms(slots_ref, rows_ref, start_ref.shape[0])
    width = start_ref.shape[1]
    for number, axis in enumerate(AXES):
        at = slice(2 * number * face, 2 * (number + 1) * face)
        to = slice(width + 2 * number * face, width + 2 * (number + 1) * face)
        local = load_ref[:, at] - dot(terms, table_ref[:, to], ((0,), (0,)))
        local_ref[:, at] = local
        for out, (name, first) in zip(outs, links(SECOND)):
            if name == axis:
                out[...] = pick_face(local, axis, first)
    iterate_ref[...] = start_ref[...] + dot(terms, table_ref[:, 0:width], ((0,), (0,)))


def last_kernel(slots_ref, rows_ref, table_ref, start_ref, out_ref):
    count, width = start_ref.shape
    two = 2 * table_ref.shape[0] // 3
    terms = coarse_terms(slots_ref, rows_ref, count)[0:two]
    update = dot(terms, table_ref[0:two, 0:width], ((0,), (0,)))
    out_ref[...] = (start_ref[...] + update).astype(jnp.bfloat16)


def body(load, schur, neumann, coarse_basis, coarse_rows):
    count, width = load.shape[3], load.shape[4]
    face = width // 6
    ncf, total = coarse_rows.shape[3], coarse_rows.shape[4]
    devices = total // ncf
    pack = max(128 // count, 1)
    while ncf % pack:
        pack -= 1
    schur2 = schur.reshape(width, width)
    swaps = len(links(FIRST))
    flat_shape = (ncf * total // 256, 256)
    part = [f32(count * face // 128, 128)] * swaps
    big = [f32(spans(face, ncf, total)[-1].stop, 128)] * swaps
    slots = f32(devices, ncf // pack, pack * count)
    blocks_shape = bf16(6, face, face)

    def gather(value):
        return lax.all_to_all(value, AXES, 0, 0)

    blocks = neumann.reshape(6, face, face)
    load_f, basis, rows, *sent = call(
        functools.partial(start_kernel, face),
        [f32(count, width), bf16(ncf, width), bf16(*flat_shape)] + part + big,
        load.reshape(count, width), blocks, coarse_basis.reshape(ncf, width),
        coarse_rows.reshape(flat_shape), far=(0, 1, 2, 3),
        scratch=[bf16(count, width), blocks_shape, pltpu.SemaphoreType.DMA((4,))],
    )
    received = swap(sent[:swaps], FIRST, IDLE_FIRST)
    blocks_received = swap(sent[swaps:], BLOCKS, IDLE_BLOCKS)
    (slot,) = call(functools.partial(residual_kernel, face, FIRST, pack), [slots], load_f, basis, *received)
    whole = gather(slot)
    start, others, table, all_rows, local = call(
        functools.partial(local_kernel, face, swaps),
        [f32(count, width), blocks_shape, bf16(24 * ncf, 2 * width), f32(8 * flat_shape[0], 256), f32(count, width)],
        load_f, blocks, basis, rows, schur2, *received, *blocks_received, far=(1, 4), far_out=(1,),
        scratch=[blocks_shape, blocks_shape, bf16(width, width), f32(8 * ncf, width), pltpu.SemaphoreType.DMA((4,))],
    )
    all_rows = all_rows.reshape(8 * ncf, total).astype(jnp.bfloat16)
    iterate, vec, *sent = call(
        functools.partial(middle_kernel, face), [f32(count, width), f32(count, width)] + part,
        whole, all_rows, table, start, local,
    )
    received = swap(sent, SECOND, IDLE_SECOND)
    (slot,) = call(functools.partial(residual_kernel, face, SECOND, pack), [slots], vec, basis, *received)
    whole = gather(slot)
    (start,) = call(
        functools.partial(advance_kernel, face), [f32(count, width)], vec, blocks, others, iterate, *received,
        far=(1, 2), scratch=[blocks_shape, blocks_shape, pltpu.SemaphoreType.DMA((2,))],
    )
    (result,) = call(last_kernel, [bf16(count, width)], whole, all_rows, table, start)
    return result.reshape(load.shape)


def solution(mesh):
    placed = (
        P("gx", "gy", "gz", None, None),
        P("gx", "gy", "gz", None, None),
        P("gx", "gy", "gz", None, None, None),
        P("gx", "gy", "gz", None, None),
        P("gx", "gy", "gz", None, None),
    )
    return jax.shard_map(
        body, mesh=mesh, in_specs=placed, out_specs=P("gx", "gy", "gz", None, None), check_vma=False
    )
```

```python
import functools
import itertools

import jax
import jax.numpy as jnp
from jax import lax
from jax.experimental import pallas as pl
from jax.experimental.pallas import tpu as pltpu
from jax.sharding import PartitionSpec as P

AXES = ("gx", "gy", "gz")


FIRST = (("gy", 1), ("gz", 0), ("gz", 1), ("gx", 0), ("gx", 1), ("gy", 0))
SECOND = (("gx", 0), ("gx", 1), ("gy", 1), ("gz", 0), ("gz", 1), ("gy", 0))
BLOCKS = (("gy", 1), ("gz", 0), ("gz", 1), ("gx", 0), ("gx", 1), ("gy", 0))
IDLE_BLOCKS = {"gx": ("gy", 1), "gy": ("gy", 0), "gz": ("gy", 2)}
IDLE_FIRST = {"gx": ("gy", 1), "gy": ("gy", 0), "gz": ("gy", 2)}
IDLE_SECOND = {"gx": ("gy", 1), "gy": ("gy", 0), "gz": ("gy", 2)}


def links(order):
    return [(axis, first) for axis, first in order if first + 1 < lax.axis_size(axis)]


def partners(axis, first, idle):
    sizes = [lax.axis_size(name) for name in AXES]
    main = AXES.index(axis)
    spare, step = idle.get(axis, (axis, 0))
    spare = AXES.index(spare)
    pairs = []
    for at in itertools.product(*map(range, sizes)):
        to = list(at)
        if first <= at[main] < sizes[main] - (sizes[main] - first) % 2:
            to[main] += 1 - 2 * ((at[main] - first) % 2)
        elif step:
            to[spare] += step - 2 * step * (at[spare] // step % 2)
        else:
            to[spare] = sizes[spare] - 1 - at[spare]
        if to[spare] < sizes[spare]:
            pairs.append(tuple((v[0] * sizes[1] + v[1]) * sizes[2] + v[2] for v in (at, to)))
    return pairs


def swap(buffers, order, idle):
    return [lax.ppermute(buf, AXES, partners(*link, idle)) for buf, link in zip(buffers, links(order))]


def odd_place(axis):
    return lax.rem(lax.axis_index(axis), 2) == 1


def weights():
    values = []
    for axis in AXES:
        place = lax.axis_index(axis)
        values.append(jnp.where(place > 0, 0.5, 1.0).astype(jnp.float32))
        values.append(jnp.where(place < lax.axis_size(axis) - 1, 0.5, 1.0).astype(jnp.float32))
    return values


def outgoing(faces, order):
    picked = []
    for axis, first in links(order):
        number = AXES.index(axis)
        lower, upper = faces[2 * number], faces[2 * number + 1]
        odd = odd_place(axis)
        picked.append(jnp.where(odd, lower, upper) if first == 0 else jnp.where(odd, upper, lower))
    return picked


def incoming(received, order):
    faces = []
    for axis in AXES:
        got = {first: buf for buf, (name, first) in zip(received, links(order)) if name == axis}
        zeros = jnp.zeros_like(received[0])
        even, other = got.get(0, zeros), got.get(1, zeros)
        odd = odd_place(axis)
        place = lax.axis_index(axis)
        faces.append(jnp.where(place > 0, jnp.where(odd, even, other), zeros))
        faces.append(jnp.where(place < lax.axis_size(axis) - 1, jnp.where(odd, other, even), zeros))
    return faces


def split(value):
    high = value.astype(jnp.bfloat16)
    low = (value - high.astype(jnp.float32)).astype(jnp.bfloat16)
    return high, low


def dot(a, b, dims):
    return lax.dot_general(a, b, (dims, ((), ())), preferred_element_type=jnp.float32)


def cut(ref, face):
    return [ref[:, f * face:(f + 1) * face].astype(jnp.float32) for f in range(6)]


def call(kernel, shapes, *args, far=(), far_out=(), scratch=()):
    vmem = pl.BlockSpec(memory_space=pltpu.VMEM)
    hbm = pl.BlockSpec(memory_space=pltpu.HBM)
    near = [a for i, a in enumerate(args) if i not in far] + list(shapes)
    near += [a for a in scratch if isinstance(a, jax.ShapeDtypeStruct)]
    size = sum(a.size * a.dtype.itemsize for a in near)
    scratch = [pltpu.VMEM(a.shape, a.dtype) if isinstance(a, jax.ShapeDtypeStruct) else a for a in scratch]
    return pl.pallas_call(
        kernel,
        out_shape=[pltpu.HBM(s.shape, s.dtype) if i in far_out else s for i, s in enumerate(shapes)],
        in_specs=[hbm if i in far else vmem for i in range(len(args))],
        out_specs=[hbm if i in far_out else vmem for i in range(len(shapes))],
        scratch_shapes=scratch,
        cost_estimate=pl.CostEstimate(flops=10 ** 7, bytes_accessed=size, transcendentals=0),
        compiler_params=pltpu.CompilerParams(vmem_limit_bytes=2 ** 21 + 3 * size // 2),
    )(*[pltpu.with_memory_space_constraint(a, pltpu.HBM) if i in far else a for i, a in enumerate(args)])


def f32(*shape):
    return jax.ShapeDtypeStruct(shape, jnp.float32)


def bf16(*shape):
    return jax.ShapeDtypeStruct(shape, jnp.bfloat16)


def fold(value):
    rows, width = value.shape
    tail = width % 128
    pieces = [value[:, i:i + 128] for i in range(0, width - tail, 128)]
    if tail:
        step = rows * tail // 128
        last = value[:, width - tail:]
        pieces.append(jnp.concatenate([last[i:i + step] for i in range(0, rows, step)], axis=1))
    return jnp.concatenate(pieces, axis=0)


def unfold(value, rows, width):
    tail = width % 128
    full = width // 128
    pieces = [value[i * rows:(i + 1) * rows] for i in range(full)]
    if tail:
        last = value[full * rows:]
        pieces.append(jnp.concatenate([last[:, i:i + tail] for i in range(0, 128, tail)], axis=0))
    return jnp.concatenate(pieces, axis=1)


def pack_face(value, upper):
    rows, width = value.shape
    tail = width % 128
    full = value[:, tail:] if upper else value[:, 0:width - tail]
    rest = value[:, 0:tail] if upper else value[:, width - tail:]
    pieces = [full[:, i:i + 128] for i in range(0, width - tail, 128)]
    if tail:
        step = rows * tail // 128
        pieces.append(jnp.concatenate([rest[i:i + step] for i in range(0, rows, step)], axis=1))
    return jnp.concatenate(pieces, axis=0)


def unpack_pair(from_upper, from_lower, rows, width):
    tail = width % 128
    full = width // 128

    def parts(value):
        pieces = [value[i * rows:(i + 1) * rows] for i in range(full)]
        rest = value[full * rows:]
        return pieces, [jnp.concatenate([rest[:, i:i + tail] for i in range(0, 128, tail)], axis=0)] if tail else []

    below, below_rest = parts(from_upper)
    above, above_rest = parts(from_lower)
    return jnp.concatenate(below_rest + below + above + above_rest, axis=1)


def pick_face(pair, axis, first):
    face = pair.shape[1] // 2
    lower, upper = pack_face(pair[:, 0:face], False), pack_face(pair[:, face:], True)
    odd = odd_place(axis)
    return jnp.where(odd, lower, upper) if first == 0 else jnp.where(odd, upper, lower)


def even_rows(ncf):
    return 2 * ncf


def spans(face, ncf, total):
    sizes = [face * face // 128, even_rows(ncf) * face // 128, ncf * total // 128]
    ends = [sum(sizes[:i + 1]) for i in range(3)]
    return [slice(e - n, e) for e, n in zip(ends, sizes)]


def start_kernel(face, load_ref, blocks_ref, basis_ref, rows_ref, vec_ref, bases_ref, flat_ref, *refs):
    load_near, near_ref, sems = refs[-3:]
    swaps = (len(refs) - 3) // 2
    outs, block_outs = refs[:swaps], refs[swaps:2 * swaps]
    pairs = ((load_ref, load_near), (basis_ref, bases_ref), (rows_ref, flat_ref), (blocks_ref, near_ref))
    copies = [pltpu.make_async_copy(far, near, sems.at[i]) for i, (far, near) in enumerate(pairs)]
    for copy in copies:
        copy.start()
    ncf = bases_ref.shape[0]
    at = spans(face, ncf, flat_ref.shape[0] * flat_ref.shape[1] // ncf)
    copies[0].wait()
    vec_ref[...] = load_near[...].astype(jnp.float32)
    for out, (axis, first) in zip(outs, links(FIRST)):
        low = 2 * face * AXES.index(axis)
        out[...] = pick_face(vec_ref[:, low:low + 2 * face], axis, first)
    copies[1].wait()
    copies[2].wait()
    zeros = jnp.zeros((even_rows(ncf) - ncf, face), jnp.float32)
    flat = fold(flat_ref[...].astype(jnp.float32))
    for out, value in zip(block_outs, outgoing(cut(bases_ref, face), BLOCKS)):
        out[at[1]] = fold(jnp.concatenate([value, zeros], axis=0))
        out[at[2]] = flat
    copies[3].wait()
    for out, (axis, first) in zip(block_outs, links(BLOCKS)):
        upper = lax.rem(lax.axis_index(axis) + 1 + first, 2)
        out[at[0]] = fold(near_ref[2 * AXES.index(axis) + upper].astype(jnp.float32))


def scaled_pairs(face, order, vec_ref, received):
    count = vec_ref.shape[0]
    other = incoming([r[...] for r in received], order)
    weight = weights()
    is_lower = lax.broadcasted_iota(jnp.int32, (1, 2 * face), 1) < face
    pairs = []
    for number in range(len(AXES)):
        low, up = 2 * number, 2 * number + 1
        resid = vec_ref[:, low * face:(low + 2) * face] + unpack_pair(other[low], other[up], count, face)
        pairs.append((resid * jnp.where(is_lower, weight[low], weight[up])).astype(jnp.bfloat16))
    return pairs


def scaled_faces(face, order, vec_ref, received):
    pairs = scaled_pairs(face, order, vec_ref, received)
    return [pair[:, i * face:(i + 1) * face] for pair in pairs for i in range(2)]


def residual_kernel(face, order, pack, vec_ref, basis_ref, *refs):
    received, slots_ref = refs[:-1], refs[-1]
    coarse = None
    for number, scaled in enumerate(scaled_pairs(face, order, vec_ref, received)):
        part = dot(basis_ref[:, 2 * number * face:2 * (number + 1) * face], scaled, ((1,), (1,)))
        coarse = part if coarse is None else coarse + part
    rows = coarse.shape[0] // pack
    slot = jnp.concatenate([coarse[i * rows:(i + 1) * rows] for i in range(pack)], axis=1)
    for d in range(slots_ref.shape[0]):
        slots_ref[d] = slot


def local_kernel(face, n_in, vec_ref, blocks_ref, basis_ref, rows_ref, schur_ref, *refs):
    ncf = basis_ref.shape[0]
    count, width = vec_ref.shape
    received, blocks_received = refs[:n_in], refs[n_in:2 * n_in]
    (start_ref, others_ref, table_ref, all_rows_ref, local_ref,
     own_ref, other_ref, near_ref, bases_ref, sems) = refs[2 * n_in:]
    copy = pltpu.make_async_copy(blocks_ref, own_ref, sems.at[0])
    size = width // 3

    def piece(i):
        rows = pl.ds(pl.multiple_of(i * size, size), size)
        return pltpu.make_async_copy(schur_ref.at[rows], near_ref.at[rows], sems.at[i + 1])

    copy.start()
    lax.fori_loop(0, 3, lambda i, _: piece(i).start(), None)
    at = spans(face, ncf, rows_ref.shape[0] * rows_ref.shape[1] // ncf)
    blocks = incoming([r[at[0]].astype(jnp.bfloat16) for r in blocks_received], BLOCKS)
    bases, rows = [incoming([r[part] for r in blocks_received], BLOCKS) for part in at[1:]]
    weight = weights()
    bases_ref[...] = jnp.zeros_like(bases_ref)
    own = cut(basis_ref, face)
    all_rows = [rows_ref[...].astype(jnp.float32)]
    scaled = scaled_faces(face, FIRST, vec_ref, received)
    copy.wait()
    for f in range(6):
        half = 0.5 * weight[f]
        to = slice(f * face, (f + 1) * face)
        block = unfold(blocks[f], face, face)
        other_ref[f] = block
        local = dot(scaled[f], own_ref[f], ((1,), (0,))) + dot(scaled[f], block, ((1,), (0,)))
        start_ref[:, to] = local * half
        bases_ref[0:ncf, to] = own[f] * half
        bases_ref[ncf * (f + 1):ncf * (f + 2), to] = unfold(bases[f], even_rows(ncf), face)[0:ncf] * half
        all_rows.append(unfold(rows[f], *rows_ref.shape))
    last = pltpu.make_async_copy(other_ref, others_ref, sems.at[0])
    last.start()
    all_rows.append(jnp.zeros_like(all_rows[0]))
    all_rows_ref[...] = jnp.concatenate(all_rows, axis=0)
    terms = bases_ref.shape[0]
    part = bases_ref[...].astype(jnp.bfloat16)
    table_ref[0:terms, 0:width] = part
    table_ref[terms:2 * terms, 0:width] = part
    table_ref[2 * terms:, 0:width] = jnp.zeros_like(part)
    high, low = split(start_ref[...])
    factors = jnp.concatenate([high, low, part], axis=0)
    columns = (slice(0, 4 * face), slice(4 * face, width))
    piece(0).wait()
    piece(1).wait()
    products = [dot(factors[:, 0:2 * size], near_ref[0:2 * size, to], ((1,), (0,))) for to in columns]
    piece(2).wait()
    for to, product in zip(columns, products):
        product = product + dot(factors[:, 2 * size:], near_ref[2 * size:, to], ((1,), (0,)))
        local_ref[:, to] = vec_ref[:, to] - (product[0:count] + product[count:2 * count])
        high, low = split(product[2 * count:])
        to = slice(width + to.start, width + to.stop)
        table_ref[0:terms, to] = high
        table_ref[terms:2 * terms, to] = high
        table_ref[2 * terms:, to] = low
    last.wait()


def advance_kernel(face, vec_ref, blocks_ref, others_ref, start_ref, terms_ref, table_ref, *refs):
    received, out_ref, own_ref, other_ref, sems = refs[:-4], refs[-4], refs[-3], refs[-2], refs[-1]
    pairs = ((blocks_ref, own_ref), (others_ref, other_ref))
    copies = [pltpu.make_async_copy(far, near, sems.at[i]) for i, (far, near) in enumerate(pairs)]
    for copy in copies:
        copy.start()
    weight = weights()
    scaled = scaled_faces(face, SECOND, vec_ref, received)
    iterate = start_ref[...] + dot(terms_ref[...], table_ref[:, 0:vec_ref.shape[1]], ((0,), (0,)))
    for copy in copies:
        copy.wait()
    for f in range(6):
        to = slice(f * face, (f + 1) * face)
        local = dot(scaled[f], own_ref[f], ((1,), (0,))) + dot(scaled[f], other_ref[f], ((1,), (0,)))
        out_ref[:, to] = iterate[:, to] + local * (0.5 * weight[f])


def coarse_terms(slots_ref, rows_ref, count):
    devices, rows, lanes = slots_ref.shape
    slots = slots_ref[...]
    whole = jnp.concatenate([slots[:, :, i:i + count] for i in range(0, lanes, count)], axis=1)
    high, low = split(whole.reshape(devices * rows * (lanes // count), count))
    matrix = rows_ref[...]
    values = dot(matrix, high, ((1,), (0,))) + dot(matrix, low, ((1,), (0,)))
    high, low = split(values)
    return jnp.concatenate([high, low, high], axis=0)


def middle_kernel(face, slots_ref, rows_ref, table_ref, load_ref, terms_ref, local_ref, *outs):
    count, width = load_ref.shape
    terms = coarse_terms(slots_ref, rows_ref, count)
    terms_ref[...] = terms
    for number, axis in enumerate(AXES):
        at = slice(2 * number * face, 2 * (number + 1) * face)
        to = slice(width + 2 * number * face, width + 2 * (number + 1) * face)
        local = load_ref[:, at] - dot(terms, table_ref[:, to], ((0,), (0,)))
        local_ref[:, at] = local
        for out, (name, first) in zip(outs, links(SECOND)):
            if name == axis:
                out[...] = pick_face(local, axis, first)


def last_kernel(slots_ref, rows_ref, table_ref, start_ref, out_ref):
    count, width = start_ref.shape
    two = 2 * table_ref.shape[0] // 3
    terms = coarse_terms(slots_ref, rows_ref, count)[0:two]
    update = dot(terms, table_ref[0:two, 0:width], ((0,), (0,)))
    out_ref[...] = (start_ref[...] + update).astype(jnp.bfloat16)


def body(load, schur, neumann, coarse_basis, coarse_rows):
    count, width = load.shape[3], load.shape[4]
    face = width // 6
    ncf, total = coarse_rows.shape[3], coarse_rows.shape[4]
    devices = total // ncf
    pack = max(128 // count, 1)
    while ncf % pack:
        pack -= 1
    schur2 = schur.reshape(width, width)
    swaps = len(links(FIRST))
    flat_shape = (ncf * total // 256, 256)
    part = [f32(count * face // 128, 128)] * swaps
    big = [f32(spans(face, ncf, total)[-1].stop, 128)] * swaps
    slots = f32(devices, ncf // pack, pack * count)
    blocks_shape = bf16(6, face, face)

    def gather(value):
        return lax.all_to_all(value, AXES, 0, 0)

    blocks = neumann.reshape(6, face, face)
    load_f, basis, rows, *sent = call(
        functools.partial(start_kernel, face),
        [f32(count, width), bf16(ncf, width), bf16(*flat_shape)] + part + big,
        load.reshape(count, width), blocks, coarse_basis.reshape(ncf, width),
        coarse_rows.reshape(flat_shape), far=(0, 1, 2, 3),
        scratch=[bf16(count, width), blocks_shape, pltpu.SemaphoreType.DMA((4,))],
    )
    received = swap(sent[:swaps], FIRST, IDLE_FIRST)
    blocks_received = swap(sent[swaps:], BLOCKS, IDLE_BLOCKS)
    (slot,) = call(functools.partial(residual_kernel, face, FIRST, pack), [slots], load_f, basis, *received)
    whole = gather(slot)
    start, others, table, all_rows, local = call(
        functools.partial(local_kernel, face, swaps),
        [f32(count, width), blocks_shape, bf16(24 * ncf, 2 * width), f32(8 * flat_shape[0], 256), f32(count, width)],
        load_f, blocks, basis, rows, schur2, *received, *blocks_received, far=(1, 4), far_out=(1,),
        scratch=[blocks_shape, blocks_shape, bf16(width, width), f32(8 * ncf, width), pltpu.SemaphoreType.DMA((4,))],
    )
    all_rows = all_rows.reshape(8 * ncf, total).astype(jnp.bfloat16)
    terms, vec, *sent = call(
        functools.partial(middle_kernel, face), [bf16(24 * ncf, count), f32(count, width)] + part,
        whole, all_rows, table, local,
    )
    received = swap(sent, SECOND, IDLE_SECOND)
    (slot,) = call(functools.partial(residual_kernel, face, SECOND, pack), [slots], vec, basis, *received)
    whole = gather(slot)
    (start,) = call(
        functools.partial(advance_kernel, face), [f32(count, width)], vec, blocks, others, start, terms, table, *received,
        far=(1, 2), scratch=[blocks_shape, blocks_shape, pltpu.SemaphoreType.DMA((2,))],
    )
    (result,) = call(last_kernel, [bf16(count, width)], whole, all_rows, table, start)
    return result.reshape(load.shape)


def solution(mesh):
    placed = (
        P("gx", "gy", "gz", None, None),
        P("gx", "gy", "gz", None, None),
        P("gx", "gy", "gz", None, None, None),
        P("gx", "gy", "gz", None, None),
        P("gx", "gy", "gz", None, None),
    )
    return jax.shard_map(
        body, mesh=mesh, in_specs=placed, out_specs=P("gx", "gy", "gz", None, None), check_vma=False
    )
```

```python
import functools
import itertools

import jax
import jax.numpy as jnp
from jax import lax
from jax.experimental import pallas as pl
from jax.experimental.pallas import tpu as pltpu
from jax.sharding import PartitionSpec as P

AXES = ("gx", "gy", "gz")


FIRST = (("gy", 1), ("gz", 0), ("gz", 1), ("gx", 0), ("gx", 1), ("gy", 0))
SECOND = (("gz", 0), ("gz", 1), ("gx", 0), ("gy", 1), ("gx", 1), ("gy", 0))
BLOCKS = (("gx", 0), ("gx", 1), ("gy", 1), ("gz", 0), ("gz", 1), ("gy", 0))
IDLE_BLOCKS = {"gx": ("gy", 1), "gy": ("gz", 1), "gz": ("gy", 2)}
IDLE_FIRST = {"gx": ("gy", 1), "gy": ("gy", 0), "gz": ("gy", 2)}
IDLE_SECOND = {"gx": ("gy", 1), "gy": ("gy", 0), "gz": ("gy", 2)}


def links(order):
    return [(axis, first) for axis, first in order if first + 1 < lax.axis_size(axis)]


def partners(axis, first, idle):
    sizes = [lax.axis_size(name) for name in AXES]
    main = AXES.index(axis)
    spare, step = idle.get(axis, (axis, 0))
    spare = AXES.index(spare)
    pairs = []
    for at in itertools.product(*map(range, sizes)):
        to = list(at)
        if first <= at[main] < sizes[main] - (sizes[main] - first) % 2:
            to[main] += 1 - 2 * ((at[main] - first) % 2)
        elif step:
            to[spare] += step - 2 * step * (at[spare] // step % 2)
        else:
            to[spare] = sizes[spare] - 1 - at[spare]
        if to[spare] < sizes[spare]:
            pairs.append(tuple((v[0] * sizes[1] + v[1]) * sizes[2] + v[2] for v in (at, to)))
    return pairs


def swap(buffers, order, idle):
    return [lax.ppermute(buf, AXES, partners(*link, idle)) for buf, link in zip(buffers, links(order))]


def odd_place(axis):
    return lax.rem(lax.axis_index(axis), 2) == 1


def weights():
    values = []
    for axis in AXES:
        place = lax.axis_index(axis)
        values.append(jnp.where(place > 0, 0.5, 1.0).astype(jnp.float32))
        values.append(jnp.where(place < lax.axis_size(axis) - 1, 0.5, 1.0).astype(jnp.float32))
    return values


def outgoing(faces, order):
    picked = []
    for axis, first in links(order):
        number = AXES.index(axis)
        lower, upper = faces[2 * number], faces[2 * number + 1]
        odd = odd_place(axis)
        picked.append(jnp.where(odd, lower, upper) if first == 0 else jnp.where(odd, upper, lower))
    return picked


def incoming(received, order):
    faces = []
    for axis in AXES:
        got = {first: buf for buf, (name, first) in zip(received, links(order)) if name == axis}
        zeros = jnp.zeros_like(received[0])
        even, other = got.get(0, zeros), got.get(1, zeros)
        odd = odd_place(axis)
        place = lax.axis_index(axis)
        faces.append(jnp.where(place > 0, jnp.where(odd, even, other), zeros))
        faces.append(jnp.where(place < lax.axis_size(axis) - 1, jnp.where(odd, other, even), zeros))
    return faces


def split(value):
    high = value.astype(jnp.bfloat16)
    low = (value - high.astype(jnp.float32)).astype(jnp.bfloat16)
    return high, low


def dot(a, b, dims):
    return lax.dot_general(a, b, (dims, ((), ())), preferred_element_type=jnp.float32)


def cut(ref, face):
    return [ref[:, f * face:(f + 1) * face].astype(jnp.float32) for f in range(6)]


def call(kernel, shapes, *args, far=(), far_out=(), scratch=()):
    vmem = pl.BlockSpec(memory_space=pltpu.VMEM)
    hbm = pl.BlockSpec(memory_space=pltpu.HBM)
    near = [a for i, a in enumerate(args) if i not in far] + list(shapes)
    near += [a for a in scratch if isinstance(a, jax.ShapeDtypeStruct)]
    size = sum(a.size * a.dtype.itemsize for a in near)
    scratch = [pltpu.VMEM(a.shape, a.dtype) if isinstance(a, jax.ShapeDtypeStruct) else a for a in scratch]
    return pl.pallas_call(
        kernel,
        out_shape=[pltpu.HBM(s.shape, s.dtype) if i in far_out else s for i, s in enumerate(shapes)],
        in_specs=[hbm if i in far else vmem for i in range(len(args))],
        out_specs=[hbm if i in far_out else vmem for i in range(len(shapes))],
        scratch_shapes=scratch,
        cost_estimate=pl.CostEstimate(flops=10 ** 7, bytes_accessed=size, transcendentals=0),
        compiler_params=pltpu.CompilerParams(vmem_limit_bytes=2 ** 21 + 3 * size // 2),
    )(*[pltpu.with_memory_space_constraint(a, pltpu.HBM) if i in far else a for i, a in enumerate(args)])


def f32(*shape):
    return jax.ShapeDtypeStruct(shape, jnp.float32)


def bf16(*shape):
    return jax.ShapeDtypeStruct(shape, jnp.bfloat16)


def fold(value):
    rows, width = value.shape
    tail = width % 128
    pieces = [value[:, i:i + 128] for i in range(0, width - tail, 128)]
    if tail:
        step = rows * tail // 128
        last = value[:, width - tail:]
        pieces.append(jnp.concatenate([last[i:i + step] for i in range(0, rows, step)], axis=1))
    return jnp.concatenate(pieces, axis=0)


def unfold(value, rows, width):
    tail = width % 128
    full = width // 128
    pieces = [value[i * rows:(i + 1) * rows] for i in range(full)]
    if tail:
        last = value[full * rows:]
        pieces.append(jnp.concatenate([last[:, i:i + tail] for i in range(0, 128, tail)], axis=0))
    return jnp.concatenate(pieces, axis=1)


def pack_face(value, upper):
    rows, width = value.shape
    tail = width % 128
    full = value[:, tail:] if upper else value[:, 0:width - tail]
    rest = value[:, 0:tail] if upper else value[:, width - tail:]
    pieces = [full[:, i:i + 128] for i in range(0, width - tail, 128)]
    if tail:
        step = rows * tail // 128
        pieces.append(jnp.concatenate([rest[i:i + step] for i in range(0, rows, step)], axis=1))
    return jnp.concatenate(pieces, axis=0)


def unpack_pair(from_upper, from_lower, rows, width):
    tail = width % 128
    full = width // 128

    def parts(value):
        pieces = [value[i * rows:(i + 1) * rows] for i in range(full)]
        rest = value[full * rows:]
        return pieces, [jnp.concatenate([rest[:, i:i + tail] for i in range(0, 128, tail)], axis=0)] if tail else []

    below, below_rest = parts(from_upper)
    above, above_rest = parts(from_lower)
    return jnp.concatenate(below_rest + below + above + above_rest, axis=1)


def pick_face(pair, axis, first):
    face = pair.shape[1] // 2
    lower, upper = pack_face(pair[:, 0:face], False), pack_face(pair[:, face:], True)
    odd = odd_place(axis)
    return jnp.where(odd, lower, upper) if first == 0 else jnp.where(odd, upper, lower)


def even_rows(ncf):
    return 2 * ncf


def spans(face, ncf, total):
    sizes = [face * face // 128, even_rows(ncf) * face // 128, ncf * total // 128]
    ends = [sum(sizes[:i + 1]) for i in range(3)]
    return [slice(e - n, e) for e, n in zip(ends, sizes)]


def start_kernel(face, load_ref, blocks_ref, basis_ref, rows_ref, vec_ref, bases_ref, flat_ref, *refs):
    load_near, near_ref, sems = refs[-3:]
    swaps = (len(refs) - 3) // 2
    outs, block_outs = refs[:swaps], refs[swaps:2 * swaps]
    pairs = ((load_ref, load_near), (basis_ref, bases_ref), (rows_ref, flat_ref), (blocks_ref, near_ref))
    copies = [pltpu.make_async_copy(far, near, sems.at[i]) for i, (far, near) in enumerate(pairs)]
    for copy in copies:
        copy.start()
    ncf = bases_ref.shape[0]
    at = spans(face, ncf, flat_ref.shape[0] * flat_ref.shape[1] // ncf)
    copies[0].wait()
    vec_ref[...] = load_near[...].astype(jnp.float32)
    for out, (axis, first) in zip(outs, links(FIRST)):
        low = 2 * face * AXES.index(axis)
        out[...] = pick_face(vec_ref[:, low:low + 2 * face], axis, first)
    copies[1].wait()
    copies[2].wait()
    zeros = jnp.zeros((even_rows(ncf) - ncf, face), jnp.float32)
    flat = fold(flat_ref[...].astype(jnp.float32))
    for out, value in zip(block_outs, outgoing(cut(bases_ref, face), BLOCKS)):
        out[at[1]] = fold(jnp.concatenate([value, zeros], axis=0))
        out[at[2]] = flat
    copies[3].wait()
    for out, (axis, first) in zip(block_outs, links(BLOCKS)):
        upper = lax.rem(lax.axis_index(axis) + 1 + first, 2)
        out[at[0]] = fold(near_ref[2 * AXES.index(axis) + upper].astype(jnp.float32))


def scaled_pairs(face, order, vec_ref, received):
    count = vec_ref.shape[0]
    other = incoming([r[...] for r in received], order)
    weight = weights()
    is_lower = lax.broadcasted_iota(jnp.int32, (1, 2 * face), 1) < face
    pairs = []
    for number in range(len(AXES)):
        low, up = 2 * number, 2 * number + 1
        resid = vec_ref[:, low * face:(low + 2) * face] + unpack_pair(other[low], other[up], count, face)
        pairs.append((resid * jnp.where(is_lower, weight[low], weight[up])).astype(jnp.bfloat16))
    return pairs


def scaled_faces(face, order, vec_ref, received):
    pairs = scaled_pairs(face, order, vec_ref, received)
    return [pair[:, i * face:(i + 1) * face] for pair in pairs for i in range(2)]


def residual_kernel(face, order, pack, vec_ref, basis_ref, *refs):
    received, slots_ref = refs[:-1], refs[-1]
    coarse = None
    for number, scaled in enumerate(scaled_pairs(face, order, vec_ref, received)):
        part = dot(basis_ref[:, 2 * number * face:2 * (number + 1) * face], scaled, ((1,), (1,)))
        coarse = part if coarse is None else coarse + part
    rows = coarse.shape[0] // pack
    slot = jnp.concatenate([coarse[i * rows:(i + 1) * rows] for i in range(pack)], axis=1)
    for d in range(slots_ref.shape[0]):
        slots_ref[d] = slot


def local_kernel(face, n_in, vec_ref, blocks_ref, basis_ref, rows_ref, schur_ref, *refs):
    ncf = basis_ref.shape[0]
    count, width = vec_ref.shape
    received, blocks_received = refs[:n_in], refs[n_in:2 * n_in]
    (start_ref, others_ref, table_ref, all_rows_ref, local_ref,
     own_ref, other_ref, near_ref, bases_ref, sems) = refs[2 * n_in:]
    copy = pltpu.make_async_copy(blocks_ref, own_ref, sems.at[0])
    size = width // 3

    def piece(i):
        rows = pl.ds(pl.multiple_of(i * size, size), size)
        return pltpu.make_async_copy(schur_ref.at[rows], near_ref.at[rows], sems.at[i + 1])

    copy.start()
    lax.fori_loop(0, 3, lambda i, _: piece(i).start(), None)
    at = spans(face, ncf, rows_ref.shape[0] * rows_ref.shape[1] // ncf)
    blocks = incoming([r[at[0]].astype(jnp.bfloat16) for r in blocks_received], BLOCKS)
    bases, rows = [incoming([r[part] for r in blocks_received], BLOCKS) for part in at[1:]]
    weight = weights()
    bases_ref[...] = jnp.zeros_like(bases_ref)
    own = cut(basis_ref, face)
    all_rows = [rows_ref[...].astype(jnp.float32)]
    scaled = scaled_faces(face, FIRST, vec_ref, received)
    copy.wait()
    for f in range(6):
        half = 0.5 * weight[f]
        to = slice(f * face, (f + 1) * face)
        block = unfold(blocks[f], face, face)
        other_ref[f] = block
        local = dot(scaled[f], own_ref[f], ((1,), (0,))) + dot(scaled[f], block, ((1,), (0,)))
        start_ref[:, to] = local * half
        bases_ref[0:ncf, to] = own[f] * half
        bases_ref[ncf * (f + 1):ncf * (f + 2), to] = unfold(bases[f], even_rows(ncf), face)[0:ncf] * half
        all_rows.append(unfold(rows[f], *rows_ref.shape))
    last = pltpu.make_async_copy(other_ref, others_ref, sems.at[0])
    last.start()
    all_rows.append(jnp.zeros_like(all_rows[0]))
    all_rows_ref[...] = jnp.concatenate(all_rows, axis=0)
    terms = bases_ref.shape[0]
    part = bases_ref[...].astype(jnp.bfloat16)
    table_ref[0:terms, 0:width] = part
    table_ref[terms:2 * terms, 0:width] = part
    table_ref[2 * terms:, 0:width] = jnp.zeros_like(part)
    high, low = split(start_ref[...])
    factors = jnp.concatenate([high, low, part], axis=0)
    columns = (slice(0, 4 * face), slice(4 * face, width))
    piece(0).wait()
    piece(1).wait()
    products = [dot(factors[:, 0:2 * size], near_ref[0:2 * size, to], ((1,), (0,))) for to in columns]
    piece(2).wait()
    for to, product in zip(columns, products):
        product = product + dot(factors[:, 2 * size:], near_ref[2 * size:, to], ((1,), (0,)))
        local_ref[:, to] = vec_ref[:, to] - (product[0:count] + product[count:2 * count])
        high, low = split(product[2 * count:])
        to = slice(width + to.start, width + to.stop)
        table_ref[0:terms, to] = high
        table_ref[terms:2 * terms, to] = high
        table_ref[2 * terms:, to] = low
    last.wait()


def advance_kernel(face, vec_ref, blocks_ref, others_ref, iterate_ref, *refs):
    received, out_ref, own_ref, other_ref, sems = refs[:-4], refs[-4], refs[-3], refs[-2], refs[-1]
    pairs = ((blocks_ref, own_ref), (others_ref, other_ref))
    copies = [pltpu.make_async_copy(far, near, sems.at[i]) for i, (far, near) in enumerate(pairs)]
    for copy in copies:
        copy.start()
    weight = weights()
    scaled = scaled_faces(face, SECOND, vec_ref, received)
    for copy in copies:
        copy.wait()
    for f in range(6):
        to = slice(f * face, (f + 1) * face)
        local = dot(scaled[f], own_ref[f], ((1,), (0,))) + dot(scaled[f], other_ref[f], ((1,), (0,)))
        out_ref[:, to] = iterate_ref[:, to] + local * (0.5 * weight[f])


def coarse_terms(slots_ref, rows_ref, count):
    devices, rows, lanes = slots_ref.shape
    slots = slots_ref[...]
    whole = jnp.concatenate([slots[:, :, i:i + count] for i in range(0, lanes, count)], axis=1)
    high, low = split(whole.reshape(devices * rows * (lanes // count), count))
    matrix = rows_ref[...]
    values = dot(matrix, high, ((1,), (0,))) + dot(matrix, low, ((1,), (0,)))
    high, low = split(values)
    return jnp.concatenate([high, low, high], axis=0)


def middle_kernel(face, slots_ref, rows_ref, table_ref, start_ref, load_ref, iterate_ref, local_ref, *outs):
    terms = coarse_terms(slots_ref, rows_ref, start_ref.shape[0])
    width = start_ref.shape[1]
    for number, axis in enumerate(AXES):
        at = slice(2 * number * face, 2 * (number + 1) * face)
        to = slice(width + 2 * number * face, width + 2 * (number + 1) * face)
        local = load_ref[:, at] - dot(terms, table_ref[:, to], ((0,), (0,)))
        local_ref[:, at] = local
        for out, (name, first) in zip(outs, links(SECOND)):
            if name == axis:
                out[...] = pick_face(local, axis, first)
    iterate_ref[...] = start_ref[...] + dot(terms, table_ref[:, 0:width], ((0,), (0,)))


def last_kernel(slots_ref, rows_ref, table_ref, start_ref, out_ref):
    count, width = start_ref.shape
    two = 2 * table_ref.shape[0] // 3
    terms = coarse_terms(slots_ref, rows_ref, count)[0:two]
    update = dot(terms, table_ref[0:two, 0:width], ((0,), (0,)))
    out_ref[...] = (start_ref[...] + update).astype(jnp.bfloat16)


def body(load, schur, neumann, coarse_basis, coarse_rows):
    count, width = load.shape[3], load.shape[4]
    face = width // 6
    ncf, total = coarse_rows.shape[3], coarse_rows.shape[4]
    devices = total // ncf
    pack = max(128 // count, 1)
    while ncf % pack:
        pack -= 1
    schur2 = schur.reshape(width, width)
    swaps = len(links(FIRST))
    flat_shape = (ncf * total // 256, 256)
    part = [f32(count * face // 128, 128)] * swaps
    big = [f32(spans(face, ncf, total)[-1].stop, 128)] * swaps
    slots = f32(devices, ncf // pack, pack * count)
    blocks_shape = bf16(6, face, face)

    def gather(value):
        return lax.all_to_all(value, AXES, 0, 0)

    blocks = neumann.reshape(6, face, face)
    load_f, basis, rows, *sent = call(
        functools.partial(start_kernel, face),
        [f32(count, width), bf16(ncf, width), bf16(*flat_shape)] + part + big,
        load.reshape(count, width), blocks, coarse_basis.reshape(ncf, width),
        coarse_rows.reshape(flat_shape), far=(0, 1, 2, 3),
        scratch=[bf16(count, width), blocks_shape, pltpu.SemaphoreType.DMA((4,))],
    )
    received = swap(sent[:swaps], FIRST, IDLE_FIRST)
    blocks_received = swap(sent[swaps:], BLOCKS, IDLE_BLOCKS)
    (slot,) = call(functools.partial(residual_kernel, face, FIRST, pack), [slots], load_f, basis, *received)
    whole = gather(slot)
    start, others, table, all_rows, local = call(
        functools.partial(local_kernel, face, swaps),
        [f32(count, width), blocks_shape, bf16(24 * ncf, 2 * width), f32(8 * flat_shape[0], 256), f32(count, width)],
        load_f, blocks, basis, rows, schur2, *received, *blocks_received, far=(1, 4), far_out=(1,),
        scratch=[blocks_shape, blocks_shape, bf16(width, width), f32(8 * ncf, width), pltpu.SemaphoreType.DMA((4,))],
    )
    all_rows = all_rows.reshape(8 * ncf, total).astype(jnp.bfloat16)
    iterate, vec, *sent = call(
        functools.partial(middle_kernel, face), [f32(count, width), f32(count, width)] + part,
        whole, all_rows, table, start, local,
    )
    received = swap(sent, SECOND, IDLE_SECOND)
    (slot,) = call(functools.partial(residual_kernel, face, SECOND, pack), [slots], vec, basis, *received)
    whole = gather(slot)
    (start,) = call(
        functools.partial(advance_kernel, face), [f32(count, width)], vec, blocks, others, iterate, *received,
        far=(1, 2), scratch=[blocks_shape, blocks_shape, pltpu.SemaphoreType.DMA((2,))],
    )
    (result,) = call(last_kernel, [bf16(count, width)], whole, all_rows, table, start)
    return result.reshape(load.shape)


def solution(mesh):
    placed = (
        P("gx", "gy", "gz", None, None),
        P("gx", "gy", "gz", None, None),
        P("gx", "gy", "gz", None, None, None),
        P("gx", "gy", "gz", None, None),
        P("gx", "gy", "gz", None, None),
    )
    return jax.shard_map(
        body, mesh=mesh, in_specs=placed, out_specs=P("gx", "gy", "gz", None, None), check_vma=False
    )
```

```python
import functools
import itertools

import jax
import jax.numpy as jnp
from jax import lax
from jax.experimental import pallas as pl
from jax.experimental.pallas import tpu as pltpu
from jax.sharding import PartitionSpec as P

AXES = ("gx", "gy", "gz")


FIRST = (("gy", 1), ("gz", 0), ("gz", 1), ("gx", 0), ("gx", 1), ("gy", 0))
SECOND = (("gz", 0), ("gz", 1), ("gx", 0), ("gy", 1), ("gx", 1), ("gy", 0))
BLOCKS = (("gx", 0), ("gx", 1), ("gy", 1), ("gz", 0), ("gz", 1), ("gy", 0))
IDLE_BLOCKS = {"gx": ("gy", 1), "gy": ("gz", 1), "gz": ("gy", 2)}
IDLE_FIRST = {"gx": ("gy", 1), "gy": ("gy", 0), "gz": ("gy", 2)}
IDLE_SECOND = {"gx": ("gy", 1), "gy": ("gy", 0), "gz": ("gy", 2)}


def links(order):
    return [(axis, first) for axis, first in order if first + 1 < lax.axis_size(axis)]


def partners(axis, first, idle):
    sizes = [lax.axis_size(name) for name in AXES]
    main = AXES.index(axis)
    spare, step = idle.get(axis, (axis, 0))
    spare = AXES.index(spare)
    pairs = []
    for at in itertools.product(*map(range, sizes)):
        to = list(at)
        if first <= at[main] < sizes[main] - (sizes[main] - first) % 2:
            to[main] += 1 - 2 * ((at[main] - first) % 2)
        elif step:
            to[spare] += step - 2 * step * (at[spare] // step % 2)
        else:
            to[spare] = sizes[spare] - 1 - at[spare]
        if to[spare] < sizes[spare]:
            pairs.append(tuple((v[0] * sizes[1] + v[1]) * sizes[2] + v[2] for v in (at, to)))
    return pairs


def swap(buffers, order, idle):
    return [lax.ppermute(buf, AXES, partners(*link, idle)) for buf, link in zip(buffers, links(order))]


def odd_place(axis):
    return lax.rem(lax.axis_index(axis), 2) == 1


def weights():
    values = []
    for axis in AXES:
        place = lax.axis_index(axis)
        values.append(jnp.where(place > 0, 0.5, 1.0).astype(jnp.float32))
        values.append(jnp.where(place < lax.axis_size(axis) - 1, 0.5, 1.0).astype(jnp.float32))
    return values


def outgoing(faces, order):
    picked = []
    for axis, first in links(order):
        number = AXES.index(axis)
        lower, upper = faces[2 * number], faces[2 * number + 1]
        odd = odd_place(axis)
        picked.append(jnp.where(odd, lower, upper) if first == 0 else jnp.where(odd, upper, lower))
    return picked


def incoming(received, order):
    faces = []
    for axis in AXES:
        got = {first: buf for buf, (name, first) in zip(received, links(order)) if name == axis}
        zeros = jnp.zeros_like(received[0])
        even, other = got.get(0, zeros), got.get(1, zeros)
        odd = odd_place(axis)
        place = lax.axis_index(axis)
        faces.append(jnp.where(place > 0, jnp.where(odd, even, other), zeros))
        faces.append(jnp.where(place < lax.axis_size(axis) - 1, jnp.where(odd, other, even), zeros))
    return faces


def split(value):
    high = value.astype(jnp.bfloat16)
    low = (value - high.astype(jnp.float32)).astype(jnp.bfloat16)
    return high, low


def dot(a, b, dims):
    return lax.dot_general(a, b, (dims, ((), ())), preferred_element_type=jnp.float32)


def cut(ref, face):
    return [ref[:, f * face:(f + 1) * face].astype(jnp.float32) for f in range(6)]


def call(kernel, shapes, *args, far=(), far_out=(), scratch=()):
    vmem = pl.BlockSpec(memory_space=pltpu.VMEM)
    hbm = pl.BlockSpec(memory_space=pltpu.HBM)
    near = [a for i, a in enumerate(args) if i not in far] + list(shapes)
    near += [a for a in scratch if isinstance(a, jax.ShapeDtypeStruct)]
    size = sum(a.size * a.dtype.itemsize for a in near)
    scratch = [pltpu.VMEM(a.shape, a.dtype) if isinstance(a, jax.ShapeDtypeStruct) else a for a in scratch]
    return pl.pallas_call(
        kernel,
        out_shape=[pltpu.HBM(s.shape, s.dtype) if i in far_out else s for i, s in enumerate(shapes)],
        in_specs=[hbm if i in far else vmem for i in range(len(args))],
        out_specs=[hbm if i in far_out else vmem for i in range(len(shapes))],
        scratch_shapes=scratch,
        cost_estimate=pl.CostEstimate(flops=10 ** 7, bytes_accessed=size, transcendentals=0),
        compiler_params=pltpu.CompilerParams(vmem_limit_bytes=2 ** 21 + 3 * size // 2),
    )(*[pltpu.with_memory_space_constraint(a, pltpu.HBM) if i in far else a for i, a in enumerate(args)])


def f32(*shape):
    return jax.ShapeDtypeStruct(shape, jnp.float32)


def bf16(*shape):
    return jax.ShapeDtypeStruct(shape, jnp.bfloat16)


def fold(value):
    rows, width = value.shape
    tail = width % 128
    pieces = [value[:, i:i + 128] for i in range(0, width - tail, 128)]
    if tail:
        step = rows * tail // 128
        last = value[:, width - tail:]
        pieces.append(jnp.concatenate([last[i:i + step] for i in range(0, rows, step)], axis=1))
    return jnp.concatenate(pieces, axis=0)


def unfold(value, rows, width):
    tail = width % 128
    full = width // 128
    pieces = [value[i * rows:(i + 1) * rows] for i in range(full)]
    if tail:
        last = value[full * rows:]
        pieces.append(jnp.concatenate([last[:, i:i + tail] for i in range(0, 128, tail)], axis=0))
    return jnp.concatenate(pieces, axis=1)


def pack_face(value, upper):
    rows, width = value.shape
    tail = width % 128
    full = value[:, tail:] if upper else value[:, 0:width - tail]
    rest = value[:, 0:tail] if upper else value[:, width - tail:]
    pieces = [full[:, i:i + 128] for i in range(0, width - tail, 128)]
    if tail:
        step = rows * tail // 128
        pieces.append(jnp.concatenate([rest[i:i + step] for i in range(0, rows, step)], axis=1))
    return jnp.concatenate(pieces, axis=0)


def unpack_pair(from_upper, from_lower, rows, width):
    tail = width % 128
    full = width // 128

    def parts(value):
        pieces = [value[i * rows:(i + 1) * rows] for i in range(full)]
        rest = value[full * rows:]
        return pieces, [jnp.concatenate([rest[:, i:i + tail] for i in range(0, 128, tail)], axis=0)] if tail else []

    below, below_rest = parts(from_upper)
    above, above_rest = parts(from_lower)
    return jnp.concatenate(below_rest + below + above + above_rest, axis=1)


def pick_face(pair, axis, first):
    face = pair.shape[1] // 2
    lower, upper = pack_face(pair[:, 0:face], False), pack_face(pair[:, face:], True)
    odd = odd_place(axis)
    return jnp.where(odd, lower, upper) if first == 0 else jnp.where(odd, upper, lower)


def even_rows(ncf):
    return 2 * ncf


def spans(face, ncf, total):
    sizes = [face * face // 128, even_rows(ncf) * face // 128, ncf * total // 128]
    ends = [sum(sizes[:i + 1]) for i in range(3)]
    return [slice(e - n, e) for e, n in zip(ends, sizes)]


def start_kernel(face, load_ref, blocks_ref, basis_ref, rows_ref, vec_ref, bases_ref, flat_ref, *refs):
    load_near, near_ref, sems = refs[-3:]
    swaps = (len(refs) - 3) // 2
    outs, block_outs = refs[:swaps], refs[swaps:2 * swaps]
    pairs = ((load_ref, load_near), (basis_ref, bases_ref), (rows_ref, flat_ref), (blocks_ref, near_ref))
    copies = [pltpu.make_async_copy(far, near, sems.at[i]) for i, (far, near) in enumerate(pairs)]
    for copy in copies:
        copy.start()
    ncf = bases_ref.shape[0]
    at = spans(face, ncf, flat_ref.shape[0] * flat_ref.shape[1] // ncf)
    copies[0].wait()
    vec_ref[...] = load_near[...].astype(jnp.float32)
    for out, (axis, first) in zip(outs, links(FIRST)):
        low = 2 * face * AXES.index(axis)
        out[...] = pick_face(vec_ref[:, low:low + 2 * face], axis, first)
    copies[1].wait()
    copies[2].wait()
    zeros = jnp.zeros((even_rows(ncf) - ncf, face), jnp.float32)
    flat = fold(flat_ref[...].astype(jnp.float32))
    for out, value in zip(block_outs, outgoing(cut(bases_ref, face), BLOCKS)):
        out[at[1]] = fold(jnp.concatenate([value, zeros], axis=0))
        out[at[2]] = flat
    copies[3].wait()
    for out, (axis, first) in zip(block_outs, links(BLOCKS)):
        upper = lax.rem(lax.axis_index(axis) + 1 + first, 2)
        out[at[0]] = fold(near_ref[2 * AXES.index(axis) + upper].astype(jnp.float32))


def scaled_pairs(face, order, vec_ref, received):
    count = vec_ref.shape[0]
    other = incoming([r[...] for r in received], order)
    weight = weights()
    is_lower = lax.broadcasted_iota(jnp.int32, (1, 2 * face), 1) < face
    pairs = []
    for number in range(len(AXES)):
        low, up = 2 * number, 2 * number + 1
        resid = vec_ref[:, low * face:(low + 2) * face] + unpack_pair(other[low], other[up], count, face)
        pairs.append((resid * jnp.where(is_lower, weight[low], weight[up])).astype(jnp.bfloat16))
    return pairs


def scaled_faces(face, order, vec_ref, received):
    pairs = scaled_pairs(face, order, vec_ref, received)
    return [pair[:, i * face:(i + 1) * face] for pair in pairs for i in range(2)]


def residual_kernel(face, order, pack, vec_ref, basis_ref, *refs):
    received, slots_ref = refs[:-1], refs[-1]
    coarse = None
    for number, scaled in enumerate(scaled_pairs(face, order, vec_ref, received)):
        part = dot(basis_ref[:, 2 * number * face:2 * (number + 1) * face], scaled, ((1,), (1,)))
        coarse = part if coarse is None else coarse + part
    rows = coarse.shape[0] // pack
    slot = jnp.concatenate([coarse[i * rows:(i + 1) * rows] for i in range(pack)], axis=1)
    for d in range(slots_ref.shape[0]):
        slots_ref[d] = slot


def local_kernel(face, n_in, vec_ref, blocks_ref, basis_ref, rows_ref, schur_ref, *refs):
    ncf = basis_ref.shape[0]
    count, width = vec_ref.shape
    received, blocks_received = refs[:n_in], refs[n_in:2 * n_in]
    (start_ref, others_ref, table_ref, all_rows_ref, local_ref,
     own_ref, other_ref, near_ref, bases_ref, sems) = refs[2 * n_in:]
    copy = pltpu.make_async_copy(blocks_ref, own_ref, sems.at[0])
    size = width // 3

    def piece(i):
        rows = pl.ds(pl.multiple_of(i * size, size), size)
        return pltpu.make_async_copy(schur_ref.at[rows], near_ref.at[rows], sems.at[i + 1])

    copy.start()
    lax.fori_loop(0, 3, lambda i, _: piece(i).start(), None)
    at = spans(face, ncf, rows_ref.shape[0] * rows_ref.shape[1] // ncf)
    blocks = incoming([r[at[0]].astype(jnp.bfloat16) for r in blocks_received], BLOCKS)
    bases, rows = [incoming([r[part] for r in blocks_received], BLOCKS) for part in at[1:]]
    weight = weights()
    bases_ref[...] = jnp.zeros_like(bases_ref)
    own = cut(basis_ref, face)
    all_rows = [rows_ref[...].astype(jnp.float32)]
    scaled = scaled_faces(face, FIRST, vec_ref, received)
    copy.wait()
    for f in range(6):
        half = 0.5 * weight[f]
        to = slice(f * face, (f + 1) * face)
        block = unfold(blocks[f], face, face)
        other_ref[f] = block
        local = dot(scaled[f], own_ref[f], ((1,), (0,))) + dot(scaled[f], block, ((1,), (0,)))
        start_ref[:, to] = local * half
        bases_ref[0:ncf, to] = own[f] * half
        bases_ref[ncf * (f + 1):ncf * (f + 2), to] = unfold(bases[f], even_rows(ncf), face)[0:ncf] * half
        all_rows.append(unfold(rows[f], *rows_ref.shape))
    last = pltpu.make_async_copy(other_ref, others_ref, sems.at[0])
    last.start()
    all_rows.append(jnp.zeros_like(all_rows[0]))
    all_rows_ref[...] = jnp.concatenate(all_rows, axis=0)
    terms = bases_ref.shape[0]
    part = bases_ref[...].astype(jnp.bfloat16)
    table_ref[0:terms, 0:width] = part
    table_ref[terms:2 * terms, 0:width] = part
    table_ref[2 * terms:, 0:width] = jnp.zeros_like(part)
    high, low = split(start_ref[...])
    factors = jnp.concatenate([high, low, part], axis=0)
    columns = (slice(0, 4 * face), slice(4 * face, width))
    piece(0).wait()
    piece(1).wait()
    products = [dot(factors[:, 0:2 * size], near_ref[0:2 * size, to], ((1,), (0,))) for to in columns]
    piece(2).wait()
    for to, product in zip(columns, products):
        product = product + dot(factors[:, 2 * size:], near_ref[2 * size:, to], ((1,), (0,)))
        local_ref[:, to] = vec_ref[:, to] - (product[0:count] + product[count:2 * count])
        high, low = split(product[2 * count:])
        to = slice(width + to.start, width + to.stop)
        table_ref[0:terms, to] = high
        table_ref[terms:2 * terms, to] = high
        table_ref[2 * terms:, to] = low
    last.wait()


def advance_kernel(face, vec_ref, blocks_ref, others_ref, start_ref, terms_ref, table_ref, *refs):
    received, out_ref, own_ref, other_ref, sems = refs[:-4], refs[-4], refs[-3], refs[-2], refs[-1]
    pairs = ((blocks_ref, own_ref), (others_ref, other_ref))
    copies = [pltpu.make_async_copy(far, near, sems.at[i]) for i, (far, near) in enumerate(pairs)]
    for copy in copies:
        copy.start()
    weight = weights()
    scaled = scaled_faces(face, SECOND, vec_ref, received)
    iterate = start_ref[...] + dot(terms_ref[...], table_ref[:, 0:vec_ref.shape[1]], ((0,), (0,)))
    for copy in copies:
        copy.wait()
    for f in range(6):
        to = slice(f * face, (f + 1) * face)
        local = dot(scaled[f], own_ref[f], ((1,), (0,))) + dot(scaled[f], other_ref[f], ((1,), (0,)))
        out_ref[:, to] = iterate[:, to] + local * (0.5 * weight[f])


def coarse_terms(slots_ref, rows_ref, count):
    devices, rows, lanes = slots_ref.shape
    slots = slots_ref[...]
    whole = jnp.concatenate([slots[:, :, i:i + count] for i in range(0, lanes, count)], axis=1)
    high, low = split(whole.reshape(devices * rows * (lanes // count), count))
    matrix = rows_ref[...]
    values = dot(matrix, high, ((1,), (0,))) + dot(matrix, low, ((1,), (0,)))
    high, low = split(values)
    return jnp.concatenate([high, low, high], axis=0)


def middle_kernel(face, slots_ref, rows_ref, table_ref, load_ref, terms_ref, local_ref, *outs):
    count, width = load_ref.shape
    terms = coarse_terms(slots_ref, rows_ref, count)
    terms_ref[...] = terms
    for number, axis in enumerate(AXES):
        at = slice(2 * number * face, 2 * (number + 1) * face)
        to = slice(width + 2 * number * face, width + 2 * (number + 1) * face)
        local = load_ref[:, at] - dot(terms, table_ref[:, to], ((0,), (0,)))
        local_ref[:, at] = local
        for out, (name, first) in zip(outs, links(SECOND)):
            if name == axis:
                out[...] = pick_face(local, axis, first)


def last_kernel(slots_ref, rows_ref, table_ref, start_ref, out_ref):
    count, width = start_ref.shape
    two = 2 * table_ref.shape[0] // 3
    terms = coarse_terms(slots_ref, rows_ref, count)[0:two]
    update = dot(terms, table_ref[0:two, 0:width], ((0,), (0,)))
    out_ref[...] = (start_ref[...] + update).astype(jnp.bfloat16)


def body(load, schur, neumann, coarse_basis, coarse_rows):
    count, width = load.shape[3], load.shape[4]
    face = width // 6
    ncf, total = coarse_rows.shape[3], coarse_rows.shape[4]
    devices = total // ncf
    pack = max(128 // count, 1)
    while ncf % pack:
        pack -= 1
    schur2 = schur.reshape(width, width)
    swaps = len(links(FIRST))
    flat_shape = (ncf * total // 256, 256)
    part = [f32(count * face // 128, 128)] * swaps
    big = [f32(spans(face, ncf, total)[-1].stop, 128)] * swaps
    slots = f32(devices, ncf // pack, pack * count)
    blocks_shape = bf16(6, face, face)

    def gather(value):
        return lax.all_to_all(value, AXES, 0, 0)

    blocks = neumann.reshape(6, face, face)
    load_f, basis, rows, *sent = call(
        functools.partial(start_kernel, face),
        [f32(count, width), bf16(ncf, width), bf16(*flat_shape)] + part + big,
        load.reshape(count, width), blocks, coarse_basis.reshape(ncf, width),
        coarse_rows.reshape(flat_shape), far=(0, 1, 2, 3),
        scratch=[bf16(count, width), blocks_shape, pltpu.SemaphoreType.DMA((4,))],
    )
    received = swap(sent[:swaps], FIRST, IDLE_FIRST)
    blocks_received = swap(sent[swaps:], BLOCKS, IDLE_BLOCKS)
    (slot,) = call(functools.partial(residual_kernel, face, FIRST, pack), [slots], load_f, basis, *received)
    whole = gather(slot)
    start, others, table, all_rows, local = call(
        functools.partial(local_kernel, face, swaps),
        [f32(count, width), blocks_shape, bf16(24 * ncf, 2 * width), f32(8 * flat_shape[0], 256), f32(count, width)],
        load_f, blocks, basis, rows, schur2, *received, *blocks_received, far=(1, 4), far_out=(1,),
        scratch=[blocks_shape, blocks_shape, bf16(width, width), f32(8 * ncf, width), pltpu.SemaphoreType.DMA((4,))],
    )
    all_rows = all_rows.reshape(8 * ncf, total).astype(jnp.bfloat16)
    terms, vec, *sent = call(
        functools.partial(middle_kernel, face), [bf16(24 * ncf, count), f32(count, width)] + part,
        whole, all_rows, table, local,
    )
    received = swap(sent, SECOND, IDLE_SECOND)
    (slot,) = call(functools.partial(residual_kernel, face, SECOND, pack), [slots], vec, basis, *received)
    whole = gather(slot)
    (start,) = call(
        functools.partial(advance_kernel, face), [f32(count, width)], vec, blocks, others, start, terms, table, *received,
        far=(1, 2), scratch=[blocks_shape, blocks_shape, pltpu.SemaphoreType.DMA((2,))],
    )
    (result,) = call(last_kernel, [bf16(count, width)], whole, all_rows, table, start)
    return result.reshape(load.shape)


def solution(mesh):
    placed = (
        P("gx", "gy", "gz", None, None),
        P("gx", "gy", "gz", None, None),
        P("gx", "gy", "gz", None, None, None),
        P("gx", "gy", "gz", None, None),
        P("gx", "gy", "gz", None, None),
    )
    return jax.shard_map(
        body, mesh=mesh, in_specs=placed, out_specs=P("gx", "gy", "gz", None, None), check_vma=False
    )
```
